512 devices in a mesh: grp: 16 (over z_lo, y), row: 32 (over z_hi, x, core).
Axes of the slice: x: 4, y: 4, z: 16 (z_hi: 4, z_lo: 4; z = z_hi * 4 + z_lo), core: 2. Of those that a mesh axis runs over, the one named last changes fastest.
Arguments:
- colatitude: float32 [1048576], P(('grp', 'row')), may hold values from 0.05 to 3.09
- longitude: float32 [1048576], P(('grp', 'row')), may hold values from -3.140625 to 3.140625
- observed: bfloat16 [2, 1048576], P(None, ('grp', 'row')), may hold values from -6 to 6
- filter_taps: bfloat16 [2, 256], replicated, may hold values from -0.375 to 0.375
- segment_start: int32 [1048576], P(('grp', 'row')), may hold values 0 or 1
- harmonic: int32 [2, 512], replicated, may hold values from -280 to 280, as said below
Outputs:
- normal: float32 [512, 512], P('row', 'grp')
- right_side: float32 [512], replicated
- diagonal: float32 [512], replicated
The draws below stay inside these ranges and needn't reach their ends.
Inputs may be any that keep to these rules, and one draw needn't show every extreme that they name: `harmonic`: row 0 holds degrees from 2 to 280; row 1 holds orders whose magnitude is at most the column's degree; no two columns name the same pair; the pairs (280, 280) and (280, -280) are always present.
All inputs are finite; a program needn't handle non-finite values. No bound on the sum of `segment_start` on one device may be relied on, other than what follows from the above.
Results may differ from the reference program's by a relative error of at most 0.0041.
Values may be sent and summed in bfloat16 or wider, within the bound.
No kernel may reach another device: no remote copies, remote signals or barrier semaphores. Data moves between devices by JAX's collectives and lax.ppermute only.
A program may use at most 64 MiB of HBM per device.

```python
import jax
import jax.numpy as jnp
from jax import lax

PANEL = 512
TAPS = 256
NMAX = 280
ROWS_DEV = 2048
ROWS = 1048576
N_ROW = 32
DEVICES = 512


def draw_harmonic(key, part):
    pairs_total = (NMAX + 1) ** 2 - 4
    lowest = NMAX * NMAX - 4
    first_key, second_key = jax.random.split(jax.random.fold_in(key, 17))
    others = jax.random.permutation(first_key, pairs_total - 2)[:PANEL - 2].astype(jnp.int32)
    others = jnp.where(others >= lowest, others + 1, others).astype(jnp.int32)
    chosen = jnp.concatenate([jnp.array([lowest, pairs_total - 1], jnp.int32), others])
    chosen = chosen[jax.random.permutation(second_key, PANEL)]
    levels = jnp.arange(3, NMAX + 1, dtype=jnp.int32)
    degree = 2 + jnp.sum(((levels * levels - 4)[None, :] <= chosen[:, None]).astype(jnp.int32), axis=1)
    order_index = chosen - (degree * degree - 4) - degree
    return jnp.stack([degree, order_index]).astype(jnp.int32)


def with_ends(values, key, low, largest):
    longest = values.shape.index(max(values.shape))
    spots = []
    for shift in (0, 1):
        where = [jax.random.randint(jax.random.fold_in(key, axis), (), 0, length) for axis, length in enumerate(values.shape)]
        where[longest] = (where[longest] + shift) % values.shape[longest]
        spots.append(tuple(where))
    return values.at[spots[0]].set(low).at[spots[1]].set(largest)


def level_of(stream_key, shape, cuts, smallest, top_value):
    def one(dim, parts):
        steps = jax.random.uniform(jax.random.fold_in(jax.random.fold_in(stream_key, 6), dim), (parts,), jnp.float32, smallest / len(cuts), top_value / len(cuts))
        return jnp.repeat(jnp.exp(steps), shape[dim] // parts).reshape((-1,) + (1,) * (len(shape) - dim - 1))

    gain = one(*cuts[0])
    for cut in cuts[1:]:
        gain = gain * one(*cut)
    return gain


def normal_values(stream_key, extent, deviation, bound, shards=(), kind=jnp.bfloat16):
    drawn = deviation * jax.random.normal(stream_key, extent, jnp.float32)
    if shards:
        drawn = drawn * level_of(stream_key, extent, shards, -0.22, 0.18)
    return jnp.clip(drawn, -bound, bound).astype(kind)


def setup_inputs(seed: int = 0) -> dict:
    splits = jax.random.split(jax.random.key(seed), 7)
    colatitude = jnp.clip(0.05 + 3.04 * jax.random.uniform(splits[0], (ROWS,), jnp.float32) ** level_of(splits[0], (ROWS,), ((0, 512),), -0.2, 0.2), 0.05, 3.09)
    longitude = jnp.clip(jax.random.uniform(splits[1], (ROWS,), jnp.float32, -3.140625, 3.140625), -3.140625, 3.140625)
    observed = normal_values(splits[2], (2, ROWS), 1.0, 6.0, ((1, 512),))
    filter_taps = normal_values(splits[3], (2, TAPS), TAPS ** -0.5, 0.375)
    segment_start = with_ends((jax.random.randint(splits[4], (ROWS,), 0, ROWS_DEV) < 2).astype(jnp.int32), jax.random.fold_in(splits[4], 1), 0, 1)
    harmonic = draw_harmonic(jax.random.fold_in(splits[6], 71), 0)
    return {"colatitude": colatitude, "longitude": longitude, "observed": observed, "filter_taps": filter_taps, "segment_start": segment_start, "harmonic": harmonic}


def design_rows(colatitude, longitude, harmonic):
    degree = harmonic[0].astype(jnp.float32)
    order_index = harmonic[1]
    polar_angle = colatitude[:, None] * degree[None, :]
    azimuth = longitude[:, None] * jnp.abs(order_index).astype(jnp.float32)[None, :]
    azimuth_wave = jnp.where(order_index[None, :] >= 0, jnp.cos(azimuth), jnp.sin(azimuth))
    radial = (jnp.cos(polar_angle) * azimuth_wave).astype(jnp.bfloat16)
    along = (jnp.sin(polar_angle) * azimuth_wave).astype(jnp.bfloat16)
    return radial, along


def reference(colatitude, longitude, observed, filter_taps, segment_start, harmonic):
    halo_rows = TAPS - 1
    group_rows = ROWS_DEV * N_ROW
    segment = jnp.cumsum(segment_start).astype(jnp.int32)
    colat_pad = jnp.concatenate([jnp.zeros((halo_rows,), colatitude.dtype), colatitude])
    long_pad = jnp.concatenate([jnp.zeros((halo_rows,), longitude.dtype), longitude])
    obs_pad = jnp.concatenate([jnp.zeros((2, halo_rows), observed.dtype), observed], axis=1)
    seg_pad = jnp.concatenate([jnp.full((halo_rows,), -1, jnp.int32), segment])
    position = jnp.arange(ROWS + halo_rows, dtype=jnp.int32) - halo_rows
    group_index = jnp.where(position >= 0, position // group_rows, -1).astype(jnp.int32)
    row_idx = jnp.arange(TAPS, dtype=jnp.int32)[:, None]
    col_idx = jnp.arange(2 * TAPS - 1, dtype=jnp.int32)[None, :]
    tap_lag = row_idx + TAPS - 1 - col_idx
    inside = (tap_lag >= 0) & (tap_lag <= TAPS - 1)
    clipped = jnp.clip(tap_lag, 0, TAPS - 1)
    toeplitz = jnp.where(inside[None], filter_taps[:, clipped], jnp.zeros((), filter_taps.dtype))

    def one_block(carried, number):
        normal_acc, rhs_acc = carried
        block_base = (number * ROWS_DEV).astype(jnp.int32)
        span = ROWS_DEV + halo_rows
        win_colat = lax.dynamic_slice_in_dim(colat_pad, block_base, span)
        win_long = lax.dynamic_slice_in_dim(long_pad, block_base, span)
        win_seg = lax.dynamic_slice_in_dim(seg_pad, block_base, span)
        win_group = lax.dynamic_slice_in_dim(group_index, block_base, span)
        win_obs = lax.dynamic_slice_in_dim(obs_pad, block_base, span, 1)
        fields = design_rows(win_colat, win_long, harmonic)
        for component in range(2):
            pieces = []
            signal_pieces = []
            for block_index in range(ROWS_DEV // TAPS):
                block_low = block_index * TAPS
                in_seg = win_seg[block_low:block_low + 2 * TAPS - 1]
                out_seg = win_seg[block_low + halo_rows:block_low + halo_rows + TAPS]
                in_group = win_group[block_low:block_low + 2 * TAPS - 1]
                out_group = win_group[block_low + halo_rows:block_low + halo_rows + TAPS]
                valid_mask = (out_seg[:, None] == in_seg[None, :]) & (out_group[:, None] == in_group[None, :])
                matrix = jnp.where(valid_mask, toeplitz[component], jnp.zeros((), toeplitz.dtype))
                pieces.append(jnp.dot(matrix, fields[component][block_low:block_low + 2 * TAPS - 1], preferred_element_type=jnp.float32).astype(jnp.bfloat16))
                signal_pieces.append(jnp.dot(matrix, win_obs[component, block_low:block_low + 2 * TAPS - 1], preferred_element_type=jnp.float32).astype(jnp.bfloat16))
            filtered = jnp.concatenate(pieces, axis=0)
            filtered_signal = jnp.concatenate(signal_pieces, axis=0)
            normal_acc = normal_acc + jnp.dot(filtered.T, filtered, preferred_element_type=jnp.float32)
            rhs_acc = rhs_acc + jnp.dot(filtered_signal, filtered, preferred_element_type=jnp.float32)
        return (normal_acc, rhs_acc), None

    start_state = (jnp.zeros((PANEL, PANEL), jnp.float32), jnp.zeros((PANEL,), jnp.float32))
    (gram, right_side), _ = lax.scan(one_block, start_state, jnp.arange(DEVICES, dtype=jnp.int32))
    same_index = jnp.arange(PANEL, dtype=jnp.int32)[:, None] == jnp.arange(PANEL, dtype=jnp.int32)[None, :]
    normal = jnp.where(same_index, jnp.zeros((), gram.dtype), gram) * (ROWS ** -0.5)
    diagonal = jnp.diagonal(gram) * (1.0 / ROWS)
    return normal, right_side * (ROWS ** -0.5), diagonal
```

```python
import functools
import math

import jax
import jax.numpy as jnp
from jax import lax
from jax.experimental import pallas as pl
from jax.experimental.pallas import tpu as pltpu
from jax.sharding import Mesh, PartitionSpec as P

F32 = jnp.float32
BF16 = jnp.bfloat16
LANES = 128
TAPS = 256
SIN_COEFFS = (3.141592639, -5.167709953, 2.550074404, -0.5982681334, 0.07760505745)
COS_COEFFS = (0.9999999504, -4.934792377, 4.058400535, -1.331796279, 0.2195071918)
TWO_PI_PARTS = (6.28125, 0.0019340515136718750, 1.2556659146854654e-06)
HALF_UP = 1.5 * 2.0**23


def horner(coeffs, z):
    total = z * coeffs[-1] + coeffs[-2]
    for coeff in coeffs[-3::-1]:
        total = total * z + coeff
    return total


def nearest(value):
    return (value + HALF_UP) - HALF_UP


def turns_of(angle):
    coarse = nearest(angle * (65536.0 / (2.0 * math.pi))) * (1.0 / 65536.0)
    rest = angle
    for part in TWO_PI_PARTS:
        rest = rest - coarse * part
    return coarse, rest * (1.0 / (2.0 * math.pi))


def dot_nt(a, b):
    return lax.dot_general(a, b, (((1,), (1,)), ((), ())), preferred_element_type=F32)


def dot_nn(a, b):
    return lax.dot_general(a, b, (((1,), (0,)), ((), ())), preferred_element_type=F32)


def iota(shape, axis):
    return lax.broadcasted_iota(jnp.int32, shape, axis)


def gram_kernel(
    colat_ref,
    lon_ref,
    obs_ref,
    start_ref,
    halo_ref,
    harmonic_ref,
    taps_ref,
    out_ref,
    design,
    filtered,
    matrices,
    columns,
    turns,
    starts,
    gram,
    *,
    panel,
    blocks,
    row_scale,
    gram_scale,
):
    own_rows = blocks * 2
    all_rows = own_rows + 2

    wide = harmonic_ref[...].astype(F32)
    tall = jnp.transpose(jnp.concatenate([wide, jnp.zeros((6, panel), F32)], axis=0))
    for zl in range(4):
        for y in range(4):
            part = tall[zl * 128 + y * 32 : zl * 128 + y * 32 + 32, :]
            low = y * 128 + zl * 32
            degree = jnp.broadcast_to(part[:, 0:1], (32, LANES))
            order = jnp.broadcast_to(part[:, 1:2], (32, LANES))
            columns[0, low : low + 32, :] = degree
            columns[1, low : low + 32, :] = jnp.abs(order)
            columns[2, low : low + 32, :] = jnp.where(order < 0.0, 0.25, 0.0)

    for slot, (own, halo_low) in enumerate(((colat_ref, 0), (lon_ref, 2))):
        coarse, fine = turns_of(halo_ref[halo_low : halo_low + 2, :])
        turns[2 * slot, 0:2, :] = coarse
        turns[2 * slot + 1, 0:2, :] = fine
        coarse, fine = turns_of(own[...])
        turns[2 * slot, 2 : 2 + own_rows, :] = coarse
        turns[2 * slot + 1, 2 : 2 + own_rows, :] = fine

    starts[...] = jnp.zeros_like(starts)
    starts[0:2, :] = halo_ref[8:10, :]
    starts[2 : 2 + own_rows, :] = start_ref[...].astype(F32)
    flags = starts[...].astype(BF16)
    square = (LANES, LANES)
    low_tri = (iota(square, 0) >= iota(square, 1)).astype(BF16)
    up_tri = (iota(square, 0) <= iota(square, 1)).astype(BF16)
    low_strict = (iota(square, 0) > iota(square, 1)).astype(BF16)
    up_strict = (iota(square, 0) < iota(square, 1)).astype(BF16)
    ones = jnp.ones(square, BF16)
    lonely = 1.0 - halo_ref[10:11, :]
    label_row = dot_nn(flags, up_tri) + dot_nn(dot_nn(low_strict, flags).astype(BF16), ones)
    label_row = label_row + jnp.where(iota(square, 0) >= 2, lonely, 0.0)
    label_col = dot_nt(low_tri, flags) + dot_nn(dot_nt(ones, flags).astype(BF16), up_strict)
    label_col = label_col + jnp.where(iota(square, 1) >= 2, lonely, 0.0)

    toeplitz = []
    for component in range(2):
        padded = jnp.concatenate(
            [taps_ref[component : component + 1, :].astype(F32), jnp.zeros((1, TAPS), F32)], axis=1
        )
        spread = jnp.broadcast_to(padded, (LANES, 2 * TAPS))
        rolled = pltpu.roll(spread, 0, 1, stride=1, stride_axis=0)
        toeplitz.append([rolled[:, d * LANES : (d + 1) * LANES] for d in range(3)])
    for block in range(blocks):
        for sb in range(4):
            source = 2 * block + sb
            left = jnp.broadcast_to(label_col[:, source : source + 1], square)
            for tb in range(2):
                d = tb - sb + 2
                place = (slice(sb * LANES, (sb + 1) * LANES), slice(tb * LANES, (tb + 1) * LANES))
                if 0 <= d <= 2:
                    target = 2 * block + 2 + tb
                    same = left == label_row[target : target + 1, :]
                    for component in range(2):
                        kept = jnp.where(same, toeplitz[component][d], 0.0)
                        matrices[block, component, place[0], place[1]] = kept.astype(BF16)
                else:
                    for component in range(2):
                        matrices[block, component, place[0], place[1]] = jnp.zeros(square, BF16)

    def some_columns(step, carry):
        low = pl.multiple_of(step * 16, 16)
        degree = columns[0, pl.ds(low, 16), :]
        order = columns[1, pl.ds(low, 16), :]
        phase = columns[2, pl.ds(low, 16), :]
        for chunk in range(all_rows):
            row = slice(chunk, chunk + 1)
            lane = slice(chunk * LANES, (chunk + 1) * LANES)
            polar = degree * turns[0, row, :]
            polar = (polar - nearest(polar)) + degree * turns[1, row, :]
            z = polar * polar
            half_sin = polar * horner(SIN_COEFFS, z)
            half_cos = horner(COS_COEFFS, z)
            twice = half_sin + half_sin
            cos_polar = 1.0 - twice * half_sin
            sin_polar = twice * half_cos
            azimuth = order * turns[2, row, :] - phase
            azimuth = (azimuth - nearest(azimuth)) + order * turns[3, row, :]
            half = azimuth * horner(SIN_COEFFS, azimuth * azimuth)
            wave = 1.0 - (half + half) * half
            design[0, pl.ds(low, 16), lane] = (cos_polar * wave).astype(BF16)
            design[1, pl.ds(low, 16), lane] = (sin_polar * wave).astype(BF16)
        return carry

    lax.fori_loop(0, panel // 16, some_columns, 0)

    for component in range(2):
        halo = jnp.concatenate(
            [halo_ref[4 + 2 * component : 5 + 2 * component, :], halo_ref[5 + 2 * component : 6 + 2 * component, :]],
            axis=1,
        )
        design[component, panel : panel + 16, 0:TAPS] = jnp.where(
            iota((16, TAPS), 0) == 0, halo, 0.0
        ).astype(BF16)
        span = own_rows * LANES
        own = obs_ref[component : component + 1, :].astype(F32)
        design[component, panel : panel + 16, TAPS : TAPS + span] = jnp.where(
            iota((16, span), 0) == 0, own, 0.0
        ).astype(BF16)

    for component in range(2):
        for block in range(blocks):
            window = design[component, :, block * TAPS : block * TAPS + 2 * TAPS]
            low = (component * blocks + block) * TAPS
            filtered[:, low : low + TAPS] = dot_nn(window, matrices[block, component]).astype(BF16)

    gram[...] = dot_nt(filtered[...], filtered[0:panel, :])

    eye = iota(square, 0) == iota(square, 1)
    rhs = [gram[panel : panel + 1, y * LANES : (y + 1) * LANES] * gram_scale for y in range(4)]
    diagonal = [
        jnp.sum(
            jnp.where(eye, gram[y * LANES : (y + 1) * LANES, y * LANES : (y + 1) * LANES], 0.0),
            axis=0,
            keepdims=True,
        )
        * row_scale
        for y in range(4)
    ]
    small = jnp.concatenate(rhs + diagonal + [jnp.zeros((8, LANES), F32)], axis=0).astype(BF16)
    for y in range(4):
        for x in range(4):
            for core in range(2):
                peer = y * 8 + x * 2 + core
                for zh in range(4):
                    low = x * 128 + zh * 32 + core * 16
                    out_ref[peer, zh * 16 : zh * 16 + 16, :] = (
                        gram[low : low + 16, y * LANES : (y + 1) * LANES] * gram_scale
                    ).astype(BF16)
                out_ref[peer, 64:80, :] = small


def middle_kernel(in_ref, out_ref):
    total = in_ref[0].astype(F32)
    for peer in range(1, in_ref.shape[0]):
        total = total + in_ref[peer].astype(F32)
    small = total[64:72, :]
    for zl in range(4):
        for zh in range(4):
            peer = zl * 4 + zh
            for b in range(4):
                rows = total[zh * 16 + 4 * b : zh * 16 + 4 * b + 4, zl * 32 : zl * 32 + 32]
                out_ref[peer, 0:4, b * 32 : b * 32 + 32] = rows
            out_ref[peer, 8:16, :] = small


def last_kernel(row_ref, in_ref, normal_ref, rhs_ref, diagonal_ref):
    total = in_ref[0]
    for peer in range(1, in_ref.shape[0]):
        total = total + in_ref[peer]
    for b in range(4):
        normal_ref[4 * b : 4 * b + 4, :] = total[0:4, b * 32 : b * 32 + 32]
    rows, cols = normal_ref.shape
    row_label = row_ref[0] + iota((rows, cols), 0)
    col_label = row_ref[1] + iota((rows, cols), 1)
    normal_ref[...] = jnp.where(row_label == col_label, 0.0, normal_ref[...])
    for out_ref, low in ((rhs_ref, 8), (diagonal_ref, 12)):
        for zl in range(4):
            for y in range(4):
                out_ref[0:1, zl * 128 + y * 32 : zl * 128 + y * 32 + 32] = total[
                    low + y : low + y + 1, zl * 32 : zl * 32 + 32
                ]


def on_device(colatitude, longitude, observed, filter_taps, segment_start, harmonic):
    rows_here = colatitude.shape[0]
    panel = harmonic.shape[1]
    blocks = rows_here // TAPS
    rows_total = rows_here * 512
    tail = rows_here - TAPS
    pieces = [
        colatitude[tail:],
        longitude[tail:],
        observed[0, tail:].astype(F32),
        observed[1, tail:].astype(F32),
        segment_start[tail:].astype(F32),
        jnp.ones((768,), F32),
    ]
    packed = jnp.concatenate(pieces)
    length = 32
    halo = lax.ppermute(packed, ("zh", "x", "core"), [(i, i + 1) for i in range(length - 1)])

    vmem = pl.BlockSpec(memory_space=pltpu.VMEM)
    kernel = functools.partial(
        gram_kernel,
        panel=panel,
        blocks=blocks,
        row_scale=1.0 / rows_total,
        gram_scale=1.0 / math.sqrt(rows_total),
    )
    payload = pl.pallas_call(
        kernel,
        name="gram_of_arc_part",
        out_shape=jax.ShapeDtypeStruct((32, 80, LANES), BF16),
        in_specs=[vmem] * 7,
        out_specs=vmem,
        scratch_shapes=[
            pltpu.VMEM((2, panel + 16, rows_here + TAPS), BF16),
            pltpu.VMEM((panel + 16, 2 * rows_here), BF16),
            pltpu.VMEM((blocks, 2, 2 * TAPS, TAPS), BF16),
            pltpu.VMEM((3, panel, LANES), F32),
            pltpu.VMEM((4, 24, LANES), F32),
            pltpu.VMEM((LANES, LANES), F32),
            pltpu.VMEM((panel + 16, panel), F32),
        ],
        compiler_params=pltpu.CompilerParams(vmem_limit_bytes=48 * 1024 * 1024),
    )(
        colatitude.reshape(-1, LANES),
        longitude.reshape(-1, LANES),
        observed,
        segment_start.reshape(-1, LANES),
        halo.reshape(-1, LANES),
        harmonic,
        filter_taps,
    )
    arrived = lax.all_to_all(payload, ("y", "x", "core"), 0, 0)
    packed_sums = pl.pallas_call(
        middle_kernel,
        name="sum_over_plane",
        out_shape=jax.ShapeDtypeStruct((16, 16, LANES), F32),
        in_specs=[vmem],
        out_specs=vmem,
    )(arrived)
    gathered = lax.all_to_all(packed_sums, ("zl", "zh"), 0, 0)
    row_low = (lax.axis_index("zh") * 8 + lax.axis_index("x") * 2 + lax.axis_index("core")) * 16
    col_low = (lax.axis_index("zl") * 4 + lax.axis_index("y")) * 32
    corner = jnp.stack([row_low, col_low]).astype(jnp.int32)
    normal, right_side, diagonal = pl.pallas_call(
        last_kernel,
        name="sum_over_z",
        out_shape=(
            jax.ShapeDtypeStruct((16, 32), F32),
            jax.ShapeDtypeStruct((1, panel), F32),
            jax.ShapeDtypeStruct((1, panel), F32),
        ),
        in_specs=[pl.BlockSpec(memory_space=pltpu.SMEM), vmem],
        out_specs=(vmem, vmem, vmem),
    )(corner, gathered)
    return normal, right_side.reshape(panel), diagonal.reshape(panel)


def solution(mesh):
    fine = Mesh(mesh.devices.reshape(4, 4, 4, 4, 2), ("zl", "y", "zh", "x", "core"))
    everywhere = ("zl", "y", "zh", "x", "core")
    return jax.shard_map(
        on_device,
        mesh=fine,
        in_specs=(P(everywhere), P(everywhere), P(None, everywhere), P(), P(everywhere), P()),
        out_specs=(P(("zh", "x", "core"), ("zl", "y")), P(), P()),
        check_vma=False,
    )
```

```python
import functools
import math

import jax
import jax.numpy as jnp
from jax import lax
from jax.experimental import pallas as pl
from jax.experimental.pallas import tpu as pltpu
from jax.sharding import Mesh, PartitionSpec as P

F32 = jnp.float32
BF16 = jnp.bfloat16
LANES = 128
TAPS = 256
SIN_COEFFS = (3.141592639, -5.167709953, 2.550074404, -0.5982681334, 0.07760505745)
COS_COEFFS = (0.9999999504, -4.934792377, 4.058400535, -1.331796279, 0.2195071918)
TWO_PI_PARTS = (6.28125, 0.0019340515136718750, 1.2556659146854654e-06)
HALF_UP = 1.5 * 2.0**23


def horner(coeffs, z):
    total = z * coeffs[-1] + coeffs[-2]
    for coeff in coeffs[-3::-1]:
        total = total * z + coeff
    return total


def nearest(value):
    return (value + HALF_UP) - HALF_UP


def turns_of(angle):
    coarse = nearest(angle * (65536.0 / (2.0 * math.pi))) * (1.0 / 65536.0)
    rest = angle
    for part in TWO_PI_PARTS:
        rest = rest - coarse * part
    return coarse, rest * (1.0 / (2.0 * math.pi))


def dot_nt(a, b):
    return lax.dot_general(a, b, (((1,), (1,)), ((), ())), preferred_element_type=F32)


def dot_nn(a, b):
    return lax.dot_general(a, b, (((1,), (0,)), ((), ())), preferred_element_type=F32)


def iota(shape, axis):
    return lax.broadcasted_iota(jnp.int32, shape, axis)


def spread_turns(turns, angle, slot, low):
    coarse, fine = turns_of(angle)
    turns[2 * slot, low : low + angle.shape[0], :] = coarse
    turns[2 * slot + 1, low : low + angle.shape[0], :] = fine


def fill_design(design, columns, turns, chunks):
    def some_columns(step, carry):
        low = pl.multiple_of(step * 16, 16)
        degree = columns[0, pl.ds(low, 16), :]
        order = columns[1, pl.ds(low, 16), :]
        phase = columns[2, pl.ds(low, 16), :]
        for chunk in range(chunks):
            row = slice(chunk, chunk + 1)
            lane = slice(chunk * LANES, (chunk + 1) * LANES)
            polar = degree * turns[0, row, :]
            polar = (polar - nearest(polar)) + degree * turns[1, row, :]
            z = polar * polar
            half_sin = polar * horner(SIN_COEFFS, z)
            half_cos = horner(COS_COEFFS, z)
            twice = half_sin + half_sin
            cos_polar = 1.0 - twice * half_sin
            sin_polar = twice * half_cos
            azimuth = order * turns[2, row, :] - phase
            azimuth = (azimuth - nearest(azimuth)) + order * turns[3, row, :]
            half = azimuth * horner(SIN_COEFFS, azimuth * azimuth)
            wave = 1.0 - (half + half) * half
            design[0, pl.ds(low, 16), lane] = (cos_polar * wave).astype(BF16)
            design[1, pl.ds(low, 16), lane] = (sin_polar * wave).astype(BF16)
        return carry

    lax.fori_loop(0, columns.shape[1] // 16, some_columns, 0)


def fill_signal(design, component, panel, values):
    span = values.shape[1]
    design[component, panel : panel + 16, 0:span] = jnp.where(
        iota((16, span), 0) == 0, values, 0.0
    ).astype(BF16)


def labels_of(flags):
    square = (LANES, LANES)
    low_tri = (iota(square, 0) >= iota(square, 1)).astype(BF16)
    up_tri = (iota(square, 0) <= iota(square, 1)).astype(BF16)
    low_strict = (iota(square, 0) > iota(square, 1)).astype(BF16)
    up_strict = (iota(square, 0) < iota(square, 1)).astype(BF16)
    ones = jnp.ones(square, BF16)
    by_lane = dot_nn(flags, up_tri) + dot_nn(dot_nn(low_strict, flags).astype(BF16), ones)
    by_sublane = dot_nt(low_tri, flags) + dot_nn(dot_nt(ones, flags).astype(BF16), up_strict)
    return by_lane, by_sublane


def fill_matrices(matrices, block, first_row, by_lane, by_sublane, toeplitz):
    square = (LANES, LANES)
    for sb in range(4):
        left = jnp.broadcast_to(by_sublane[:, first_row + sb : first_row + sb + 1], square)
        for tb in range(2):
            d = tb - sb + 2
            place = (slice(sb * LANES, (sb + 1) * LANES), slice(tb * LANES, (tb + 1) * LANES))
            if 0 <= d <= 2:
                same = left == by_lane[first_row + 2 + tb : first_row + 3 + tb, :]
                for component in range(2):
                    kept = jnp.where(same, toeplitz(component, d), 0.0)
                    matrices[block, component, place[0], place[1]] = kept.astype(BF16)
            else:
                for component in range(2):
                    matrices[block, component, place[0], place[1]] = jnp.zeros(square, BF16)


def own_kernel(
    colat_ref,
    lon_ref,
    obs_ref,
    start_ref,
    harmonic_ref,
    taps_ref,
    gram_ref,
    head_ref,
    columns_ref,
    toeplitz_ref,
    design,
    filtered,
    matrices,
    turns,
    starts,
):
    rows, _ = colat_ref.shape
    panel = harmonic_ref.shape[1]
    blocks = rows // 2

    wide = harmonic_ref[...].astype(F32)
    tall = jnp.transpose(jnp.concatenate([wide, jnp.zeros((6, panel), F32)], axis=0))
    for zl in range(4):
        for y in range(4):
            part = tall[zl * 128 + y * 32 : zl * 128 + y * 32 + 32, :]
            low = y * 128 + zl * 32
            degree = jnp.broadcast_to(part[:, 0:1], (32, LANES))
            order = jnp.broadcast_to(part[:, 1:2], (32, LANES))
            columns_ref[0, low : low + 32, :] = degree
            columns_ref[1, low : low + 32, :] = jnp.abs(order)
            columns_ref[2, low : low + 32, :] = jnp.where(order < 0.0, 0.25, 0.0)

    spread_turns(turns, colat_ref[...], 0, 0)
    spread_turns(turns, lon_ref[...], 1, 0)

    starts[...] = jnp.zeros_like(starts)
    starts[0:rows, :] = start_ref[...].astype(F32)
    by_lane, by_sublane = labels_of(starts[...].astype(BF16))

    for component in range(2):
        padded = jnp.concatenate(
            [taps_ref[component : component + 1, :].astype(F32), jnp.zeros((1, TAPS), F32)], axis=1
        )
        spread = jnp.broadcast_to(padded, (LANES, 2 * TAPS))
        rolled = pltpu.roll(spread, 0, 1, stride=1, stride_axis=0)
        for d in range(3):
            toeplitz_ref[component, d] = rolled[:, d * LANES : (d + 1) * LANES]
    for block in range(blocks - 1):
        fill_matrices(
            matrices, block, 2 * block, by_lane, by_sublane, lambda c, d: toeplitz_ref[c, d]
        )

    fill_design(design, columns_ref, turns, rows)
    for component in range(2):
        fill_signal(design, component, panel, obs_ref[component : component + 1, :].astype(F32))
        head_ref[component] = design[component, :, 0:TAPS]

    for component in range(2):
        for block in range(blocks - 1):
            window = design[component, :, block * TAPS : block * TAPS + 2 * TAPS]
            low = (component * (blocks - 1) + block) * TAPS
            filtered[:, low : low + TAPS] = dot_nn(window, matrices[block, component]).astype(BF16)
    gram_ref[...] = dot_nt(filtered[...], filtered[0:panel, :])


def edge_kernel(
    halo_ref,
    start_ref,
    before_ref,
    head_ref,
    columns_ref,
    toeplitz_ref,
    out_ref,
    design,
    filtered,
    matrices,
    turns,
    starts,
    gram,
    *,
    row_scale,
    gram_scale,
):
    panel = columns_ref.shape[1]
    spread_turns(turns, halo_ref[0:2, :], 0, 0)
    spread_turns(turns, halo_ref[2:4, :], 1, 0)

    square = (LANES, LANES)
    starts[...] = jnp.zeros_like(starts)
    starts[0:2, :] = halo_ref[8:10, :]
    starts[2:4, :] = start_ref[0:2, :].astype(F32)
    by_lane, by_sublane = labels_of(starts[...].astype(BF16))
    lonely = 1.0 - halo_ref[10:11, :]
    by_lane = by_lane + jnp.where(iota(square, 0) >= 2, lonely, 0.0)
    by_sublane = by_sublane + jnp.where(iota(square, 1) >= 2, lonely, 0.0)
    fill_matrices(matrices, 0, 0, by_lane, by_sublane, lambda c, d: toeplitz_ref[c, d])

    fill_design(design, columns_ref, turns, 2)
    for component in range(2):
        low = 4 + 2 * component
        halo = jnp.concatenate([halo_ref[low : low + 1, :], halo_ref[low + 1 : low + 2, :]], axis=1)
        fill_signal(design, component, panel, halo)
        sums = dot_nn(design[component], matrices[0, component, 0:TAPS, :]) + dot_nn(
            head_ref[component], matrices[0, component, TAPS : 2 * TAPS, :]
        )
        filtered[:, component * TAPS : (component + 1) * TAPS] = sums.astype(BF16)

    gram[...] = before_ref[...] + dot_nt(filtered[...], filtered[0:panel, :])

    eye = iota(square, 0) == iota(square, 1)
    rhs = [gram[panel : panel + 1, y * LANES : (y + 1) * LANES] * gram_scale for y in range(4)]
    diagonal = [
        jnp.sum(
            jnp.where(eye, gram[y * LANES : (y + 1) * LANES, y * LANES : (y + 1) * LANES], 0.0),
            axis=0,
            keepdims=True,
        )
        * row_scale
        for y in range(4)
    ]
    small = jnp.concatenate(rhs + diagonal, axis=0).astype(BF16)
    for y in range(4):
        for x in range(4):
            for core in range(2):
                peer = y * 8 + x * 2 + core
                for zh in range(4):
                    low = x * 128 + zh * 32 + core * 16
                    out_ref[peer, zh * 16 : zh * 16 + 16, :] = (
                        gram[low : low + 16, y * LANES : (y + 1) * LANES] * gram_scale
                    ).astype(BF16)
                out_ref[peer, 64:72, :] = small


def middle_kernel(in_ref, out_ref):
    total = in_ref[0].astype(F32)
    for peer in range(1, in_ref.shape[0]):
        total = total + in_ref[peer].astype(F32)
    small = total[64:72, :].astype(BF16)
    head = total[0:64, :].astype(BF16)
    tail = (total[0:64, :] - head.astype(F32)).astype(BF16)
    for zl in range(4):
        for zh in range(4):
            peer = zl * 4 + zh
            for b in range(4):
                rows = slice(zh * 16 + 4 * b, zh * 16 + 4 * b + 4)
                lanes = slice(zl * 32, zl * 32 + 32)
                out_ref[peer, 0:4, b * 32 : b * 32 + 32] = head[rows, lanes]
                out_ref[peer, 4:8, b * 32 : b * 32 + 32] = tail[rows, lanes]
            out_ref[peer, 8:16, :] = small


def last_kernel(in_ref, normal_ref, rhs_ref, diagonal_ref):
    total = in_ref[0].astype(F32)
    for peer in range(1, in_ref.shape[0]):
        total = total + in_ref[peer].astype(F32)
    tile = total[0:4, :] + total[4:8, :]
    for b in range(4):
        normal_ref[4 * b : 4 * b + 4, :] = tile[:, b * 32 : b * 32 + 32]
    rows, cols = normal_ref.shape
    row_low = (lax.axis_index("zh") * 8 + lax.axis_index("x") * 2 + lax.axis_index("core")) * rows
    col_low = (lax.axis_index("zl") * 4 + lax.axis_index("y")) * cols
    on_diagonal = row_low + iota((rows, cols), 0) == col_low + iota((rows, cols), 1)
    normal_ref[...] = jnp.where(on_diagonal, 0.0, normal_ref[...])
    for out_ref, low in ((rhs_ref, 8), (diagonal_ref, 12)):
        for zl in range(4):
            for y in range(4):
                out_ref[0:1, zl * 128 + y * 32 : zl * 128 + y * 32 + 32] = total[
                    low + y : low + y + 1, zl * 32 : zl * 32 + 32
                ]


def load_kernel(*refs):
    count = (len(refs) - 2) // 2
    sources, packed_ref, targets, sems = refs[:count], refs[count], refs[count + 1 : -1], refs[-1]
    copies = [
        pltpu.make_async_copy(source, target, sems.at[index])
        for index, (source, target) in enumerate(zip(sources, targets))
    ]
    for copy in copies:
        copy.start()
    for copy in copies:
        copy.wait()
    colat_ref, lon_ref, obs_ref, start_ref = targets[:4]
    last = colat_ref.shape[0] - 2
    span = obs_ref.shape[1]
    packed_ref[0:2, :] = colat_ref[last : last + 2, :]
    packed_ref[2:4, :] = lon_ref[last : last + 2, :]
    for component in range(2):
        for half in range(2):
            low = span - (2 - half) * LANES
            row = 4 + 2 * component + half
            packed_ref[row : row + 1, :] = obs_ref[component : component + 1, low : low + LANES].astype(
                F32
            )
    packed_ref[8:10, :] = start_ref[last : last + 2, :].astype(F32)
    packed_ref[10:16, :] = jnp.ones((6, LANES), F32)


def on_device(colatitude, longitude, observed, filter_taps, segment_start, harmonic):
    rows_here = colatitude.shape[0]
    panel = harmonic.shape[1]
    blocks = rows_here // TAPS
    rows_total = rows_here * 512
    vmem = pl.BlockSpec(memory_space=pltpu.VMEM)

    def kernel(body, name, outs, scratch, mebibytes, operands, estimate=None):
        return pl.pallas_call(
            body,
            name=name,
            out_shape=outs,
            in_specs=[vmem] * len(operands),
            out_specs=jax.tree.map(lambda _: vmem, outs),
            scratch_shapes=scratch,
            cost_estimate=estimate,
            compiler_params=pltpu.CompilerParams(vmem_limit_bytes=mebibytes * 1024 * 1024),
        )(*operands)

    colat = colatitude.reshape(-1, LANES)
    lon = longitude.reshape(-1, LANES)
    start = segment_start.reshape(-1, LANES)
    arguments = (colat, lon, observed, start, harmonic, filter_taps)
    packed, colat, lon, observed, start, harmonic, filter_taps = pl.pallas_call(
        load_kernel,
        name="load_and_pack",
        out_shape=(
            jax.ShapeDtypeStruct((16, LANES), F32),
            *(jax.ShapeDtypeStruct(value.shape, value.dtype) for value in arguments),
        ),
        in_specs=[pl.BlockSpec(memory_space=pltpu.HBM)] * len(arguments),
        out_specs=(vmem,) * (len(arguments) + 1),
        scratch_shapes=[pltpu.SemaphoreType.DMA((len(arguments),))],
        compiler_params=pltpu.CompilerParams(vmem_limit_bytes=4 * 1024 * 1024),
    )(*(pltpu.with_memory_space_constraint(value, pltpu.HBM) for value in arguments))
    halo = lax.ppermute(packed, ("zh", "x", "core"), [(i, i + 1) for i in range(31)])
    before, head, columns, toeplitz = kernel(
        own_kernel,
        "own_epochs",
        (
            jax.ShapeDtypeStruct((panel + 16, panel), F32),
            jax.ShapeDtypeStruct((2, panel + 16, TAPS), BF16),
            jax.ShapeDtypeStruct((3, panel, LANES), F32),
            jax.ShapeDtypeStruct((2, 3, LANES, LANES), F32),
        ),
        [
            pltpu.VMEM((2, panel + 16, rows_here), BF16),
            pltpu.VMEM((panel + 16, 2 * (rows_here - TAPS)), BF16),
            pltpu.VMEM((blocks - 1, 2, 2 * TAPS, TAPS), BF16),
            pltpu.VMEM((4, 16, LANES), F32),
            pltpu.VMEM((LANES, LANES), F32),
        ],
        32,
        (colat, lon, observed, start, harmonic, filter_taps),
        pl.CostEstimate(flops=4_000_000_000, bytes_accessed=4_000_000, transcendentals=3_000_000),
    )
    payload = kernel(
        functools.partial(
            edge_kernel, row_scale=1.0 / rows_total, gram_scale=1.0 / math.sqrt(rows_total)
        ),
        "edge_epochs",
        jax.ShapeDtypeStruct((32, 72, LANES), BF16),
        [
            pltpu.VMEM((2, panel + 16, TAPS), BF16),
            pltpu.VMEM((panel + 16, 2 * TAPS), BF16),
            pltpu.VMEM((1, 2, 2 * TAPS, TAPS), BF16),
            pltpu.VMEM((4, 8, LANES), F32),
            pltpu.VMEM((LANES, LANES), F32),
            pltpu.VMEM((panel + 16, panel), F32),
        ],
        16,
        (halo, start, before, head, columns, toeplitz),
    )
    arrived = lax.all_to_all(payload, ("y", "x", "core"), 0, 0)
    sums = kernel(
        middle_kernel, "sum_over_plane", jax.ShapeDtypeStruct((16, 16, LANES), BF16), [], 8, (arrived,)
    )
    gathered = lax.all_to_all(sums, ("zl", "zh"), 0, 0)
    normal, right_side, diagonal = kernel(
        last_kernel,
        "sum_over_z",
        (
            jax.ShapeDtypeStruct((16, 32), F32),
            jax.ShapeDtypeStruct((1, panel), F32),
            jax.ShapeDtypeStruct((1, panel), F32),
        ),
        [],
        8,
        (gathered,),
    )
    return normal, right_side.reshape(panel), diagonal.reshape(panel)


def solution(mesh):
    fine = Mesh(mesh.devices.reshape(4, 4, 4, 4, 2), ("zl", "y", "zh", "x", "core"))
    everywhere = ("zl", "y", "zh", "x", "core")
    return jax.shard_map(
        on_device,
        mesh=fine,
        in_specs=(P(everywhere), P(everywhere), P(None, everywhere), P(), P(everywhere), P()),
        out_specs=(P(("zh", "x", "core"), ("zl", "y")), P(), P()),
        check_vma=False,
    )
```

```python
import functools
import math

import jax
import jax.numpy as jnp
from jax import lax
from jax.experimental import pallas as pl
from jax.experimental.pallas import tpu as pltpu
from jax.sharding import Mesh, PartitionSpec as P

F32 = jnp.float32
BF16 = jnp.bfloat16
LANES = 128
TAPS = 256
MULTIPLES = 288
SIN_COEFFS = (3.141592639, -5.167709953, 2.550074404, -0.5982681334, 0.07760505745)
COS_COEFFS = (0.9999999504, -4.934792377, 4.058400535, -1.331796279, 0.2195071918)
TWO_PI_PARTS = (6.28125, 0.0019340515136718750, 1.2556659146854654e-06)
HALF_UP = 1.5 * 2.0**23


def horner(coeffs, z):
    total = z * coeffs[-1] + coeffs[-2]
    for coeff in coeffs[-3::-1]:
        total = total * z + coeff
    return total


def nearest(value):
    return (value + HALF_UP) - HALF_UP


def turns_of(angle):
    coarse = nearest(angle * (65536.0 / (2.0 * math.pi))) * (1.0 / 65536.0)
    rest = angle
    for part in TWO_PI_PARTS:
        rest = rest - coarse * part
    return coarse, rest * (1.0 / (2.0 * math.pi))


def dot_nt(a, b):
    return lax.dot_general(a, b, (((1,), (1,)), ((), ())), preferred_element_type=F32)


def dot_nn(a, b):
    return lax.dot_general(a, b, (((1,), (0,)), ((), ())), preferred_element_type=F32)


def iota(shape, axis):
    return lax.broadcasted_iota(jnp.int32, shape, axis)


def spread_turns(turns, angle, slot, low):
    coarse, fine = turns_of(angle)
    turns[2 * slot, low : low + angle.shape[0], :] = coarse
    turns[2 * slot + 1, low : low + angle.shape[0], :] = fine


def fill_design(design, columns, turns, chunks):
    def some_columns(step, carry):
        low = pl.multiple_of(step * 16, 16)
        degree = columns[0, pl.ds(low, 16), :]
        order = columns[1, pl.ds(low, 16), :]
        phase = columns[2, pl.ds(low, 16), :]
        for chunk in range(chunks):
            row = slice(chunk, chunk + 1)
            lane = slice(chunk * LANES, (chunk + 1) * LANES)
            polar = degree * turns[0, row, :]
            polar = (polar - nearest(polar)) + degree * turns[1, row, :]
            z = polar * polar
            half_sin = polar * horner(SIN_COEFFS, z)
            half_cos = horner(COS_COEFFS, z)
            twice = half_sin + half_sin
            cos_polar = 1.0 - twice * half_sin
            sin_polar = twice * half_cos
            azimuth = order * turns[2, row, :] - phase
            azimuth = (azimuth - nearest(azimuth)) + order * turns[3, row, :]
            half = azimuth * horner(SIN_COEFFS, azimuth * azimuth)
            wave = 1.0 - (half + half) * half
            design[0, pl.ds(low, 16), lane] = (cos_polar * wave).astype(BF16)
            design[1, pl.ds(low, 16), lane] = (sin_polar * wave).astype(BF16)
        return carry

    lax.fori_loop(0, columns.shape[1] // 16, some_columns, 0)


def sine_and_cosine(turns, slot, factor):
    part = turns[2 * slot] * factor
    part = (part - nearest(part)) + turns[2 * slot + 1] * factor
    z = part * part
    half_sin = part * horner(SIN_COEFFS, z)
    twice = half_sin + half_sin
    return twice * horner(COS_COEFFS, z), 1.0 - twice * half_sin


def fill_tables(tables, turns, small):
    rows = turns.shape[1]
    for slot in range(2):
        for b in range(16):
            sine, cosine = sine_and_cosine(turns, slot, float(b))
            small[slot, 0, b] = cosine
            small[slot, 1, b] = sine

    def some_multiples(a, carry):
        for slot, table in enumerate(tables):
            sine, cosine = sine_and_cosine(turns, slot, (16 * a).astype(F32))
            for b in range(16):
                place = pl.ds(pl.multiple_of(a * (16 * rows), 16 * rows) + b * rows, rows)
                table[0, place, :] = cosine * small[slot, 0, b] - sine * small[slot, 1, b]
                table[1, place, :] = sine * small[slot, 0, b] + cosine * small[slot, 1, b]
        return carry

    lax.fori_loop(0, MULTIPLES // 16, some_multiples, 0)


def fill_products(products, rows_of, tables):
    polar, azimuth = tables
    rows = 8 * products.shape[1]

    def some_columns(group, carry):
        start = pl.multiple_of(group * 256, 256)
        for offset in range(32):
            degree = pl.multiple_of(rows_of[group, offset], rows)
            order = pl.multiple_of(rows_of[16 + group, offset], rows)
            wave = azimuth[pl.ds(order, rows), :]
            place = pl.ds(start + offset * 8, 8)
            for component in range(2):
                value = polar[component, pl.ds(degree, rows), :] * wave
                for half in range(rows // 8):
                    products[component, half, place, :] = value[8 * half : 8 * half + 8, :]
        return carry

    lax.fori_loop(0, 16, some_columns, 0)


def fill_signal(design, component, panel, values):
    span = values.shape[1]
    design[component, panel : panel + 16, 0:span] = jnp.where(
        iota((16, span), 0) == 0, values, 0.0
    ).astype(BF16)


def labels_of(flags):
    square = (LANES, LANES)
    low_tri = (iota(square, 0) >= iota(square, 1)).astype(BF16)
    up_tri = (iota(square, 0) <= iota(square, 1)).astype(BF16)
    low_strict = (iota(square, 0) > iota(square, 1)).astype(BF16)
    up_strict = (iota(square, 0) < iota(square, 1)).astype(BF16)
    ones = jnp.ones(square, BF16)
    by_lane = dot_nn(flags, up_tri) + dot_nn(dot_nn(low_strict, flags).astype(BF16), ones)
    by_sublane = dot_nt(low_tri, flags) + dot_nn(dot_nt(ones, flags).astype(BF16), up_strict)
    return by_lane, by_sublane


def fill_matrices(matrices, block, first_row, by_lane, by_sublane, toeplitz):
    square = (LANES, LANES)
    for sb in range(4):
        left = jnp.broadcast_to(by_sublane[:, first_row + sb : first_row + sb + 1], square)
        for tb in range(2):
            d = tb - sb + 2
            place = (slice(sb * LANES, (sb + 1) * LANES), slice(tb * LANES, (tb + 1) * LANES))
            if 0 <= d <= 2:
                same = left == by_lane[first_row + 2 + tb : first_row + 3 + tb, :]
                for component in range(2):
                    kept = jnp.where(same, toeplitz(component, d), 0.0)
                    matrices[block, component, place[0], place[1]] = kept.astype(BF16)
            else:
                for component in range(2):
                    matrices[block, component, place[0], place[1]] = jnp.zeros(square, BF16)


def own_kernel(
    colat_ref,
    lon_ref,
    obs_ref,
    start_ref,
    harmonic_ref,
    scalar_ref,
    taps_ref,
    gram_ref,
    head_ref,
    columns_ref,
    toeplitz_ref,
    design,
    filtered,
    matrices,
    turns,
    starts,
    polar,
    azimuth,
    small,
    products,
    scalars,
    scalars_sem,
):
    scalars_copy = pltpu.make_async_copy(scalar_ref, scalars, scalars_sem)
    scalars_copy.start()
    rows, _ = colat_ref.shape
    panel = harmonic_ref.shape[1]
    blocks = rows // 2

    wide = harmonic_ref[...].astype(F32)
    tall = jnp.transpose(jnp.concatenate([wide, jnp.zeros((6, panel), F32)], axis=0))
    for zl in range(4):
        for y in range(4):
            part = tall[zl * 128 + y * 32 : zl * 128 + y * 32 + 32, :]
            low = y * 128 + zl * 32
            degree = jnp.broadcast_to(part[:, 0:1], (32, LANES))
            order = jnp.broadcast_to(part[:, 1:2], (32, LANES))
            columns_ref[0, low : low + 32, :] = degree
            columns_ref[1, low : low + 32, :] = jnp.abs(order)
            columns_ref[2, low : low + 32, :] = jnp.where(order < 0.0, 0.25, 0.0)

    spread_turns(turns, colat_ref[...], 0, 0)
    spread_turns(turns, lon_ref[...], 1, 0)

    starts[...] = jnp.zeros_like(starts)
    starts[0:rows, :] = start_ref[...].astype(F32)
    by_lane, by_sublane = labels_of(starts[...].astype(BF16))

    for component in range(2):
        padded = jnp.concatenate(
            [taps_ref[component : component + 1, :].astype(F32), jnp.zeros((1, TAPS), F32)], axis=1
        )
        spread = jnp.broadcast_to(padded, (LANES, 2 * TAPS))
        rolled = pltpu.roll(spread, 0, 1, stride=1, stride_axis=0)
        for d in range(3):
            toeplitz_ref[component, d] = rolled[:, d * LANES : (d + 1) * LANES]
    fill_tables((polar, azimuth.reshape(2, MULTIPLES * rows, LANES)), turns, small)
    scalars_copy.wait()
    fill_products(products, scalars, (polar, azimuth))
    for component in range(2):
        fill_signal(design, component, panel, obs_ref[component : component + 1, :].astype(F32))

    def to_lanes(block):
        for component in range(2):
            for row in (2 * block, 2 * block + 1):
                for low in range(0, panel, 16):
                    tile = products[component, row // 8, pl.ds(low * 8 + row % 8, 16, stride=8), :]
                    design[component, low : low + 16, row * LANES : (row + 1) * LANES] = tile.astype(BF16)

    to_lanes(0)
    for component in range(2):
        head_ref[component] = design[component, :, 0:TAPS]
    for block in range(blocks - 1):
        to_lanes(block + 1)
        fill_matrices(
            matrices, block, 2 * block, by_lane, by_sublane, lambda c, d: toeplitz_ref[c, d]
        )
        for component in range(2):
            window = design[component, :, block * TAPS : block * TAPS + 2 * TAPS]
            low = (component * (blocks - 1) + block) * TAPS
            filtered[:, low : low + TAPS] = dot_nn(window, matrices[block, component]).astype(BF16)
    gram_ref[...] = dot_nt(filtered[...], filtered[0:panel, :])


def edge_kernel(
    halo_ref,
    start_ref,
    before_ref,
    head_ref,
    columns_ref,
    toeplitz_ref,
    out_ref,
    design,
    filtered,
    matrices,
    turns,
    starts,
    gram,
    *,
    row_scale,
    gram_scale,
):
    panel = columns_ref.shape[1]
    spread_turns(turns, halo_ref[0:2, :], 0, 0)
    spread_turns(turns, halo_ref[2:4, :], 1, 0)

    square = (LANES, LANES)
    starts[...] = jnp.zeros_like(starts)
    starts[0:2, :] = halo_ref[8:10, :]
    starts[2:4, :] = start_ref[0:2, :].astype(F32)
    by_lane, by_sublane = labels_of(starts[...].astype(BF16))
    lonely = 1.0 - halo_ref[10:11, :]
    by_lane = by_lane + jnp.where(iota(square, 0) >= 2, lonely, 0.0)
    by_sublane = by_sublane + jnp.where(iota(square, 1) >= 2, lonely, 0.0)
    fill_matrices(matrices, 0, 0, by_lane, by_sublane, lambda c, d: toeplitz_ref[c, d])

    fill_design(design, columns_ref, turns, 2)
    for component in range(2):
        low = 4 + 2 * component
        halo = jnp.concatenate([halo_ref[low : low + 1, :], halo_ref[low + 1 : low + 2, :]], axis=1)
        fill_signal(design, component, panel, halo)
        sums = dot_nn(design[component], matrices[0, component, 0:TAPS, :]) + dot_nn(
            head_ref[component], matrices[0, component, TAPS : 2 * TAPS, :]
        )
        filtered[:, component * TAPS : (component + 1) * TAPS] = sums.astype(BF16)

    gram[...] = before_ref[...] + dot_nt(filtered[...], filtered[0:panel, :])

    eye = iota(square, 0) == iota(square, 1)
    rhs = [gram[panel : panel + 1, y * LANES : (y + 1) * LANES] * gram_scale for y in range(4)]
    diagonal = [
        jnp.sum(
            jnp.where(eye, gram[y * LANES : (y + 1) * LANES, y * LANES : (y + 1) * LANES], 0.0),
            axis=0,
            keepdims=True,
        )
        * row_scale
        for y in range(4)
    ]
    small = jnp.concatenate(rhs + diagonal, axis=0).astype(BF16)
    for y in range(4):
        for x in range(4):
            for core in range(2):
                peer = y * 8 + x * 2 + core
                for zh in range(4):
                    low = x * 128 + zh * 32 + core * 16
                    out_ref[peer, zh * 16 : zh * 16 + 16, :] = (
                        gram[low : low + 16, y * LANES : (y + 1) * LANES] * gram_scale
                    ).astype(BF16)
                out_ref[peer, 64:72, :] = small


def middle_kernel(in_ref, out_ref):
    total = in_ref[0].astype(F32)
    for peer in range(1, in_ref.shape[0]):
        total = total + in_ref[peer].astype(F32)
    small = total[64:72, :].astype(BF16)
    head = total[0:64, :].astype(BF16)
    tail = (total[0:64, :] - head.astype(F32)).astype(BF16)
    for zl in range(4):
        for zh in range(4):
            peer = zl * 4 + zh
            for b in range(4):
                rows = slice(zh * 16 + 4 * b, zh * 16 + 4 * b + 4)
                lanes = slice(zl * 32, zl * 32 + 32)
                out_ref[peer, 0:4, b * 32 : b * 32 + 32] = head[rows, lanes]
                out_ref[peer, 4:8, b * 32 : b * 32 + 32] = tail[rows, lanes]
            out_ref[peer, 8:16, :] = small


def last_kernel(in_ref, normal_ref, rhs_ref, diagonal_ref):
    total = in_ref[0].astype(F32)
    for peer in range(1, in_ref.shape[0]):
        total = total + in_ref[peer].astype(F32)
    tile = total[0:4, :] + total[4:8, :]
    for b in range(4):
        normal_ref[4 * b : 4 * b + 4, :] = tile[:, b * 32 : b * 32 + 32]
    rows, cols = normal_ref.shape
    row_low = (lax.axis_index("zh") * 8 + lax.axis_index("x") * 2 + lax.axis_index("core")) * rows
    col_low = (lax.axis_index("zl") * 4 + lax.axis_index("y")) * cols
    on_diagonal = row_low + iota((rows, cols), 0) == col_low + iota((rows, cols), 1)
    normal_ref[...] = jnp.where(on_diagonal, 0.0, normal_ref[...])
    for out_ref, low in ((rhs_ref, 8), (diagonal_ref, 12)):
        for zl in range(4):
            for y in range(4):
                out_ref[0:1, zl * 128 + y * 32 : zl * 128 + y * 32 + 32] = total[
                    low + y : low + y + 1, zl * 32 : zl * 32 + 32
                ]


def load_kernel(*refs):
    count = (len(refs) - 3) // 2
    sources, packed_ref, rows_ref = refs[:count], refs[count], refs[count + 1]
    targets, sems = refs[count + 2 : -1], refs[-1]
    copies = [
        pltpu.make_async_copy(source, target, sems.at[index])
        for index, (source, target) in enumerate(zip(sources, targets))
    ]
    for copy in copies:
        copy.start()
    for copy in copies:
        copy.wait()
    colat_ref, lon_ref, obs_ref, start_ref = targets[:4]
    last = colat_ref.shape[0] - 2
    span = obs_ref.shape[1]
    packed_ref[0:2, :] = colat_ref[last : last + 2, :]
    packed_ref[2:4, :] = lon_ref[last : last + 2, :]
    for component in range(2):
        for half in range(2):
            low = span - (2 - half) * LANES
            row = 4 + 2 * component + half
            packed_ref[row : row + 1, :] = obs_ref[component : component + 1, low : low + LANES].astype(
                F32
            )
    packed_ref[8:10, :] = start_ref[last : last + 2, :].astype(F32)
    packed_ref[10:16, :] = jnp.ones((6, LANES), F32)
    rows = colat_ref.shape[0]
    degree = targets[4][0:1, :]
    order = targets[4][1:2, :]
    wave = jnp.abs(order) + jnp.where(order < 0, MULTIPLES, 0)
    for y in range(4):
        for zl in range(4):
            group = y * 4 + zl
            lanes = slice(zl * LANES + y * 32, zl * LANES + y * 32 + 32)
            rows_ref[group : group + 1, 0:32] = degree[:, lanes] * rows
            rows_ref[16 + group : 17 + group, 0:32] = wave[:, lanes] * rows


def on_device(colatitude, longitude, observed, filter_taps, segment_start, harmonic):
    rows_here = colatitude.shape[0]
    panel = harmonic.shape[1]
    blocks = rows_here // TAPS
    rows_total = rows_here * 512
    vmem = pl.BlockSpec(memory_space=pltpu.VMEM)
    hbm = pl.BlockSpec(memory_space=pltpu.HBM)

    def kernel(body, name, outs, scratch, mebibytes, operands, estimate=None):
        return pl.pallas_call(
            body,
            name=name,
            out_shape=outs,
            in_specs=[vmem] * len(operands),
            out_specs=jax.tree.map(lambda _: vmem, outs),
            scratch_shapes=scratch,
            cost_estimate=estimate,
            compiler_params=pltpu.CompilerParams(vmem_limit_bytes=mebibytes * 1024 * 1024),
        )(*operands)

    colat = colatitude.reshape(-1, LANES)
    lon = longitude.reshape(-1, LANES)
    start = segment_start.reshape(-1, LANES)
    arguments = (colat, lon, observed, start, harmonic, filter_taps)
    packed, table_rows, colat, lon, observed, start, harmonic, filter_taps = pl.pallas_call(
        load_kernel,
        name="load_and_pack",
        out_shape=(
            jax.ShapeDtypeStruct((16, LANES), F32),
            jax.ShapeDtypeStruct((32, LANES), jnp.int32),
            *(jax.ShapeDtypeStruct(value.shape, value.dtype) for value in arguments),
        ),
        in_specs=[hbm] * len(arguments),
        out_specs=(vmem,) * (len(arguments) + 2),
        scratch_shapes=[pltpu.SemaphoreType.DMA((len(arguments),))],
        compiler_params=pltpu.CompilerParams(vmem_limit_bytes=4 * 1024 * 1024),
    )(*(pltpu.with_memory_space_constraint(value, pltpu.HBM) for value in arguments))
    halo = lax.ppermute(packed, ("zh", "x", "core"), [(i, i + 1) for i in range(31)])
    before, head, columns, toeplitz = kernel(
        own_kernel,
        "own_epochs",
        (
            jax.ShapeDtypeStruct((panel + 16, panel), F32),
            jax.ShapeDtypeStruct((2, panel + 16, TAPS), BF16),
            jax.ShapeDtypeStruct((3, panel, LANES), F32),
            jax.ShapeDtypeStruct((2, 3, LANES, LANES), F32),
        ),
        [
            pltpu.VMEM((2, panel + 16, rows_here), BF16),
            pltpu.VMEM((panel + 16, 2 * (rows_here - TAPS)), BF16),
            pltpu.VMEM((blocks - 1, 2, 2 * TAPS, TAPS), BF16),
            pltpu.VMEM((4, rows_here // LANES, LANES), F32),
            pltpu.VMEM((LANES, LANES), F32),
            pltpu.VMEM((2, MULTIPLES * rows_here // LANES, LANES), F32),
            pltpu.VMEM((2 * MULTIPLES * rows_here // LANES, LANES), F32),
            pltpu.VMEM((2, 2, 16, rows_here // LANES, LANES), F32),
            pltpu.VMEM((2, rows_here // LANES // 8, panel * 8, LANES), F32),
            pltpu.SMEM((32, LANES), jnp.int32),
            pltpu.SemaphoreType.DMA(()),
        ],
        48,
        (colat, lon, observed, start, harmonic, table_rows, filter_taps),
        pl.CostEstimate(flops=4_000_000_000, bytes_accessed=4_000_000, transcendentals=3_000_000),
    )
    payload = kernel(
        functools.partial(
            edge_kernel, row_scale=1.0 / rows_total, gram_scale=1.0 / math.sqrt(rows_total)
        ),
        "edge_epochs",
        jax.ShapeDtypeStruct((32, 72, LANES), BF16),
        [
            pltpu.VMEM((2, panel + 16, TAPS), BF16),
            pltpu.VMEM((panel + 16, 2 * TAPS), BF16),
            pltpu.VMEM((1, 2, 2 * TAPS, TAPS), BF16),
            pltpu.VMEM((4, 8, LANES), F32),
            pltpu.VMEM((LANES, LANES), F32),
            pltpu.VMEM((panel + 16, panel), F32),
        ],
        16,
        (halo, start, before, head, columns, toeplitz),
    )
    arrived = lax.all_to_all(payload, ("y", "x", "core"), 0, 0)
    sums = kernel(
        middle_kernel, "sum_over_plane", jax.ShapeDtypeStruct((16, 16, LANES), BF16), [], 8, (arrived,)
    )
    gathered = lax.all_to_all(sums, ("zl", "zh"), 0, 0)
    normal, right_side, diagonal = kernel(
        last_kernel,
        "sum_over_z",
        (
            jax.ShapeDtypeStruct((16, 32), F32),
            jax.ShapeDtypeStruct((1, panel), F32),
            jax.ShapeDtypeStruct((1, panel), F32),
        ),
        [],
        8,
        (gathered,),
    )
    return normal, right_side.reshape(panel), diagonal.reshape(panel)


def solution(mesh):
    fine = Mesh(mesh.devices.reshape(4, 4, 4, 4, 2), ("zl", "y", "zh", "x", "core"))
    everywhere = ("zl", "y", "zh", "x", "core")
    return jax.shard_map(
        on_device,
        mesh=fine,
        in_specs=(P(everywhere), P(everywhere), P(None, everywhere), P(), P(everywhere), P()),
        out_specs=(P(("zh", "x", "core"), ("zl", "y")), P(), P()),
        check_vma=False,
    )
```

```python
import functools
import math

import jax
import jax.numpy as jnp
from jax import lax
from jax.experimental import pallas as pl
from jax.experimental.pallas import tpu as pltpu
from jax.sharding import Mesh, PartitionSpec as P

F32 = jnp.float32
BF16 = jnp.bfloat16
LANES = 128
TAPS = 256
MULTIPLES = 288
SIN_COEFFS = (3.141592639, -5.167709953, 2.550074404, -0.5982681334, 0.07760505745)
COS_COEFFS = (0.9999999504, -4.934792377, 4.058400535, -1.331796279, 0.2195071918)
TWO_PI_PARTS = (6.28125, 0.0019340515136718750, 1.2556659146854654e-06)
HALF_UP = 1.5 * 2.0**23


def horner(coeffs, z):
    total = z * coeffs[-1] + coeffs[-2]
    for coeff in coeffs[-3::-1]:
        total = total * z + coeff
    return total


def nearest(value):
    return (value + HALF_UP) - HALF_UP


def turns_of(angle):
    coarse = nearest(angle * (65536.0 / (2.0 * math.pi))) * (1.0 / 65536.0)
    rest = angle
    for part in TWO_PI_PARTS:
        rest = rest - coarse * part
    return coarse, rest * (1.0 / (2.0 * math.pi))


def dot_nt(a, b):
    return lax.dot_general(a, b, (((1,), (1,)), ((), ())), preferred_element_type=F32)


def dot_nn(a, b):
    return lax.dot_general(a, b, (((1,), (0,)), ((), ())), preferred_element_type=F32)


def iota(shape, axis):
    return lax.broadcasted_iota(jnp.int32, shape, axis)


def spread_turns(turns, angle, slot, low):
    coarse, fine = turns_of(angle)
    turns[2 * slot, low : low + angle.shape[0], :] = coarse
    turns[2 * slot + 1, low : low + angle.shape[0], :] = fine


def fill_design(design, columns, turns, chunks):
    def some_columns(step, carry):
        low = pl.multiple_of(step * 32, 32)
        degree = columns[0, pl.ds(low, 32), :]
        order = columns[1, pl.ds(low, 32), :]
        phase = columns[2, pl.ds(low, 32), :]
        for chunk in range(chunks):
            row = slice(chunk, chunk + 1)
            lane = slice(chunk * LANES, (chunk + 1) * LANES)
            polar = degree * turns[0, row, :]
            polar = (polar - nearest(polar)) + degree * turns[1, row, :]
            z = polar * polar
            half_sin = polar * horner(SIN_COEFFS, z)
            half_cos = horner(COS_COEFFS, z)
            twice = half_sin + half_sin
            cos_polar = 1.0 - twice * half_sin
            sin_polar = twice * half_cos
            azimuth = order * turns[2, row, :] - phase
            azimuth = (azimuth - nearest(azimuth)) + order * turns[3, row, :]
            half = azimuth * horner(SIN_COEFFS, azimuth * azimuth)
            wave = 1.0 - (half + half) * half
            design[0, pl.ds(low, 32), lane] = (cos_polar * wave).astype(BF16)
            design[1, pl.ds(low, 32), lane] = (sin_polar * wave).astype(BF16)
        return carry

    lax.fori_loop(0, columns.shape[1] // 32, some_columns, 0)


def sine_and_cosine(turns, slot, factor):
    part = turns[2 * slot] * factor
    part = (part - nearest(part)) + turns[2 * slot + 1] * factor
    z = part * part
    half_sin = part * horner(SIN_COEFFS, z)
    twice = half_sin + half_sin
    return twice * horner(COS_COEFFS, z), 1.0 - twice * half_sin


def fill_tables(tables, turns, small):
    rows = turns.shape[1]
    for slot in range(2):
        for b in range(16):
            sine, cosine = sine_and_cosine(turns, slot, float(b))
            small[slot, 0, b] = cosine
            small[slot, 1, b] = sine

    def some_multiples(a, carry):
        for slot, table in enumerate(tables):
            sine, cosine = sine_and_cosine(turns, slot, (16 * a).astype(F32))
            for b in range(16):
                place = pl.ds(pl.multiple_of(a * (16 * rows), 16 * rows) + b * rows, rows)
                table[0, place, :] = cosine * small[slot, 0, b] - sine * small[slot, 1, b]
                table[1, place, :] = sine * small[slot, 0, b] + cosine * small[slot, 1, b]
        return carry

    lax.fori_loop(0, MULTIPLES // 16, some_multiples, 0)


def fill_products(products, rows_of, tables):
    polar, azimuth = tables
    rows = 4 * products.shape[1]
    upper = iota((8, LANES), 0) >= 4

    def some_columns(group, carry):
        start = pl.multiple_of(group * 128, 128)
        for pair in range(16):
            values = []
            for offset in (2 * pair, 2 * pair + 1):
                degree = pl.multiple_of(rows_of[group, offset], rows)
                order = pl.multiple_of(rows_of[16 + group, offset], rows)
                wave = azimuth[pl.ds(order, rows), :]
                values.append([polar[c, pl.ds(degree, rows), :] * wave for c in range(2)])
            place = pl.ds(start + pair * 8, 8)
            for component in range(2):
                for half in range(rows // 8):
                    one = values[0][component][8 * half : 8 * half + 8, :]
                    two = values[1][component][8 * half : 8 * half + 8, :]
                    products[component, 2 * half, place, :] = jnp.where(upper, pltpu.roll(two, 4, 0), one)
                    products[component, 2 * half + 1, place, :] = jnp.where(
                        upper, two, pltpu.roll(one, 4, 0)
                    )
        return carry

    lax.fori_loop(0, 16, some_columns, 0)


def fill_signal(design, component, panel, values):
    span = values.shape[1]
    design[component, panel : panel + 16, 0:span] = jnp.where(
        iota((16, span), 0) == 0, values, 0.0
    ).astype(BF16)


def labels_of(flags):
    square = (LANES, LANES)
    low_tri = (iota(square, 0) >= iota(square, 1)).astype(BF16)
    up_tri = (iota(square, 0) <= iota(square, 1)).astype(BF16)
    low_strict = (iota(square, 0) > iota(square, 1)).astype(BF16)
    up_strict = (iota(square, 0) < iota(square, 1)).astype(BF16)
    ones = jnp.ones(square, BF16)
    by_lane = dot_nn(flags, up_tri) + dot_nn(dot_nn(low_strict, flags).astype(BF16), ones)
    by_sublane = dot_nt(low_tri, flags) + dot_nn(dot_nt(ones, flags).astype(BF16), up_strict)
    return by_lane, by_sublane


def fill_matrices(matrices, block, first_row, by_lane, by_sublane, toeplitz):
    square = (LANES, LANES)
    for sb in range(4):
        left = jnp.broadcast_to(by_sublane[:, first_row + sb : first_row + sb + 1], square)
        for tb in range(2):
            d = tb - sb + 2
            place = (slice(sb * LANES, (sb + 1) * LANES), slice(tb * LANES, (tb + 1) * LANES))
            if 0 <= d <= 2:
                same = left == by_lane[first_row + 2 + tb : first_row + 3 + tb, :]
                for component in range(2):
                    kept = jnp.where(same, toeplitz(component, d), 0.0)
                    matrices[block, component, place[0], place[1]] = kept.astype(BF16)
            else:
                for component in range(2):
                    matrices[block, component, place[0], place[1]] = jnp.zeros(square, BF16)


def own_kernel(
    colat_ref,
    lon_ref,
    obs_ref,
    start_ref,
    harmonic_ref,
    scalar_ref,
    taps_ref,
    gram_ref,
    head_ref,
    columns_ref,
    toeplitz_ref,
    design,
    filtered,
    matrices,
    turns,
    starts,
    polar,
    azimuth,
    small,
    products,
    scalars,
    scalars_sem,
):
    scalars_copy = pltpu.make_async_copy(scalar_ref, scalars, scalars_sem)
    scalars_copy.start()
    rows, _ = colat_ref.shape
    panel = harmonic_ref.shape[1]
    blocks = rows // 2

    wide = harmonic_ref[...].astype(F32)
    tall = jnp.transpose(jnp.concatenate([wide, jnp.zeros((6, panel), F32)], axis=0))
    for zl in range(4):
        for y in range(4):
            part = tall[zl * 128 + y * 32 : zl * 128 + y * 32 + 32, :]
            low = y * 128 + zl * 32
            degree = jnp.broadcast_to(part[:, 0:1], (32, LANES))
            order = jnp.broadcast_to(part[:, 1:2], (32, LANES))
            columns_ref[0, low : low + 32, :] = degree
            columns_ref[1, low : low + 32, :] = jnp.abs(order)
            columns_ref[2, low : low + 32, :] = jnp.where(order < 0.0, 0.25, 0.0)

    spread_turns(turns, colat_ref[...], 0, 0)
    spread_turns(turns, lon_ref[...], 1, 0)

    starts[...] = jnp.zeros_like(starts)
    starts[0:rows, :] = start_ref[...].astype(F32)
    by_lane, by_sublane = labels_of(starts[...].astype(BF16))

    for component in range(2):
        padded = jnp.concatenate(
            [taps_ref[component : component + 1, :].astype(F32), jnp.zeros((1, TAPS), F32)], axis=1
        )
        spread = jnp.broadcast_to(padded, (LANES, 2 * TAPS))
        rolled = pltpu.roll(spread, 0, 1, stride=1, stride_axis=0)
        for d in range(3):
            toeplitz_ref[component, d] = rolled[:, d * LANES : (d + 1) * LANES]
    fill_tables((polar, azimuth.reshape(2, MULTIPLES * rows, LANES)), turns, small)
    scalars_copy.wait()
    fill_products(products, scalars, (polar, azimuth))
    for component in range(2):
        fill_signal(design, component, panel, obs_ref[component : component + 1, :].astype(F32))

    def to_lanes(block):
        for component in range(2):
            for row in (2 * block, 2 * block + 1):
                for low in range(0, panel, 16):
                    tile = products[component, row // 4, pl.ds(low * 4 + row % 4, 16, stride=4), :]
                    design[component, low : low + 16, row * LANES : (row + 1) * LANES] = tile.astype(BF16)

    to_lanes(0)
    for component in range(2):
        head_ref[component] = design[component, :, 0:TAPS]
    for block in range(blocks - 1):
        to_lanes(block + 1)
        fill_matrices(
            matrices, block, 2 * block, by_lane, by_sublane, lambda c, d: toeplitz_ref[c, d]
        )
        for component in range(2):
            window = design[component, :, block * TAPS : block * TAPS + 2 * TAPS]
            low = (component * (blocks - 1) + block) * TAPS
            filtered[:, low : low + TAPS] = dot_nn(window, matrices[block, component]).astype(BF16)
    gram_ref[...] = dot_nt(filtered[...], filtered[0:panel, :])


def edge_kernel(
    halo_ref,
    start_ref,
    before_ref,
    head_ref,
    columns_ref,
    toeplitz_ref,
    out_ref,
    design,
    filtered,
    matrices,
    turns,
    starts,
    gram,
    *,
    row_scale,
    gram_scale,
):
    panel = columns_ref.shape[1]
    spread_turns(turns, halo_ref[0:2, :], 0, 0)
    spread_turns(turns, halo_ref[2:4, :], 1, 0)

    square = (LANES, LANES)
    starts[...] = jnp.zeros_like(starts)
    starts[0:2, :] = halo_ref[8:10, :]
    starts[2:4, :] = start_ref[0:2, :].astype(F32)
    by_lane, by_sublane = labels_of(starts[...].astype(BF16))
    lonely = 1.0 - halo_ref[10:11, :]
    by_lane = by_lane + jnp.where(iota(square, 0) >= 2, lonely, 0.0)
    by_sublane = by_sublane + jnp.where(iota(square, 1) >= 2, lonely, 0.0)
    fill_matrices(matrices, 0, 0, by_lane, by_sublane, lambda c, d: toeplitz_ref[c, d])

    fill_design(design, columns_ref, turns, 2)
    for component in range(2):
        low = 4 + 2 * component
        halo = jnp.concatenate([halo_ref[low : low + 1, :], halo_ref[low + 1 : low + 2, :]], axis=1)
        fill_signal(design, component, panel, halo)
        sums = dot_nn(design[component], matrices[0, component, 0:TAPS, :]) + dot_nn(
            head_ref[component], matrices[0, component, TAPS : 2 * TAPS, :]
        )
        filtered[:, component * TAPS : (component + 1) * TAPS] = sums.astype(BF16)

    gram[...] = before_ref[...] + dot_nt(filtered[...], filtered[0:panel, :])

    eye = iota(square, 0) == iota(square, 1)
    rhs = [gram[panel : panel + 1, y * LANES : (y + 1) * LANES] * gram_scale for y in range(4)]
    diagonal = [
        jnp.sum(
            jnp.where(eye, gram[y * LANES : (y + 1) * LANES, y * LANES : (y + 1) * LANES], 0.0),
            axis=0,
            keepdims=True,
        )
        * row_scale
        for y in range(4)
    ]
    small = jnp.concatenate(rhs + diagonal, axis=0).astype(BF16)
    for y in range(4):
        for x in range(4):
            for core in range(2):
                peer = y * 8 + x * 2 + core
                for zh in range(4):
                    low = x * 128 + zh * 32 + core * 16
                    out_ref[peer, zh * 16 : zh * 16 + 16, :] = (
                        gram[low : low + 16, y * LANES : (y + 1) * LANES] * gram_scale
                    ).astype(BF16)
                out_ref[peer, 64:72, :] = small


def middle_kernel(in_ref, out_ref):
    total = in_ref[0].astype(F32)
    for peer in range(1, in_ref.shape[0]):
        total = total + in_ref[peer].astype(F32)
    small = total[64:72, :].astype(BF16)
    head = total[0:64, :].astype(BF16)
    tail = (total[0:64, :] - head.astype(F32)).astype(BF16)
    for zl in range(4):
        for zh in range(4):
            peer = zl * 4 + zh
            for b in range(4):
                rows = slice(zh * 16 + 4 * b, zh * 16 + 4 * b + 4)
                lanes = slice(zl * 32, zl * 32 + 32)
                out_ref[peer, 0:4, b * 32 : b * 32 + 32] = head[rows, lanes]
                out_ref[peer, 4:8, b * 32 : b * 32 + 32] = tail[rows, lanes]
            out_ref[peer, 8:16, :] = small


def last_kernel(in_ref, normal_ref, rhs_ref, diagonal_ref):
    total = in_ref[0].astype(F32)
    for peer in range(1, in_ref.shape[0]):
        total = total + in_ref[peer].astype(F32)
    tile = total[0:4, :] + total[4:8, :]
    for b in range(4):
        normal_ref[4 * b : 4 * b + 4, :] = tile[:, b * 32 : b * 32 + 32]
    rows, cols = normal_ref.shape
    row_low = (lax.axis_index("zh") * 8 + lax.axis_index("x") * 2 + lax.axis_index("core")) * rows
    col_low = (lax.axis_index("zl") * 4 + lax.axis_index("y")) * cols
    on_diagonal = row_low + iota((rows, cols), 0) == col_low + iota((rows, cols), 1)
    normal_ref[...] = jnp.where(on_diagonal, 0.0, normal_ref[...])
    for out_ref, low in ((rhs_ref, 8), (diagonal_ref, 12)):
        for zl in range(4):
            for y in range(4):
                out_ref[0:1, zl * 128 + y * 32 : zl * 128 + y * 32 + 32] = total[
                    low + y : low + y + 1, zl * 32 : zl * 32 + 32
                ]


def load_kernel(*refs):
    count = (len(refs) - 3) // 2
    sources, packed_ref, rows_ref = refs[:count], refs[count], refs[count + 1]
    targets, sems = refs[count + 2 : -1], refs[-1]
    copies = [
        pltpu.make_async_copy(source, target, sems.at[index])
        for index, (source, target) in enumerate(zip(sources, targets))
    ]
    for copy in copies:
        copy.start()
    for copy in copies:
        copy.wait()
    colat_ref, lon_ref, obs_ref, start_ref = targets[:4]
    last = colat_ref.shape[0] - 2
    span = obs_ref.shape[1]
    packed_ref[0:2, :] = colat_ref[last : last + 2, :]
    packed_ref[2:4, :] = lon_ref[last : last + 2, :]
    for component in range(2):
        for half in range(2):
            low = span - (2 - half) * LANES
            row = 4 + 2 * component + half
            packed_ref[row : row + 1, :] = obs_ref[component : component + 1, low : low + LANES].astype(
                F32
            )
    packed_ref[8:10, :] = start_ref[last : last + 2, :].astype(F32)
    packed_ref[10:16, :] = jnp.ones((6, LANES), F32)
    rows = colat_ref.shape[0]
    degree = targets[4][0:1, :]
    order = targets[4][1:2, :]
    wave = jnp.abs(order) + jnp.where(order < 0, MULTIPLES, 0)
    for y in range(4):
        for zl in range(4):
            group = y * 4 + zl
            lanes = slice(zl * LANES + y * 32, zl * LANES + y * 32 + 32)
            rows_ref[group : group + 1, 0:32] = degree[:, lanes] * rows
            rows_ref[16 + group : 17 + group, 0:32] = wave[:, lanes] * rows


def on_device(colatitude, longitude, observed, filter_taps, segment_start, harmonic):
    rows_here = colatitude.shape[0]
    panel = harmonic.shape[1]
    blocks = rows_here // TAPS
    rows_total = rows_here * 512
    vmem = pl.BlockSpec(memory_space=pltpu.VMEM)
    hbm = pl.BlockSpec(memory_space=pltpu.HBM)

    def kernel(body, name, outs, scratch, mebibytes, operands, estimate=None):
        return pl.pallas_call(
            body,
            name=name,
            out_shape=outs,
            in_specs=[vmem] * len(operands),
            out_specs=jax.tree.map(lambda _: vmem, outs),
            scratch_shapes=scratch,
            cost_estimate=estimate,
            compiler_params=pltpu.CompilerParams(vmem_limit_bytes=mebibytes * 1024 * 1024),
        )(*operands)

    colat = colatitude.reshape(-1, LANES)
    lon = longitude.reshape(-1, LANES)
    start = segment_start.reshape(-1, LANES)
    arguments = (colat, lon, observed, start, harmonic, filter_taps)
    packed, table_rows, colat, lon, observed, start, harmonic, filter_taps = pl.pallas_call(
        load_kernel,
        name="load_and_pack",
        out_shape=(
            jax.ShapeDtypeStruct((16, LANES), F32),
            jax.ShapeDtypeStruct((32, LANES), jnp.int32),
            *(jax.ShapeDtypeStruct(value.shape, value.dtype) for value in arguments),
        ),
        in_specs=[hbm] * len(arguments),
        out_specs=(vmem,) * (len(arguments) + 2),
        scratch_shapes=[pltpu.SemaphoreType.DMA((len(arguments),))],
        compiler_params=pltpu.CompilerParams(vmem_limit_bytes=4 * 1024 * 1024),
    )(*(pltpu.with_memory_space_constraint(value, pltpu.HBM) for value in arguments))
    halo = lax.ppermute(packed, ("zh", "x", "core"), [(i, i + 1) for i in range(31)])
    before, head, columns, toeplitz = kernel(
        own_kernel,
        "own_epochs",
        (
            jax.ShapeDtypeStruct((panel + 16, panel), F32),
            jax.ShapeDtypeStruct((2, panel + 16, TAPS), BF16),
            jax.ShapeDtypeStruct((3, panel, LANES), F32),
            jax.ShapeDtypeStruct((2, 3, LANES, LANES), F32),
        ),
        [
            pltpu.VMEM((2, panel + 16, rows_here), BF16),
            pltpu.VMEM((panel + 16, 2 * (rows_here - TAPS)), BF16),
            pltpu.VMEM((blocks - 1, 2, 2 * TAPS, TAPS), BF16),
            pltpu.VMEM((4, rows_here // LANES, LANES), F32),
            pltpu.VMEM((LANES, LANES), F32),
            pltpu.VMEM((2, MULTIPLES * rows_here // LANES, LANES), F32),
            pltpu.VMEM((2 * MULTIPLES * rows_here // LANES, LANES), F32),
            pltpu.VMEM((2, 2, 16, rows_here // LANES, LANES), F32),
            pltpu.VMEM((2, rows_here // LANES // 4, panel * 4, LANES), F32),
            pltpu.SMEM((32, LANES), jnp.int32),
            pltpu.SemaphoreType.DMA(()),
        ],
        48,
        (colat, lon, observed, start, harmonic, table_rows, filter_taps),
        pl.CostEstimate(flops=4_000_000_000, bytes_accessed=4_000_000, transcendentals=3_000_000),
    )
    payload = kernel(
        functools.partial(
            edge_kernel, row_scale=1.0 / rows_total, gram_scale=1.0 / math.sqrt(rows_total)
        ),
        "edge_epochs",
        jax.ShapeDtypeStruct((32, 72, LANES), BF16),
        [
            pltpu.VMEM((2, panel + 16, TAPS), BF16),
            pltpu.VMEM((panel + 16, 2 * TAPS), BF16),
            pltpu.VMEM((1, 2, 2 * TAPS, TAPS), BF16),
            pltpu.VMEM((4, 8, LANES), F32),
            pltpu.VMEM((LANES, LANES), F32),
            pltpu.VMEM((panel + 16, panel), F32),
        ],
        16,
        (halo, start, before, head, columns, toeplitz),
    )
    arrived = lax.all_to_all(payload, ("y", "x", "core"), 0, 0)
    sums = kernel(
        middle_kernel, "sum_over_plane", jax.ShapeDtypeStruct((16, 16, LANES), BF16), [], 8, (arrived,)
    )
    gathered = lax.all_to_all(sums, ("zl", "zh"), 0, 0)
    normal, right_side, diagonal = kernel(
        last_kernel,
        "sum_over_z",
        (
            jax.ShapeDtypeStruct((16, 32), F32),
            jax.ShapeDtypeStruct((1, panel), F32),
            jax.ShapeDtypeStruct((1, panel), F32),
        ),
        [],
        8,
        (gathered,),
    )
    return normal, right_side.reshape(panel), diagonal.reshape(panel)


def solution(mesh):
    fine = Mesh(mesh.devices.reshape(4, 4, 4, 4, 2), ("zl", "y", "zh", "x", "core"))
    everywhere = ("zl", "y", "zh", "x", "core")
    return jax.shard_map(
        on_device,
        mesh=fine,
        in_specs=(P(everywhere), P(everywhere), P(None, everywhere), P(), P(everywhere), P()),
        out_specs=(P(("zh", "x", "core"), ("zl", "y")), P(), P()),
        check_vma=False,
    )
```

```python
import functools
import math

import jax
import jax.numpy as jnp
from jax import lax
from jax.experimental import pallas as pl
from jax.experimental.pallas import tpu as pltpu
from jax.sharding import Mesh, PartitionSpec as P

F32 = jnp.float32
BF16 = jnp.bfloat16
LANES = 128
TAPS = 256
MULTIPLES = 288
SIN_COEFFS = (3.141592639, -5.167709953, 2.550074404, -0.5982681334, 0.07760505745)
COS_COEFFS = (0.9999999504, -4.934792377, 4.058400535, -1.331796279, 0.2195071918)
TWO_PI_PARTS = (6.28125, 0.0019340515136718750, 1.2556659146854654e-06)
HALF_UP = 1.5 * 2.0**23


def horner(coeffs, z):
    total = z * coeffs[-1] + coeffs[-2]
    for coeff in coeffs[-3::-1]:
        total = total * z + coeff
    return total


def nearest(value):
    return (value + HALF_UP) - HALF_UP


def turns_of(angle):
    coarse = nearest(angle * (65536.0 / (2.0 * math.pi))) * (1.0 / 65536.0)
    rest = angle
    for part in TWO_PI_PARTS:
        rest = rest - coarse * part
    return coarse, rest * (1.0 / (2.0 * math.pi))


def dot_nt(a, b):
    return lax.dot_general(a, b, (((1,), (1,)), ((), ())), preferred_element_type=F32)


def dot_nn(a, b):
    return lax.dot_general(a, b, (((1,), (0,)), ((), ())), preferred_element_type=F32)


def iota(shape, axis):
    return lax.broadcasted_iota(jnp.int32, shape, axis)


def spread_turns(turns, angle, slot, low):
    coarse, fine = turns_of(angle)
    turns[2 * slot, low : low + angle.shape[0], :] = coarse
    turns[2 * slot + 1, low : low + angle.shape[0], :] = fine


def fill_design(design, columns, turns, chunks):
    def some_columns(step, carry):
        low = pl.multiple_of(step * 32, 32)
        degree = columns[0, pl.ds(low, 32), :]
        order = columns[1, pl.ds(low, 32), :]
        phase = columns[2, pl.ds(low, 32), :]
        for chunk in range(chunks):
            row = slice(chunk, chunk + 1)
            lane = slice(chunk * LANES, (chunk + 1) * LANES)
            polar = degree * turns[0, row, :]
            polar = (polar - nearest(polar)) + degree * turns[1, row, :]
            z = polar * polar
            half_sin = polar * horner(SIN_COEFFS, z)
            half_cos = horner(COS_COEFFS, z)
            twice = half_sin + half_sin
            cos_polar = 1.0 - twice * half_sin
            sin_polar = twice * half_cos
            azimuth = order * turns[2, row, :] - phase
            azimuth = (azimuth - nearest(azimuth)) + order * turns[3, row, :]
            half = azimuth * horner(SIN_COEFFS, azimuth * azimuth)
            wave = 1.0 - (half + half) * half
            design[0, pl.ds(low, 32), lane] = (cos_polar * wave).astype(BF16)
            design[1, pl.ds(low, 32), lane] = (sin_polar * wave).astype(BF16)
        return carry

    lax.fori_loop(0, columns.shape[1] // 32, some_columns, 0)


def sine_and_cosine(turns, slot, factor):
    part = turns[2 * slot] * factor
    part = (part - nearest(part)) + turns[2 * slot + 1] * factor
    z = part * part
    half_sin = part * horner(SIN_COEFFS, z)
    twice = half_sin + half_sin
    return twice * horner(COS_COEFFS, z), 1.0 - twice * half_sin


def fill_tables(tables, turns, small):
    rows = turns.shape[1]
    for slot in range(2):
        for b in range(16):
            sine, cosine = sine_and_cosine(turns, slot, float(b))
            small[slot, 0, b] = cosine
            small[slot, 1, b] = sine

    def some_multiples(a, carry):
        for slot, table in enumerate(tables):
            sine, cosine = sine_and_cosine(turns, slot, (16 * a).astype(F32))
            for b in range(16):
                place = pl.ds(pl.multiple_of(a * (16 * rows), 16 * rows) + b * rows, rows)
                table[0, place, :] = cosine * small[slot, 0, b] - sine * small[slot, 1, b]
                table[1, place, :] = sine * small[slot, 0, b] + cosine * small[slot, 1, b]
        return carry

    lax.fori_loop(0, MULTIPLES // 16, some_multiples, 0)


def fill_products(products, rows_of, tables):
    polar, azimuth = tables
    rows = 4 * products.shape[1]
    upper = iota((8, LANES), 0) >= 4

    def some_columns(group, carry):
        start = pl.multiple_of(group * 128, 128)
        for pair in range(16):
            values = []
            for offset in (2 * pair, 2 * pair + 1):
                degree = pl.multiple_of(rows_of[group, offset], rows)
                order = pl.multiple_of(rows_of[16 + group, offset], rows)
                wave = azimuth[pl.ds(order, rows), :]
                values.append([polar[c, pl.ds(degree, rows), :] * wave for c in range(2)])
            place = pl.ds(start + pair * 8, 8)
            for component in range(2):
                for half in range(rows // 8):
                    one = values[0][component][8 * half : 8 * half + 8, :]
                    two = values[1][component][8 * half : 8 * half + 8, :]
                    products[component, 2 * half, place, :] = jnp.where(upper, pltpu.roll(two, 4, 0), one)
                    products[component, 2 * half + 1, place, :] = jnp.where(
                        upper, two, pltpu.roll(one, 4, 0)
                    )
        return carry

    lax.fori_loop(0, 16, some_columns, 0)


def fill_signal(design, component, panel, values):
    span = values.shape[1]
    design[component, panel : panel + 16, 0:span] = jnp.where(
        iota((16, span), 0) == 0, values, 0.0
    ).astype(BF16)


def labels_of(flags):
    square = (LANES, LANES)
    low_tri = (iota(square, 0) >= iota(square, 1)).astype(BF16)
    up_tri = (iota(square, 0) <= iota(square, 1)).astype(BF16)
    low_strict = (iota(square, 0) > iota(square, 1)).astype(BF16)
    up_strict = (iota(square, 0) < iota(square, 1)).astype(BF16)
    ones = jnp.ones(square, BF16)
    by_lane = dot_nn(flags, up_tri) + dot_nn(dot_nn(low_strict, flags).astype(BF16), ones)
    by_sublane = dot_nt(low_tri, flags) + dot_nn(dot_nt(ones, flags).astype(BF16), up_strict)
    return by_lane, by_sublane


def fill_matrices(matrices, block, first_row, by_lane, by_sublane, toeplitz):
    square = (LANES, LANES)
    for sb in range(4):
        left = jnp.broadcast_to(by_sublane[:, first_row + sb : first_row + sb + 1], square)
        for tb in range(2):
            d = tb - sb + 2
            place = (slice(sb * LANES, (sb + 1) * LANES), slice(tb * LANES, (tb + 1) * LANES))
            if 0 <= d <= 2:
                same = left == by_lane[first_row + 2 + tb : first_row + 3 + tb, :]
                for component in range(2):
                    kept = jnp.where(same, toeplitz(component, d), 0.0)
                    matrices[block, component, place[0], place[1]] = kept.astype(BF16)
            else:
                for component in range(2):
                    matrices[block, component, place[0], place[1]] = jnp.zeros(square, BF16)


def products_kernel(
    *refs,
    core,
):
    colat_ref, lon_ref, scalar_ref = refs[:3]
    products, turns, polar, azimuth, small, scalars, scalars_sem = refs[-7:]
    if len(refs) == 12:
        refs[4][...] = refs[3][...]

    @pl.when(lax.axis_index("core") == core)
    def _():
        scalars_copy = pltpu.make_async_copy(scalar_ref, scalars, scalars_sem)
        scalars_copy.start()
        rows, _ = colat_ref.shape
        spread_turns(turns, colat_ref[...], 0, 0)
        spread_turns(turns, lon_ref[...], 1, 0)
        fill_tables((polar, azimuth.reshape(2, MULTIPLES * rows, LANES)), turns, small)
        scalars_copy.wait()
        fill_products(products, scalars, (polar, azimuth))


def own_kernel(
    products,
    obs_ref,
    start_ref,
    harmonic_ref,
    taps_ref,
    gram_ref,
    head_ref,
    columns_ref,
    toeplitz_ref,
    design,
    filtered,
    matrices,
    starts,
):
    rows, _ = start_ref.shape
    panel = harmonic_ref.shape[1]
    blocks = rows // 2

    wide = harmonic_ref[...].astype(F32)
    tall = jnp.transpose(jnp.concatenate([wide, jnp.zeros((6, panel), F32)], axis=0))
    for zl in range(4):
        for y in range(4):
            part = tall[zl * 128 + y * 32 : zl * 128 + y * 32 + 32, :]
            low = y * 128 + zl * 32
            degree = jnp.broadcast_to(part[:, 0:1], (32, LANES))
            order = jnp.broadcast_to(part[:, 1:2], (32, LANES))
            columns_ref[0, low : low + 32, :] = degree
            columns_ref[1, low : low + 32, :] = jnp.abs(order)
            columns_ref[2, low : low + 32, :] = jnp.where(order < 0.0, 0.25, 0.0)

    starts[...] = jnp.zeros_like(starts)
    starts[0:rows, :] = start_ref[...].astype(F32)
    by_lane, by_sublane = labels_of(starts[...].astype(BF16))

    for component in range(2):
        padded = jnp.concatenate(
            [taps_ref[component : component + 1, :].astype(F32), jnp.zeros((1, TAPS), F32)], axis=1
        )
        spread = jnp.broadcast_to(padded, (LANES, 2 * TAPS))
        rolled = pltpu.roll(spread, 0, 1, stride=1, stride_axis=0)
        for d in range(3):
            toeplitz_ref[component, d] = rolled[:, d * LANES : (d + 1) * LANES]
    for component in range(2):
        fill_signal(design, component, panel, obs_ref[component : component + 1, :].astype(F32))

    def to_lanes(block):
        for component in range(2):
            for row in (2 * block, 2 * block + 1):
                for low in range(0, panel, 16):
                    tile = products[component, row // 4, pl.ds(low * 4 + row % 4, 16, stride=4), :]
                    design[component, low : low + 16, row * LANES : (row + 1) * LANES] = tile.astype(BF16)

    to_lanes(0)
    for component in range(2):
        head_ref[component] = design[component, :, 0:TAPS]
    for block in range(blocks - 1):
        to_lanes(block + 1)
        fill_matrices(
            matrices, block, 2 * block, by_lane, by_sublane, lambda c, d: toeplitz_ref[c, d]
        )
        for component in range(2):
            window = design[component, :, block * TAPS : block * TAPS + 2 * TAPS]
            low = (component * (blocks - 1) + block) * TAPS
            filtered[:, low : low + TAPS] = dot_nn(window, matrices[block, component]).astype(BF16)
    gram_ref[...] = dot_nt(filtered[...], filtered[0:panel, :])


def edge_kernel(
    near_ref,
    far_ref,
    start_ref,
    before_ref,
    head_ref,
    columns_ref,
    toeplitz_ref,
    out_ref,
    design,
    filtered,
    matrices,
    turns,
    starts,
    gram,
    halo_ref,
    *,
    row_scale,
    gram_scale,
):
    panel = columns_ref.shape[1]
    halo_ref[...] = near_ref[...] + far_ref[...]
    spread_turns(turns, halo_ref[0:2, :], 0, 0)
    spread_turns(turns, halo_ref[2:4, :], 1, 0)

    square = (LANES, LANES)
    starts[...] = jnp.zeros_like(starts)
    starts[0:2, :] = halo_ref[8:10, :]
    starts[2:4, :] = start_ref[0:2, :].astype(F32)
    by_lane, by_sublane = labels_of(starts[...].astype(BF16))
    lonely = 1.0 - halo_ref[10:11, :]
    by_lane = by_lane + jnp.where(iota(square, 0) >= 2, lonely, 0.0)
    by_sublane = by_sublane + jnp.where(iota(square, 1) >= 2, lonely, 0.0)
    fill_matrices(matrices, 0, 0, by_lane, by_sublane, lambda c, d: toeplitz_ref[c, d])

    fill_design(design, columns_ref, turns, 2)
    for component in range(2):
        low = 4 + 2 * component
        halo = jnp.concatenate([halo_ref[low : low + 1, :], halo_ref[low + 1 : low + 2, :]], axis=1)
        fill_signal(design, component, panel, halo)
        sums = dot_nn(design[component], matrices[0, component, 0:TAPS, :]) + dot_nn(
            head_ref[component], matrices[0, component, TAPS : 2 * TAPS, :]
        )
        filtered[:, component * TAPS : (component + 1) * TAPS] = sums.astype(BF16)

    gram[...] = before_ref[...] + dot_nt(filtered[...], filtered[0:panel, :])

    eye = iota(square, 0) == iota(square, 1)
    rhs = [gram[panel : panel + 1, y * LANES : (y + 1) * LANES] * gram_scale for y in range(4)]
    diagonal = [
        jnp.sum(
            jnp.where(eye, gram[y * LANES : (y + 1) * LANES, y * LANES : (y + 1) * LANES], 0.0),
            axis=0,
            keepdims=True,
        )
        * row_scale
        for y in range(4)
    ]
    small = jnp.concatenate(rhs + diagonal, axis=0).astype(BF16)
    for y in range(4):
        for x in range(4):
            for core in range(2):
                peer = y * 8 + x * 2 + core
                for zh in range(4):
                    low = x * 128 + zh * 32 + core * 16
                    out_ref[peer, zh * 16 : zh * 16 + 16, :] = (
                        gram[low : low + 16, y * LANES : (y + 1) * LANES] * gram_scale
                    ).astype(BF16)
                out_ref[peer, 64:72, :] = small


def middle_kernel(in_ref, out_ref):
    total = in_ref[0].astype(F32)
    for peer in range(1, in_ref.shape[0]):
        total = total + in_ref[peer].astype(F32)
    small = total[64:72, :].astype(BF16)
    head = total[0:64, :].astype(BF16)
    tail = (total[0:64, :] - head.astype(F32)).astype(BF16)
    for zl in range(4):
        for zh in range(4):
            peer = zl * 4 + zh
            for b in range(4):
                rows = slice(zh * 16 + 4 * b, zh * 16 + 4 * b + 4)
                lanes = slice(zl * 32, zl * 32 + 32)
                out_ref[peer, 0:4, b * 32 : b * 32 + 32] = head[rows, lanes]
                out_ref[peer, 4:8, b * 32 : b * 32 + 32] = tail[rows, lanes]
            out_ref[peer, 8:16, :] = small


def last_kernel(in_ref, normal_ref, rhs_ref, diagonal_ref):
    total = in_ref[0].astype(F32)
    for peer in range(1, in_ref.shape[0]):
        total = total + in_ref[peer].astype(F32)
    tile = total[0:4, :] + total[4:8, :]
    for b in range(4):
        normal_ref[4 * b : 4 * b + 4, :] = tile[:, b * 32 : b * 32 + 32]
    rows, cols = normal_ref.shape
    row_low = (lax.axis_index("zh") * 8 + lax.axis_index("x") * 2 + lax.axis_index("core")) * rows
    col_low = (lax.axis_index("zl") * 4 + lax.axis_index("y")) * cols
    on_diagonal = row_low + iota((rows, cols), 0) == col_low + iota((rows, cols), 1)
    normal_ref[...] = jnp.where(on_diagonal, 0.0, normal_ref[...])
    for out_ref, low in ((rhs_ref, 8), (diagonal_ref, 12)):
        for zl in range(4):
            for y in range(4):
                out_ref[0:1, zl * 128 + y * 32 : zl * 128 + y * 32 + 32] = total[
                    low + y : low + y + 1, zl * 32 : zl * 32 + 32
                ]


def load_kernel(*refs):
    count = (len(refs) - 3) // 2
    sources, packed_ref, rows_ref = refs[:count], refs[count], refs[count + 1]
    targets, sems = refs[count + 2 : -1], refs[-1]
    copies = [
        pltpu.make_async_copy(source, target, sems.at[index])
        for index, (source, target) in enumerate(zip(sources, targets))
    ]
    for copy in copies:
        copy.start()
    for copy in copies:
        copy.wait()
    colat_ref, lon_ref, obs_ref, start_ref = targets[:4]
    last = colat_ref.shape[0] - 2
    span = obs_ref.shape[1]
    packed_ref[0:2, :] = colat_ref[last : last + 2, :]
    packed_ref[2:4, :] = lon_ref[last : last + 2, :]
    for component in range(2):
        for half in range(2):
            low = span - (2 - half) * LANES
            row = 4 + 2 * component + half
            packed_ref[row : row + 1, :] = obs_ref[component : component + 1, low : low + LANES].astype(
                F32
            )
    packed_ref[8:10, :] = start_ref[last : last + 2, :].astype(F32)
    packed_ref[10:16, :] = jnp.ones((6, LANES), F32)
    rows = colat_ref.shape[0]
    degree = targets[4][0:1, :]
    order = targets[4][1:2, :]
    wave = jnp.abs(order) + jnp.where(order < 0, MULTIPLES, 0)
    for y in range(4):
        for zl in range(4):
            group = y * 4 + zl
            lanes = slice(zl * LANES + y * 32, zl * LANES + y * 32 + 32)
            rows_ref[group : group + 1, 0:32] = degree[:, lanes] * rows
            rows_ref[16 + group : 17 + group, 0:32] = wave[:, lanes] * rows


def on_device(colatitude, longitude, observed, filter_taps, segment_start, harmonic):
    rows_here = colatitude.shape[0]
    panel = harmonic.shape[1]
    blocks = rows_here // TAPS
    rows_total = rows_here * 512
    vmem = pl.BlockSpec(memory_space=pltpu.VMEM)
    hbm = pl.BlockSpec(memory_space=pltpu.HBM)

    def kernel(body, name, outs, scratch, mebibytes, operands, estimate=None):
        return pl.pallas_call(
            body,
            name=name,
            out_shape=outs,
            in_specs=[vmem] * len(operands),
            out_specs=jax.tree.map(lambda _: vmem, outs),
            scratch_shapes=scratch,
            cost_estimate=estimate,
            compiler_params=pltpu.CompilerParams(vmem_limit_bytes=mebibytes * 1024 * 1024),
        )(*operands)

    colat = colatitude.reshape(-1, LANES)
    lon = longitude.reshape(-1, LANES)
    start = segment_start.reshape(-1, LANES)
    arguments = (colat, lon, observed, start, harmonic, filter_taps)
    packed, table_rows, colat, lon, observed, start, harmonic, filter_taps = pl.pallas_call(
        load_kernel,
        name="load_and_pack",
        out_shape=(
            jax.ShapeDtypeStruct((16, LANES), F32),
            jax.ShapeDtypeStruct((32, LANES), jnp.int32),
            *(jax.ShapeDtypeStruct(value.shape, value.dtype) for value in arguments),
        ),
        in_specs=[hbm] * len(arguments),
        out_specs=(vmem,) * (len(arguments) + 2),
        scratch_shapes=[pltpu.SemaphoreType.DMA((len(arguments),))],
        compiler_params=pltpu.CompilerParams(vmem_limit_bytes=4 * 1024 * 1024),
    )(*(pltpu.with_memory_space_constraint(value, pltpu.HBM) for value in arguments))
    ring = ("zh", "x", "core")
    halo_near = lax.ppermute(packed, ring, [(i, i + 1) for i in range(0, 31, 2)])
    sub_rows = rows_here // LANES

    def products_on(core, *before):
        operands = (colat, lon, table_rows, *(before or (packed,)))
        outs = [jax.ShapeDtypeStruct((2, sub_rows // 4, panel * 4, LANES), F32)]
        if not before:
            outs.insert(0, jax.ShapeDtypeStruct((16, LANES), F32))
        return pl.pallas_call(
            functools.partial(products_kernel, core=core),
            name=f"products_on_core_{core}",
            out_shape=outs,
            in_specs=[vmem] * len(operands),
            out_specs=[vmem] * len(outs),
            scratch_shapes=[
                pltpu.VMEM((4, sub_rows, LANES), F32),
                pltpu.VMEM((2, MULTIPLES * sub_rows, LANES), F32),
                pltpu.VMEM((2 * MULTIPLES * sub_rows, LANES), F32),
                pltpu.VMEM((2, 2, 16, sub_rows, LANES), F32),
                pltpu.SMEM((32, LANES), jnp.int32),
                pltpu.SemaphoreType.DMA(()),
            ],
            input_output_aliases={3: 0} if before else {},
            cost_estimate=pl.CostEstimate(
                flops=40_000_000, bytes_accessed=8_000_000, transcendentals=0
            ),
            compiler_params=pltpu.CompilerParams(vmem_limit_bytes=16 * 1024 * 1024),
        )(*operands)

    packed_again, products = products_on(1)
    halo_far = lax.ppermute(packed_again, ring, [(i, i + 1) for i in range(1, 31, 2)])
    (products,) = products_on(0, products)
    before, head, columns, toeplitz = kernel(
        own_kernel,
        "own_epochs",
        (
            jax.ShapeDtypeStruct((panel + 16, panel), F32),
            jax.ShapeDtypeStruct((2, panel + 16, TAPS), BF16),
            jax.ShapeDtypeStruct((3, panel, LANES), F32),
            jax.ShapeDtypeStruct((2, 3, LANES, LANES), F32),
        ),
        [
            pltpu.VMEM((2, panel + 16, rows_here), BF16),
            pltpu.VMEM((panel + 16, 2 * (rows_here - TAPS)), BF16),
            pltpu.VMEM((blocks - 1, 2, 2 * TAPS, TAPS), BF16),
            pltpu.VMEM((LANES, LANES), F32),
        ],
        24,
        (products, observed, start, harmonic, filter_taps),
        pl.CostEstimate(flops=4_000_000_000, bytes_accessed=4_000_000, transcendentals=0),
    )
    payload = kernel(
        functools.partial(
            edge_kernel, row_scale=1.0 / rows_total, gram_scale=1.0 / math.sqrt(rows_total)
        ),
        "edge_epochs",
        jax.ShapeDtypeStruct((32, 72, LANES), BF16),
        [
            pltpu.VMEM((2, panel + 16, TAPS), BF16),
            pltpu.VMEM((panel + 16, 2 * TAPS), BF16),
            pltpu.VMEM((1, 2, 2 * TAPS, TAPS), BF16),
            pltpu.VMEM((4, 8, LANES), F32),
            pltpu.VMEM((LANES, LANES), F32),
            pltpu.VMEM((panel + 16, panel), F32),
            pltpu.VMEM((16, LANES), F32),
        ],
        16,
        (halo_near, halo_far, start, before, head, columns, toeplitz),
    )
    arrived = lax.all_to_all(payload, ("y", "x", "core"), 0, 0)
    sums = kernel(
        middle_kernel, "sum_over_plane", jax.ShapeDtypeStruct((16, 16, LANES), BF16), [], 8, (arrived,)
    )
    gathered = lax.all_to_all(sums, ("zl", "zh"), 0, 0)
    normal, right_side, diagonal = kernel(
        last_kernel,
        "sum_over_z",
        (
            jax.ShapeDtypeStruct((16, 32), F32),
            jax.ShapeDtypeStruct((1, panel), F32),
            jax.ShapeDtypeStruct((1, panel), F32),
        ),
        [],
        8,
        (gathered,),
    )
    return normal, right_side.reshape(panel), diagonal.reshape(panel)


def solution(mesh):
    fine = Mesh(mesh.devices.reshape(4, 4, 4, 4, 2), ("zl", "y", "zh", "x", "core"))
    everywhere = ("zl", "y", "zh", "x", "core")
    return jax.shard_map(
        on_device,
        mesh=fine,
        in_specs=(P(everywhere), P(everywhere), P(None, everywhere), P(), P(everywhere), P()),
        out_specs=(P(("zh", "x", "core"), ("zl", "y")), P(), P()),
        check_vma=False,
    )
```

```python
import functools
import math

import jax
import jax.numpy as jnp
from jax import lax
from jax.experimental import pallas as pl
from jax.experimental.pallas import tpu as pltpu
from jax.sharding import Mesh, PartitionSpec as P

F32 = jnp.float32
BF16 = jnp.bfloat16
LANES = 128
TAPS = 256
MULTIPLES = 288
SIN_COEFFS = (3.141592639, -5.167709953, 2.550074404, -0.5982681334, 0.07760505745)
COS_COEFFS = (0.9999999504, -4.934792377, 4.058400535, -1.331796279, 0.2195071918)
TWO_PI_PARTS = (6.28125, 0.0019340515136718750, 1.2556659146854654e-06)
HALF_UP = 1.5 * 2.0**23


def horner(coeffs, z):
    total = z * coeffs[-1] + coeffs[-2]
    for coeff in coeffs[-3::-1]:
        total = total * z + coeff
    return total


def nearest(value):
    return (value + HALF_UP) - HALF_UP


def turns_of(angle):
    coarse = nearest(angle * (65536.0 / (2.0 * math.pi))) * (1.0 / 65536.0)
    rest = angle
    for part in TWO_PI_PARTS:
        rest = rest - coarse * part
    return coarse, rest * (1.0 / (2.0 * math.pi))


def dot_nt(a, b):
    return lax.dot_general(a, b, (((1,), (1,)), ((), ())), preferred_element_type=F32)


def dot_nn(a, b):
    return lax.dot_general(a, b, (((1,), (0,)), ((), ())), preferred_element_type=F32)


def iota(shape, axis):
    return lax.broadcasted_iota(jnp.int32, shape, axis)


def spread_turns(turns, angle, slot, low):
    coarse, fine = turns_of(angle)
    turns[2 * slot, low : low + angle.shape[0], :] = coarse
    turns[2 * slot + 1, low : low + angle.shape[0], :] = fine


def fill_design(design, columns, turns, chunks):
    def some_columns(step, carry):
        low = pl.multiple_of(step * 32, 32)
        degree = columns[0, pl.ds(low, 32), :]
        order = columns[1, pl.ds(low, 32), :]
        phase = columns[2, pl.ds(low, 32), :]
        for chunk in range(chunks):
            row = slice(chunk, chunk + 1)
            lane = slice(chunk * LANES, (chunk + 1) * LANES)
            polar = degree * turns[0, row, :]
            polar = (polar - nearest(polar)) + degree * turns[1, row, :]
            z = polar * polar
            half_sin = polar * horner(SIN_COEFFS, z)
            half_cos = horner(COS_COEFFS, z)
            twice = half_sin + half_sin
            cos_polar = 1.0 - twice * half_sin
            sin_polar = twice * half_cos
            azimuth = order * turns[2, row, :] - phase
            azimuth = (azimuth - nearest(azimuth)) + order * turns[3, row, :]
            half = azimuth * horner(SIN_COEFFS, azimuth * azimuth)
            wave = 1.0 - (half + half) * half
            design[0, pl.ds(low, 32), lane] = (cos_polar * wave).astype(BF16)
            design[1, pl.ds(low, 32), lane] = (sin_polar * wave).astype(BF16)
        return carry

    lax.fori_loop(0, columns.shape[1] // 32, some_columns, 0)


def sine_and_cosine(turns, slot, factor):
    part = turns[2 * slot] * factor
    part = (part - nearest(part)) + turns[2 * slot + 1] * factor
    z = part * part
    half_sin = part * horner(SIN_COEFFS, z)
    twice = half_sin + half_sin
    return twice * horner(COS_COEFFS, z), 1.0 - twice * half_sin


def fill_tables(tables, turns, small):
    rows = turns.shape[1]
    for slot in range(2):
        for b in range(16):
            sine, cosine = sine_and_cosine(turns, slot, float(b))
            small[slot, 0, b] = cosine
            small[slot, 1, b] = sine

    def some_multiples(a, carry):
        for slot, table in enumerate(tables):
            sine, cosine = sine_and_cosine(turns, slot, (16 * a).astype(F32))
            for b in range(16):
                place = pl.ds(pl.multiple_of(a * (16 * rows), 16 * rows) + b * rows, rows)
                table[0, place, :] = cosine * small[slot, 0, b] - sine * small[slot, 1, b]
                table[1, place, :] = sine * small[slot, 0, b] + cosine * small[slot, 1, b]
        return carry

    lax.fori_loop(0, MULTIPLES // 16, some_multiples, 0)


def fill_products(products, rows_of, tables):
    polar, azimuth = tables
    rows = 4 * products.shape[1]
    upper = iota((8, LANES), 0) >= 4

    def some_columns(group, carry):
        start = pl.multiple_of(group * 128, 128)
        for pair in range(16):
            values = []
            for offset in (2 * pair, 2 * pair + 1):
                degree = pl.multiple_of(rows_of[group, offset], rows)
                order = pl.multiple_of(rows_of[16 + group, offset], rows)
                wave = azimuth[pl.ds(order, rows), :]
                values.append([polar[c, pl.ds(degree, rows), :] * wave for c in range(2)])
            place = pl.ds(start + pair * 8, 8)
            for component in range(2):
                for half in range(rows // 8):
                    one = values[0][component][8 * half : 8 * half + 8, :]
                    two = values[1][component][8 * half : 8 * half + 8, :]
                    products[component, 2 * half, place, :] = jnp.where(upper, pltpu.roll(two, 4, 0), one)
                    products[component, 2 * half + 1, place, :] = jnp.where(
                        upper, two, pltpu.roll(one, 4, 0)
                    )
        return carry

    lax.fori_loop(0, 16, some_columns, 0)


def fill_signal(design, component, panel, values):
    span = values.shape[1]
    design[component, panel : panel + 16, 0:span] = jnp.where(
        iota((16, span), 0) == 0, values, 0.0
    ).astype(BF16)


def labels_of(flags):
    square = (LANES, LANES)
    low_tri = (iota(square, 0) >= iota(square, 1)).astype(BF16)
    up_tri = (iota(square, 0) <= iota(square, 1)).astype(BF16)
    low_strict = (iota(square, 0) > iota(square, 1)).astype(BF16)
    up_strict = (iota(square, 0) < iota(square, 1)).astype(BF16)
    ones = jnp.ones(square, BF16)
    by_lane = dot_nn(flags, up_tri) + dot_nn(dot_nn(low_strict, flags).astype(BF16), ones)
    by_sublane = dot_nt(low_tri, flags) + dot_nn(dot_nt(ones, flags).astype(BF16), up_strict)
    return by_lane, by_sublane


def fill_matrices(matrices, block, first_row, by_lane, by_sublane, toeplitz):
    square = (LANES, LANES)
    for sb in range(4):
        left = jnp.broadcast_to(by_sublane[:, first_row + sb : first_row + sb + 1], square)
        for tb in range(2):
            d = tb - sb + 2
            place = (slice(sb * LANES, (sb + 1) * LANES), slice(tb * LANES, (tb + 1) * LANES))
            if 0 <= d <= 2:
                same = left == by_lane[first_row + 2 + tb : first_row + 3 + tb, :]
                for component in range(2):
                    kept = jnp.where(same, toeplitz(component, d), 0.0)
                    matrices[block, component, place[0], place[1]] = kept.astype(BF16)
            else:
                for component in range(2):
                    matrices[block, component, place[0], place[1]] = jnp.zeros(square, BF16)


def products_kernel(
    *refs,
    core,
):
    colat_ref, lon_ref, scalar_ref = refs[:3]
    products, turns, polar, azimuth, small, scalars, scalars_sem = refs[-7:]
    if len(refs) == 12:
        refs[4][...] = refs[3][...]

    @pl.when(lax.axis_index("core") == core)
    def _():
        scalars_copy = pltpu.make_async_copy(scalar_ref, scalars, scalars_sem)
        scalars_copy.start()
        rows, _ = colat_ref.shape
        spread_turns(turns, colat_ref[...], 0, 0)
        spread_turns(turns, lon_ref[...], 1, 0)
        fill_tables((polar, azimuth.reshape(2, MULTIPLES * rows, LANES)), turns, small)
        scalars_copy.wait()
        fill_products(products, scalars, (polar, azimuth))


def three_quadrants(filtered, panel):
    half = panel // 2
    upper = jnp.concatenate([filtered[0:half, :], filtered[panel : panel + 16, :]], axis=0)
    lower = filtered[half:panel, :]
    return dot_nt(upper, filtered[0:panel, :]), dot_nt(lower, lower)


def own_kernel(
    products,
    obs_ref,
    start_ref,
    harmonic_ref,
    taps_ref,
    gram_ref,
    head_ref,
    columns_ref,
    toeplitz_ref,
    design,
    filtered,
    matrices,
    starts,
):
    rows, _ = start_ref.shape
    panel = harmonic_ref.shape[1]
    blocks = rows // 2

    wide = harmonic_ref[...].astype(F32)
    tall = jnp.transpose(jnp.concatenate([wide, jnp.zeros((6, panel), F32)], axis=0))
    for zl in range(4):
        for y in range(4):
            part = tall[zl * 128 + y * 32 : zl * 128 + y * 32 + 32, :]
            low = y * 128 + zl * 32
            degree = jnp.broadcast_to(part[:, 0:1], (32, LANES))
            order = jnp.broadcast_to(part[:, 1:2], (32, LANES))
            columns_ref[0, low : low + 32, :] = degree
            columns_ref[1, low : low + 32, :] = jnp.abs(order)
            columns_ref[2, low : low + 32, :] = jnp.where(order < 0.0, 0.25, 0.0)

    starts[...] = jnp.zeros_like(starts)
    starts[0:rows, :] = start_ref[...].astype(F32)
    by_lane, by_sublane = labels_of(starts[...].astype(BF16))

    for component in range(2):
        padded = jnp.concatenate(
            [taps_ref[component : component + 1, :].astype(F32), jnp.zeros((1, TAPS), F32)], axis=1
        )
        spread = jnp.broadcast_to(padded, (LANES, 2 * TAPS))
        rolled = pltpu.roll(spread, 0, 1, stride=1, stride_axis=0)
        for d in range(3):
            toeplitz_ref[component, d] = rolled[:, d * LANES : (d + 1) * LANES]
    for component in range(2):
        fill_signal(design, component, panel, obs_ref[component : component + 1, :].astype(F32))

    def to_lanes(block):
        for component in range(2):
            for row in (2 * block, 2 * block + 1):
                for low in range(0, panel, 16):
                    tile = products[component, row // 4, pl.ds(low * 4 + row % 4, 16, stride=4), :]
                    design[component, low : low + 16, row * LANES : (row + 1) * LANES] = tile.astype(BF16)

    to_lanes(0)
    for component in range(2):
        head_ref[component] = design[component, :, 0:TAPS]
    for block in range(blocks - 1):
        to_lanes(block + 1)
        fill_matrices(
            matrices, block, 2 * block, by_lane, by_sublane, lambda c, d: toeplitz_ref[c, d]
        )
        for component in range(2):
            window = design[component, :, block * TAPS : block * TAPS + 2 * TAPS]
            low = (component * (blocks - 1) + block) * TAPS
            filtered[:, low : low + TAPS] = dot_nn(window, matrices[block, component]).astype(BF16)
    upper, lower = three_quadrants(filtered, panel)
    half = panel // 2
    gram_ref[0 : half + 16, :] = upper
    gram_ref[half + 16 : panel + 16, half:panel] = lower


def edge_kernel(
    near_ref,
    far_ref,
    start_ref,
    before_ref,
    head_ref,
    columns_ref,
    toeplitz_ref,
    out_ref,
    design,
    filtered,
    matrices,
    turns,
    starts,
    gram,
    halo_ref,
    *,
    row_scale,
    gram_scale,
):
    panel = columns_ref.shape[1]
    halo_ref[...] = near_ref[...] + far_ref[...]
    spread_turns(turns, halo_ref[0:2, :], 0, 0)
    spread_turns(turns, halo_ref[2:4, :], 1, 0)

    square = (LANES, LANES)
    starts[...] = jnp.zeros_like(starts)
    starts[0:2, :] = halo_ref[8:10, :]
    starts[2:4, :] = start_ref[0:2, :].astype(F32)
    by_lane, by_sublane = labels_of(starts[...].astype(BF16))
    lonely = 1.0 - halo_ref[10:11, :]
    by_lane = by_lane + jnp.where(iota(square, 0) >= 2, lonely, 0.0)
    by_sublane = by_sublane + jnp.where(iota(square, 1) >= 2, lonely, 0.0)
    fill_matrices(matrices, 0, 0, by_lane, by_sublane, lambda c, d: toeplitz_ref[c, d])

    fill_design(design, columns_ref, turns, 2)
    for component in range(2):
        low = 4 + 2 * component
        halo = jnp.concatenate([halo_ref[low : low + 1, :], halo_ref[low + 1 : low + 2, :]], axis=1)
        fill_signal(design, component, panel, halo)
        sums = dot_nn(design[component], matrices[0, component, 0:TAPS, :]) + dot_nn(
            head_ref[component], matrices[0, component, TAPS : 2 * TAPS, :]
        )
        filtered[:, component * TAPS : (component + 1) * TAPS] = sums.astype(BF16)

    upper, lower = three_quadrants(filtered, panel)
    half = panel // 2
    upper = upper + before_ref[0 : half + 16, :]
    gram[0:half, :] = upper[0:half, :]
    gram[panel : panel + 16, :] = upper[half : half + 16, :]
    gram[half:panel, half:panel] = lower + before_ref[half + 16 : panel + 16, half:panel]
    gram[half:panel, 0:half] = jnp.transpose(upper[0:half, half:panel])

    eye = iota(square, 0) == iota(square, 1)
    rhs = [gram[panel : panel + 1, y * LANES : (y + 1) * LANES] * gram_scale for y in range(4)]
    diagonal = [
        jnp.sum(
            jnp.where(eye, gram[y * LANES : (y + 1) * LANES, y * LANES : (y + 1) * LANES], 0.0),
            axis=0,
            keepdims=True,
        )
        * row_scale
        for y in range(4)
    ]
    small = jnp.concatenate(rhs + diagonal, axis=0).astype(BF16)
    for y in range(4):
        for x in range(4):
            for core in range(2):
                peer = y * 8 + x * 2 + core
                for zh in range(4):
                    low = x * 128 + zh * 32 + core * 16
                    out_ref[peer, zh * 16 : zh * 16 + 16, :] = (
                        gram[low : low + 16, y * LANES : (y + 1) * LANES] * gram_scale
                    ).astype(BF16)
                out_ref[peer, 64:72, :] = small


def middle_kernel(in_ref, out_ref):
    total = in_ref[0].astype(F32)
    for peer in range(1, in_ref.shape[0]):
        total = total + in_ref[peer].astype(F32)
    rounded = total.astype(BF16)
    for zl in range(4):
        for zh in range(4):
            low = 3 * (zl * 4 + zh)
            for b in range(4):
                out_ref[low, :, b * 32 : b * 32 + 32] = rounded[
                    zh * 16 + 4 * b : zh * 16 + 4 * b + 4, zl * 32 : zl * 32 + 32
                ]
            out_ref[low + 1] = rounded[64:68, :]
            out_ref[low + 2] = rounded[68:72, :]


def last_kernel(in_ref, normal_ref, rhs_ref, diagonal_ref):
    totals = []
    for part in range(3):
        total = in_ref[part].astype(F32)
        for peer in range(1, in_ref.shape[0] // 3):
            total = total + in_ref[3 * peer + part].astype(F32)
        totals.append(total)
    for b in range(4):
        normal_ref[4 * b : 4 * b + 4, :] = totals[0][:, b * 32 : b * 32 + 32]
    rows, cols = normal_ref.shape
    row_low = (lax.axis_index("zh") * 8 + lax.axis_index("x") * 2 + lax.axis_index("core")) * rows
    col_low = (lax.axis_index("zl") * 4 + lax.axis_index("y")) * cols
    on_diagonal = row_low + iota((rows, cols), 0) == col_low + iota((rows, cols), 1)
    normal_ref[...] = jnp.where(on_diagonal, 0.0, normal_ref[...])
    for out_ref, total in ((rhs_ref, totals[1]), (diagonal_ref, totals[2])):
        for zl in range(4):
            for y in range(4):
                out_ref[0:1, zl * 128 + y * 32 : zl * 128 + y * 32 + 32] = total[
                    y : y + 1, zl * 32 : zl * 32 + 32
                ]


def load_kernel(*refs):
    count = (len(refs) - 3) // 2
    sources, packed_ref, rows_ref = refs[:count], refs[count], refs[count + 1]
    targets, sems = refs[count + 2 : -1], refs[-1]
    copies = [
        pltpu.make_async_copy(source, target, sems.at[index])
        for index, (source, target) in enumerate(zip(sources, targets))
    ]
    for copy in copies:
        copy.start()
    for copy in copies:
        copy.wait()
    colat_ref, lon_ref, obs_ref, start_ref = targets[:4]
    last = colat_ref.shape[0] - 2
    span = obs_ref.shape[1]
    packed_ref[0:2, :] = colat_ref[last : last + 2, :]
    packed_ref[2:4, :] = lon_ref[last : last + 2, :]
    for component in range(2):
        for half in range(2):
            low = span - (2 - half) * LANES
            row = 4 + 2 * component + half
            packed_ref[row : row + 1, :] = obs_ref[component : component + 1, low : low + LANES].astype(
                F32
            )
    packed_ref[8:10, :] = start_ref[last : last + 2, :].astype(F32)
    packed_ref[10:16, :] = jnp.ones((6, LANES), F32)
    rows = colat_ref.shape[0]
    degree = targets[4][0:1, :]
    order = targets[4][1:2, :]
    wave = jnp.abs(order) + jnp.where(order < 0, MULTIPLES, 0)
    for y in range(4):
        for zl in range(4):
            group = y * 4 + zl
            lanes = slice(zl * LANES + y * 32, zl * LANES + y * 32 + 32)
            rows_ref[group : group + 1, 0:32] = degree[:, lanes] * rows
            rows_ref[16 + group : 17 + group, 0:32] = wave[:, lanes] * rows


def on_device(colatitude, longitude, observed, filter_taps, segment_start, harmonic):
    rows_here = colatitude.shape[0]
    panel = harmonic.shape[1]
    blocks = rows_here // TAPS
    rows_total = rows_here * 512
    vmem = pl.BlockSpec(memory_space=pltpu.VMEM)
    hbm = pl.BlockSpec(memory_space=pltpu.HBM)

    def kernel(body, name, outs, scratch, mebibytes, operands, estimate=None):
        return pl.pallas_call(
            body,
            name=name,
            out_shape=outs,
            in_specs=[vmem] * len(operands),
            out_specs=jax.tree.map(lambda _: vmem, outs),
            scratch_shapes=scratch,
            cost_estimate=estimate,
            compiler_params=pltpu.CompilerParams(vmem_limit_bytes=mebibytes * 1024 * 1024),
        )(*operands)

    colat = colatitude.reshape(-1, LANES)
    lon = longitude.reshape(-1, LANES)
    start = segment_start.reshape(-1, LANES)
    arguments = (colat, lon, observed, start, harmonic, filter_taps)
    packed, table_rows, colat, lon, observed, start, harmonic, filter_taps = pl.pallas_call(
        load_kernel,
        name="load_and_pack",
        out_shape=(
            jax.ShapeDtypeStruct((16, LANES), F32),
            jax.ShapeDtypeStruct((32, LANES), jnp.int32),
            *(jax.ShapeDtypeStruct(value.shape, value.dtype) for value in arguments),
        ),
        in_specs=[hbm] * len(arguments),
        out_specs=(vmem,) * (len(arguments) + 2),
        scratch_shapes=[pltpu.SemaphoreType.DMA((len(arguments),))],
        compiler_params=pltpu.CompilerParams(vmem_limit_bytes=4 * 1024 * 1024),
    )(*(pltpu.with_memory_space_constraint(value, pltpu.HBM) for value in arguments))
    ring = ("zh", "x", "core")
    halo_near = lax.ppermute(packed, ring, [(i, i + 1) for i in range(0, 31, 2)])
    sub_rows = rows_here // LANES

    def products_on(core, *before):
        operands = (colat, lon, table_rows, *(before or (packed,)))
        outs = [jax.ShapeDtypeStruct((2, sub_rows // 4, panel * 4, LANES), F32)]
        if not before:
            outs.insert(0, jax.ShapeDtypeStruct((16, LANES), F32))
        return pl.pallas_call(
            functools.partial(products_kernel, core=core),
            name=f"products_on_core_{core}",
            out_shape=outs,
            in_specs=[vmem] * len(operands),
            out_specs=[vmem] * len(outs),
            scratch_shapes=[
                pltpu.VMEM((4, sub_rows, LANES), F32),
                pltpu.VMEM((2, MULTIPLES * sub_rows, LANES), F32),
                pltpu.VMEM((2 * MULTIPLES * sub_rows, LANES), F32),
                pltpu.VMEM((2, 2, 16, sub_rows, LANES), F32),
                pltpu.SMEM((32, LANES), jnp.int32),
                pltpu.SemaphoreType.DMA(()),
            ],
            input_output_aliases={3: 0} if before else {},
            cost_estimate=pl.CostEstimate(
                flops=40_000_000, bytes_accessed=8_000_000, transcendentals=0
            ),
            compiler_params=pltpu.CompilerParams(vmem_limit_bytes=16 * 1024 * 1024),
        )(*operands)

    packed_again, products = products_on(1)
    halo_far = lax.ppermute(packed_again, ring, [(i, i + 1) for i in range(1, 31, 2)])
    (products,) = products_on(0, products)
    before, head, columns, toeplitz = kernel(
        own_kernel,
        "own_epochs",
        (
            jax.ShapeDtypeStruct((panel + 16, panel), F32),
            jax.ShapeDtypeStruct((2, panel + 16, TAPS), BF16),
            jax.ShapeDtypeStruct((3, panel, LANES), F32),
            jax.ShapeDtypeStruct((2, 3, LANES, LANES), F32),
        ),
        [
            pltpu.VMEM((2, panel + 16, rows_here), BF16),
            pltpu.VMEM((panel + 16, 2 * (rows_here - TAPS)), BF16),
            pltpu.VMEM((blocks - 1, 2, 2 * TAPS, TAPS), BF16),
            pltpu.VMEM((LANES, LANES), F32),
        ],
        24,
        (products, observed, start, harmonic, filter_taps),
        pl.CostEstimate(flops=4_000_000_000, bytes_accessed=4_000_000, transcendentals=0),
    )
    payload = kernel(
        functools.partial(
            edge_kernel, row_scale=1.0 / rows_total, gram_scale=1.0 / math.sqrt(rows_total)
        ),
        "edge_epochs",
        jax.ShapeDtypeStruct((32, 72, LANES), BF16),
        [
            pltpu.VMEM((2, panel + 16, TAPS), BF16),
            pltpu.VMEM((panel + 16, 2 * TAPS), BF16),
            pltpu.VMEM((1, 2, 2 * TAPS, TAPS), BF16),
            pltpu.VMEM((4, 8, LANES), F32),
            pltpu.VMEM((LANES, LANES), F32),
            pltpu.VMEM((panel + 16, panel), F32),
            pltpu.VMEM((16, LANES), F32),
        ],
        16,
        (halo_near, halo_far, start, before, head, columns, toeplitz),
    )
    arrived = lax.all_to_all(payload, ("y", "x", "core"), 0, 0)
    sums = kernel(
        middle_kernel, "sum_over_plane", jax.ShapeDtypeStruct((48, 4, LANES), BF16), [], 8, (arrived,)
    )
    gathered = lax.all_to_all(sums, ("zl", "zh"), 0, 0, tiled=True)
    normal, right_side, diagonal = kernel(
        last_kernel,
        "sum_over_z",
        (
            jax.ShapeDtypeStruct((16, 32), F32),
            jax.ShapeDtypeStruct((1, panel), F32),
            jax.ShapeDtypeStruct((1, panel), F32),
        ),
        [],
        8,
        (gathered,),
    )
    return normal, right_side.reshape(panel), diagonal.reshape(panel)


def solution(mesh):
    fine = Mesh(mesh.devices.reshape(4, 4, 4, 4, 2), ("zl", "y", "zh", "x", "core"))
    everywhere = ("zl", "y", "zh", "x", "core")
    return jax.shard_map(
        on_device,
        mesh=fine,
        in_specs=(P(everywhere), P(everywhere), P(None, everywhere), P(), P(everywhere), P()),
        out_specs=(P(("zh", "x", "core"), ("zl", "y")), P(), P()),
        check_vma=False,
    )
```

```python
import functools
import math

import jax
import jax.numpy as jnp
from jax import lax
from jax.experimental import pallas as pl
from jax.experimental.pallas import tpu as pltpu
from jax.sharding import Mesh, PartitionSpec as P


F32 = jnp.float32
BF16 = jnp.bfloat16
LANES = 128
TAPS = 256
MULTIPLES = 288
SIN_COEFFS = (3.141592639, -5.167709953, 2.550074404, -0.5982681334, 0.07760505745)
COS_COEFFS = (0.9999999504, -4.934792377, 4.058400535, -1.331796279, 0.2195071918)
TWO_PI_PARTS = (6.28125, 0.0019340515136718750, 1.2556659146854654e-06)
HALF_UP = 1.5 * 2.0**23


def horner(coeffs, z):
    total = z * coeffs[-1] + coeffs[-2]
    for coeff in coeffs[-3::-1]:
        total = total * z + coeff
    return total


def nearest(value):
    return (value + HALF_UP) - HALF_UP


def turns_of(angle):
    coarse = nearest(angle * (65536.0 / (2.0 * math.pi))) * (1.0 / 65536.0)
    rest = angle
    for part in TWO_PI_PARTS:
        rest = rest - coarse * part
    return coarse, rest * (1.0 / (2.0 * math.pi))


def dot_nt(a, b):
    return lax.dot_general(a, b, (((1,), (1,)), ((), ())), preferred_element_type=F32)


def dot_nn(a, b):
    return lax.dot_general(a, b, (((1,), (0,)), ((), ())), preferred_element_type=F32)


def iota(shape, axis):
    return lax.broadcasted_iota(jnp.int32, shape, axis)


def spread_turns(turns, angle, slot, low):
    coarse, fine = turns_of(angle)
    turns[2 * slot, low : low + angle.shape[0], :] = coarse
    turns[2 * slot + 1, low : low + angle.shape[0], :] = fine


def fill_design(design, columns, turns, chunks):
    def some_columns(step, carry):
        low = pl.multiple_of(step * 32, 32)
        degree = columns[0, pl.ds(low, 32), :]
        order = columns[1, pl.ds(low, 32), :]
        phase = columns[2, pl.ds(low, 32), :]
        for chunk in range(chunks):
            row = slice(chunk, chunk + 1)
            lane = slice(chunk * LANES, (chunk + 1) * LANES)
            polar = degree * turns[0, row, :]
            polar = (polar - nearest(polar)) + degree * turns[1, row, :]
            z = polar * polar
            half_sin = polar * horner(SIN_COEFFS, z)
            half_cos = horner(COS_COEFFS, z)
            twice = half_sin + half_sin
            cos_polar = 1.0 - twice * half_sin
            sin_polar = twice * half_cos
            azimuth = order * turns[2, row, :] - phase
            azimuth = (azimuth - nearest(azimuth)) + order * turns[3, row, :]
            half = azimuth * horner(SIN_COEFFS, azimuth * azimuth)
            wave = 1.0 - (half + half) * half
            design[0, pl.ds(low, 32), lane] = (cos_polar * wave).astype(BF16)
            design[1, pl.ds(low, 32), lane] = (sin_polar * wave).astype(BF16)
        return carry

    lax.fori_loop(0, columns.shape[1] // 32, some_columns, 0)


def sine_and_cosine(turns, slot, factor):
    part = turns[2 * slot] * factor
    part = (part - nearest(part)) + turns[2 * slot + 1] * factor
    z = part * part
    half_sin = part * horner(SIN_COEFFS, z)
    twice = half_sin + half_sin
    return twice * horner(COS_COEFFS, z), 1.0 - twice * half_sin


def fill_tables(tables, turns, small):
    rows = turns.shape[1]
    for slot in range(2):
        for b in range(16):
            sine, cosine = sine_and_cosine(turns, slot, float(b))
            small[slot, 0, b] = cosine
            small[slot, 1, b] = sine

    def some_multiples(a, carry):
        for slot, table in enumerate(tables):
            sine, cosine = sine_and_cosine(turns, slot, (16 * a).astype(F32))
            for b in range(16):
                place = pl.ds(pl.multiple_of(a * (16 * rows), 16 * rows) + b * rows, rows)
                table[0, place, :] = cosine * small[slot, 0, b] - sine * small[slot, 1, b]
                table[1, place, :] = sine * small[slot, 0, b] + cosine * small[slot, 1, b]
        return carry

    lax.fori_loop(0, MULTIPLES // 16, some_multiples, 0)


def fill_products(products, rows_of, tables):
    polar, azimuth = tables
    rows = 4 * products.shape[1]
    upper = iota((8, LANES), 0) >= 4

    def some_columns(group, carry):
        start = pl.multiple_of(group * 128, 128)
        for pair in range(16):
            values = []
            for offset in (2 * pair, 2 * pair + 1):
                degree = pl.multiple_of(rows_of[group, offset], rows)
                order = pl.multiple_of(rows_of[16 + group, offset], rows)
                wave = azimuth[pl.ds(order, rows), :]
                values.append([polar[c, pl.ds(degree, rows), :] * wave for c in range(2)])
            place = pl.ds(start + pair * 8, 8)
            for component in range(2):
                for half in range(rows // 8):
                    one = values[0][component][8 * half : 8 * half + 8, :]
                    two = values[1][component][8 * half : 8 * half + 8, :]
                    products[component, 2 * half, place, :] = jnp.where(upper, pltpu.roll(two, 4, 0), one)
                    products[component, 2 * half + 1, place, :] = jnp.where(
                        upper, two, pltpu.roll(one, 4, 0)
                    )
        return carry

    lax.fori_loop(0, 16, some_columns, 0)


def fill_signal(design, component, panel, values):
    span = values.shape[1]
    design[component, panel : panel + 16, 0:span] = jnp.where(
        iota((16, span), 0) == 0, values, 0.0
    ).astype(BF16)


def labels_of(flags):
    square = (LANES, LANES)
    low_tri = (iota(square, 0) >= iota(square, 1)).astype(BF16)
    up_tri = (iota(square, 0) <= iota(square, 1)).astype(BF16)
    low_strict = (iota(square, 0) > iota(square, 1)).astype(BF16)
    up_strict = (iota(square, 0) < iota(square, 1)).astype(BF16)
    ones = jnp.ones(square, BF16)
    by_lane = dot_nn(flags, up_tri) + dot_nn(dot_nn(low_strict, flags).astype(BF16), ones)
    by_sublane = dot_nt(low_tri, flags) + dot_nn(dot_nt(ones, flags).astype(BF16), up_strict)
    return by_lane, by_sublane


def fill_matrices(matrices, block, first_row, by_lane, by_sublane, toeplitz):
    square = (LANES, LANES)
    for sb in range(4):
        left = jnp.broadcast_to(by_sublane[:, first_row + sb : first_row + sb + 1], square)
        for tb in range(2):
            d = tb - sb + 2
            place = (slice(sb * LANES, (sb + 1) * LANES), slice(tb * LANES, (tb + 1) * LANES))
            if 0 <= d <= 2:
                same = left == by_lane[first_row + 2 + tb : first_row + 3 + tb, :]
                for component in range(2):
                    kept = jnp.where(same, toeplitz(component, d), 0.0)
                    matrices[block, component, place[0], place[1]] = kept.astype(BF16)
            else:
                for component in range(2):
                    matrices[block, component, place[0], place[1]] = jnp.zeros(square, BF16)


def products_kernel(
    *refs,
    core,
):
    colat_ref, lon_ref, scalar_ref = refs[:3]
    packed_ref = refs[3]
    packed_out, products, turns, polar, azimuth, small, scalars, scalars_sem = refs[-8:]
    packed_out[...] = packed_ref[...]

    @pl.when(lax.axis_index("core") == core)
    def _():
        scalars_copy = pltpu.make_async_copy(scalar_ref, scalars, scalars_sem)
        scalars_copy.start()
        rows, _ = colat_ref.shape
        spread_turns(turns, colat_ref[...], 0, 0)
        spread_turns(turns, lon_ref[...], 1, 0)
        fill_tables((polar, azimuth.reshape(2, MULTIPLES * rows, LANES)), turns, small)
        scalars_copy.wait()
        fill_products(products, scalars, (polar, azimuth))


def three_quadrants(filtered, panel):
    half = panel // 2
    upper = jnp.concatenate([filtered[0:half, :], filtered[panel : panel + 16, :]], axis=0)
    lower = filtered[half:panel, :]
    return dot_nt(upper, filtered[0:panel, :]), dot_nt(lower, lower)


def own_kernel(
    products,
    obs_ref,
    start_ref,
    harmonic_ref,
    taps_ref,
    gram_ref,
    head_ref,
    columns_ref,
    toeplitz_ref,
    design,
    filtered,
    matrices,
    starts,
):
    rows, _ = start_ref.shape
    panel = harmonic_ref.shape[1]
    blocks = rows // 2

    wide = harmonic_ref[...].astype(F32)
    tall = jnp.transpose(jnp.concatenate([wide, jnp.zeros((6, panel), F32)], axis=0))
    for zl in range(4):
        for y in range(4):
            part = tall[zl * 128 + y * 32 : zl * 128 + y * 32 + 32, :]
            low = y * 128 + zl * 32
            degree = jnp.broadcast_to(part[:, 0:1], (32, LANES))
            order = jnp.broadcast_to(part[:, 1:2], (32, LANES))
            columns_ref[0, low : low + 32, :] = degree
            columns_ref[1, low : low + 32, :] = jnp.abs(order)
            columns_ref[2, low : low + 32, :] = jnp.where(order < 0.0, 0.25, 0.0)

    starts[...] = jnp.zeros_like(starts)
    starts[0:rows, :] = start_ref[...].astype(F32)
    by_lane, by_sublane = labels_of(starts[...].astype(BF16))

    for component in range(2):
        padded = jnp.concatenate(
            [taps_ref[component : component + 1, :].astype(F32), jnp.zeros((1, TAPS), F32)], axis=1
        )
        spread = jnp.broadcast_to(padded, (LANES, 2 * TAPS))
        rolled = pltpu.roll(spread, 0, 1, stride=1, stride_axis=0)
        for d in range(3):
            toeplitz_ref[component, d] = rolled[:, d * LANES : (d + 1) * LANES]
    for component in range(2):
        fill_signal(design, component, panel, obs_ref[component : component + 1, :].astype(F32))

    def to_lanes(block):
        for component in range(2):
            for row in (2 * block, 2 * block + 1):
                for low in range(0, panel, 16):
                    tile = products[component, row // 4, pl.ds(low * 4 + row % 4, 16, stride=4), :]
                    design[component, low : low + 16, row * LANES : (row + 1) * LANES] = tile.astype(BF16)

    to_lanes(0)
    for component in range(2):
        head_ref[component] = design[component, :, 0:TAPS]
    for block in range(blocks - 1):
        to_lanes(block + 1)
        fill_matrices(
            matrices, block, 2 * block, by_lane, by_sublane, lambda c, d: toeplitz_ref[c, d]
        )
        for component in range(2):
            window = design[component, :, block * TAPS : block * TAPS + 2 * TAPS]
            low = (component * (blocks - 1) + block) * TAPS
            filtered[:, low : low + TAPS] = dot_nn(window, matrices[block, component]).astype(BF16)
    upper, lower = three_quadrants(filtered, panel)
    half = panel // 2
    gram_ref[0 : half + 16, :] = upper
    gram_ref[half + 16 : panel + 16, half:panel] = lower


def edge_kernel(
    near_ref,
    far_ref,
    start_ref,
    before_ref,
    head_ref,
    columns_ref,
    toeplitz_ref,
    out_ref,
    design,
    filtered,
    matrices,
    turns,
    starts,
    gram,
    halo_ref,
    *,
    row_scale,
    gram_scale,
):
    panel = columns_ref.shape[1]
    halo_ref[...] = near_ref[...] + far_ref[...]
    spread_turns(turns, halo_ref[0:2, :], 0, 0)
    spread_turns(turns, halo_ref[2:4, :], 1, 0)

    square = (LANES, LANES)
    starts[...] = jnp.zeros_like(starts)
    starts[0:2, :] = halo_ref[8:10, :]
    starts[2:4, :] = start_ref[0:2, :].astype(F32)
    by_lane, by_sublane = labels_of(starts[...].astype(BF16))
    lonely = 1.0 - halo_ref[10:11, :]
    by_lane = by_lane + jnp.where(iota(square, 0) >= 2, lonely, 0.0)
    by_sublane = by_sublane + jnp.where(iota(square, 1) >= 2, lonely, 0.0)
    fill_matrices(matrices, 0, 0, by_lane, by_sublane, lambda c, d: toeplitz_ref[c, d])

    fill_design(design, columns_ref, turns, 2)
    for component in range(2):
        low = 4 + 2 * component
        halo = jnp.concatenate([halo_ref[low : low + 1, :], halo_ref[low + 1 : low + 2, :]], axis=1)
        fill_signal(design, component, panel, halo)
        sums = dot_nn(design[component], matrices[0, component, 0:TAPS, :]) + dot_nn(
            head_ref[component], matrices[0, component, TAPS : 2 * TAPS, :]
        )
        filtered[:, component * TAPS : (component + 1) * TAPS] = sums.astype(BF16)

    upper, lower = three_quadrants(filtered, panel)
    half = panel // 2
    upper = upper + before_ref[0 : half + 16, :]
    gram[0:half, :] = upper[0:half, :]
    gram[panel : panel + 16, :] = upper[half : half + 16, :]
    gram[half:panel, half:panel] = lower + before_ref[half + 16 : panel + 16, half:panel]
    gram[half:panel, 0:half] = jnp.transpose(upper[0:half, half:panel])

    eye = iota(square, 0) == iota(square, 1)
    rhs = [gram[panel : panel + 1, y * LANES : (y + 1) * LANES] * gram_scale for y in range(4)]
    diagonal = [
        jnp.sum(
            jnp.where(eye, gram[y * LANES : (y + 1) * LANES, y * LANES : (y + 1) * LANES], 0.0),
            axis=0,
            keepdims=True,
        )
        * row_scale
        for y in range(4)
    ]
    small = jnp.concatenate(rhs + diagonal, axis=0).astype(BF16)
    for y in range(4):
        for x in range(4):
            for core in range(2):
                peer = y * 8 + x * 2 + core
                for zh in range(4):
                    low = x * 128 + zh * 32 + core * 16
                    out_ref[peer, zh * 16 : zh * 16 + 16, :] = (
                        gram[low : low + 16, y * LANES : (y + 1) * LANES] * gram_scale
                    ).astype(BF16)
                out_ref[peer, 64:72, :] = small


def middle_kernel(in_ref, out_ref):
    total = in_ref[0].astype(F32)
    for peer in range(1, in_ref.shape[0]):
        total = total + in_ref[peer].astype(F32)
    rounded = total.astype(BF16)
    for zl in range(4):
        for zh in range(4):
            low = 3 * (zl * 4 + zh)
            for b in range(4):
                out_ref[low, :, b * 32 : b * 32 + 32] = rounded[
                    zh * 16 + 4 * b : zh * 16 + 4 * b + 4, zl * 32 : zl * 32 + 32
                ]
            out_ref[low + 1] = rounded[64:68, :]
            out_ref[low + 2] = rounded[68:72, :]


def last_kernel(in_ref, normal_ref, rhs_ref, diagonal_ref):
    totals = []
    for part in range(3):
        total = in_ref[part].astype(F32)
        for peer in range(1, in_ref.shape[0] // 3):
            total = total + in_ref[3 * peer + part].astype(F32)
        totals.append(total)
    for b in range(4):
        normal_ref[4 * b : 4 * b + 4, :] = totals[0][:, b * 32 : b * 32 + 32]
    rows, cols = normal_ref.shape
    row_low = (lax.axis_index("zh") * 8 + lax.axis_index("x") * 2 + lax.axis_index("core")) * rows
    col_low = (lax.axis_index("zl") * 4 + lax.axis_index("y")) * cols
    on_diagonal = row_low + iota((rows, cols), 0) == col_low + iota((rows, cols), 1)
    normal_ref[...] = jnp.where(on_diagonal, 0.0, normal_ref[...])
    for out_ref, total in ((rhs_ref, totals[1]), (diagonal_ref, totals[2])):
        for zl in range(4):
            for y in range(4):
                out_ref[0:1, zl * 128 + y * 32 : zl * 128 + y * 32 + 32] = total[
                    y : y + 1, zl * 32 : zl * 32 + 32
                ]


def load_kernel(*refs):
    count = (len(refs) - 3) // 2
    sources, packed_ref, rows_ref = refs[:count], refs[count], refs[count + 1]
    targets, sems = refs[count + 2 : -1], refs[-1]
    copies = [
        pltpu.make_async_copy(source, target, sems.at[index])
        for index, (source, target) in enumerate(zip(sources, targets))
    ]
    for copy in copies:
        copy.start()
    for copy in copies:
        copy.wait()
    colat_ref, lon_ref, obs_ref, start_ref = targets[:4]
    last = colat_ref.shape[0] - 2
    span = obs_ref.shape[1]
    packed_ref[0:2, :] = colat_ref[last : last + 2, :]
    packed_ref[2:4, :] = lon_ref[last : last + 2, :]
    for component in range(2):
        for half in range(2):
            low = span - (2 - half) * LANES
            row = 4 + 2 * component + half
            packed_ref[row : row + 1, :] = obs_ref[component : component + 1, low : low + LANES].astype(
                F32
            )
    packed_ref[8:10, :] = start_ref[last : last + 2, :].astype(F32)
    packed_ref[10:16, :] = jnp.ones((6, LANES), F32)
    rows = colat_ref.shape[0]
    degree = targets[4][0:1, :]
    order = targets[4][1:2, :]
    wave = jnp.abs(order) + jnp.where(order < 0, MULTIPLES, 0)
    for y in range(4):
        for zl in range(4):
            group = y * 4 + zl
            lanes = slice(zl * LANES + y * 32, zl * LANES + y * 32 + 32)
            rows_ref[group : group + 1, 0:32] = degree[:, lanes] * rows
            rows_ref[16 + group : 17 + group, 0:32] = wave[:, lanes] * rows


def on_device(colatitude, longitude, observed, filter_taps, segment_start, harmonic):
    rows_here = colatitude.shape[0]
    panel = harmonic.shape[1]
    blocks = rows_here // TAPS
    rows_total = rows_here * 512
    vmem = pl.BlockSpec(memory_space=pltpu.VMEM)
    hbm = pl.BlockSpec(memory_space=pltpu.HBM)

    def kernel(body, outs, scratch, mebibytes, operands, estimate=None):
        return pl.pallas_call(
            body,
            out_shape=outs,
            in_specs=[vmem] * len(operands),
            out_specs=jax.tree.map(lambda _: vmem, outs),
            scratch_shapes=scratch,
            cost_estimate=estimate,
            compiler_params=pltpu.CompilerParams(vmem_limit_bytes=mebibytes * 1024 * 1024),
        )(*operands)

    colat = colatitude.reshape(-1, LANES)
    lon = longitude.reshape(-1, LANES)
    start = segment_start.reshape(-1, LANES)
    arguments = (colat, lon, observed, start, harmonic, filter_taps)
    packed, table_rows, colat, lon, observed, start, harmonic, filter_taps = pl.pallas_call(
        load_kernel,
        name="load_and_pack",
        out_shape=(
            jax.ShapeDtypeStruct((16, LANES), F32),
            jax.ShapeDtypeStruct((32, LANES), jnp.int32),
            *(jax.ShapeDtypeStruct(value.shape, value.dtype) for value in arguments),
        ),
        in_specs=[hbm] * len(arguments),
        out_specs=(vmem,) * (len(arguments) + 2),
        scratch_shapes=[pltpu.SemaphoreType.DMA((len(arguments),))],
        compiler_params=pltpu.CompilerParams(vmem_limit_bytes=4 * 1024 * 1024),
    )(*(pltpu.with_memory_space_constraint(value, pltpu.HBM) for value in arguments))
    ring = ("zh", "x", "core")
    sub_rows = rows_here // LANES

    def products_on(core, *before):
        operands = (colat, lon, table_rows, packed, *before)
        outs = (
            jax.ShapeDtypeStruct((16, LANES), F32),
            jax.ShapeDtypeStruct((2, sub_rows // 4, panel * 4, LANES), F32),
        )
        return pl.pallas_call(
            functools.partial(products_kernel, core=core),
            out_shape=outs,
            in_specs=[vmem] * len(operands),
            out_specs=(vmem, vmem),
            scratch_shapes=[
                pltpu.VMEM((4, sub_rows, LANES), F32),
                pltpu.VMEM((2, MULTIPLES * sub_rows, LANES), F32),
                pltpu.VMEM((2 * MULTIPLES * sub_rows, LANES), F32),
                pltpu.VMEM((2, 2, 16, sub_rows, LANES), F32),
                pltpu.SMEM((32, LANES), jnp.int32),
                pltpu.SemaphoreType.DMA(()),
            ],
            input_output_aliases={4: 1} if before else {},
            cost_estimate=pl.CostEstimate(
                flops=40_000_000, bytes_accessed=8_000_000, transcendentals=0
            ),
            compiler_params=pltpu.CompilerParams(vmem_limit_bytes=16 * 1024 * 1024),
        )(*operands)

    packed_far, products = products_on(1)
    halo_far = lax.ppermute(packed_far, ring, [(i, i + 1) for i in range(1, 31, 2)])
    packed_near, products = products_on(0, products)
    halo_near = lax.ppermute(packed_near, ring, [(i, i + 1) for i in range(0, 31, 2)])
    before, head, columns, toeplitz = kernel(
        own_kernel,
        (
            jax.ShapeDtypeStruct((panel + 16, panel), F32),
            jax.ShapeDtypeStruct((2, panel + 16, TAPS), BF16),
            jax.ShapeDtypeStruct((3, panel, LANES), F32),
            jax.ShapeDtypeStruct((2, 3, LANES, LANES), F32),
        ),
        [
            pltpu.VMEM((2, panel + 16, rows_here), BF16),
            pltpu.VMEM((panel + 16, 2 * (rows_here - TAPS)), BF16),
            pltpu.VMEM((blocks - 1, 2, 2 * TAPS, TAPS), BF16),
            pltpu.VMEM((LANES, LANES), F32),
        ],
        24,
        (products, observed, start, harmonic, filter_taps),
        pl.CostEstimate(flops=4_000_000_000, bytes_accessed=4_000_000, transcendentals=0),
    )
    payload = kernel(
        functools.partial(
            edge_kernel, row_scale=1.0 / rows_total, gram_scale=1.0 / math.sqrt(rows_total)
        ),
        jax.ShapeDtypeStruct((32, 72, LANES), BF16),
        [
            pltpu.VMEM((2, panel + 16, TAPS), BF16),
            pltpu.VMEM((panel + 16, 2 * TAPS), BF16),
            pltpu.VMEM((1, 2, 2 * TAPS, TAPS), BF16),
            pltpu.VMEM((4, 8, LANES), F32),
            pltpu.VMEM((LANES, LANES), F32),
            pltpu.VMEM((panel + 16, panel), F32),
            pltpu.VMEM((16, LANES), F32),
        ],
        16,
        (halo_near, halo_far, start, before, head, columns, toeplitz),
    )
    arrived = lax.all_to_all(payload, ("y", "x", "core"), 0, 0)
    sums = kernel(middle_kernel, jax.ShapeDtypeStruct((48, 4, LANES), BF16), [], 8, (arrived,))
    gathered = lax.all_to_all(sums, ("zl", "zh"), 0, 0, tiled=True)
    normal, right_side, diagonal = kernel(
        last_kernel,
        (
            jax.ShapeDtypeStruct((16, 32), F32),
            jax.ShapeDtypeStruct((1, panel), F32),
            jax.ShapeDtypeStruct((1, panel), F32),
        ),
        [],
        8,
        (gathered,),
    )
    return normal, right_side.reshape(panel), diagonal.reshape(panel)


def solution(mesh):
    fine = Mesh(mesh.devices.reshape(4, 4, 4, 4, 2), ("zl", "y", "zh", "x", "core"))
    everywhere = ("zl", "y", "zh", "x", "core")
    return jax.shard_map(
        on_device,
        mesh=fine,
        in_specs=(P(everywhere), P(everywhere), P(None, everywhere), P(), P(everywhere), P()),
        out_specs=(P(("zh", "x", "core"), ("zl", "y")), P(), P()),
        check_vma=False,
    )
```

```python
import functools
import math

import jax
import jax.numpy as jnp
from jax import lax
from jax.experimental import pallas as pl
from jax.experimental.pallas import tpu as pltpu
from jax.sharding import Mesh, PartitionSpec as P


F32 = jnp.float32
BF16 = jnp.bfloat16
LANES = 128
TAPS = 256
MULTIPLES = 288
SIN_COEFFS = (3.141592639, -5.167709953, 2.550074404, -0.5982681334, 0.07760505745)
COS_COEFFS = (0.9999999504, -4.934792377, 4.058400535, -1.331796279, 0.2195071918)
TWO_PI_PARTS = (6.28125, 0.0019340515136718750, 1.2556659146854654e-06)
HALF_UP = 1.5 * 2.0**23


def horner(coeffs, z):
    total = z * coeffs[-1] + coeffs[-2]
    for coeff in coeffs[-3::-1]:
        total = total * z + coeff
    return total


def nearest(value):
    return (value + HALF_UP) - HALF_UP


def turns_of(angle):
    coarse = nearest(angle * (65536.0 / (2.0 * math.pi))) * (1.0 / 65536.0)
    rest = angle
    for part in TWO_PI_PARTS:
        rest = rest - coarse * part
    return coarse, rest * (1.0 / (2.0 * math.pi))


def dot_nt(a, b):
    return lax.dot_general(a, b, (((1,), (1,)), ((), ())), preferred_element_type=F32)


def dot_nn(a, b):
    return lax.dot_general(a, b, (((1,), (0,)), ((), ())), preferred_element_type=F32)


def iota(shape, axis):
    return lax.broadcasted_iota(jnp.int32, shape, axis)


def spread_turns(turns, angle, slot, low):
    coarse, fine = turns_of(angle)
    turns[2 * slot, low : low + angle.shape[0], :] = coarse
    turns[2 * slot + 1, low : low + angle.shape[0], :] = fine


def fill_design(design, columns, turns, chunks):
    def some_columns(step, carry):
        low = pl.multiple_of(step * 32, 32)
        degree = columns[0, pl.ds(low, 32), :]
        order = columns[1, pl.ds(low, 32), :]
        phase = columns[2, pl.ds(low, 32), :]
        for chunk in range(chunks):
            row = slice(chunk, chunk + 1)
            lane = slice(chunk * LANES, (chunk + 1) * LANES)
            polar = degree * turns[0, row, :]
            polar = (polar - nearest(polar)) + degree * turns[1, row, :]
            z = polar * polar
            half_sin = polar * horner(SIN_COEFFS, z)
            half_cos = horner(COS_COEFFS, z)
            twice = half_sin + half_sin
            cos_polar = 1.0 - twice * half_sin
            sin_polar = twice * half_cos
            azimuth = order * turns[2, row, :] - phase
            azimuth = (azimuth - nearest(azimuth)) + order * turns[3, row, :]
            half = azimuth * horner(SIN_COEFFS, azimuth * azimuth)
            wave = 1.0 - (half + half) * half
            design[0, pl.ds(low, 32), lane] = (cos_polar * wave).astype(BF16)
            design[1, pl.ds(low, 32), lane] = (sin_polar * wave).astype(BF16)
        return carry

    lax.fori_loop(0, columns.shape[1] // 32, some_columns, 0)


def sine_and_cosine(turns, slot, factor):
    part = turns[2 * slot] * factor
    part = (part - nearest(part)) + turns[2 * slot + 1] * factor
    z = part * part
    half_sin = part * horner(SIN_COEFFS, z)
    twice = half_sin + half_sin
    return twice * horner(COS_COEFFS, z), 1.0 - twice * half_sin


def fill_tables(tables, turns, small):
    rows = turns.shape[1]
    for slot in range(2):
        for b in range(16):
            sine, cosine = sine_and_cosine(turns, slot, float(b))
            small[slot, 0, b] = cosine
            small[slot, 1, b] = sine

    def some_multiples(a, carry):
        for slot, table in enumerate(tables):
            sine, cosine = sine_and_cosine(turns, slot, (16 * a).astype(F32))
            for b in range(16):
                place = pl.ds(pl.multiple_of(a * (16 * rows), 16 * rows) + b * rows, rows)
                table[0, place, :] = cosine * small[slot, 0, b] - sine * small[slot, 1, b]
                table[1, place, :] = sine * small[slot, 0, b] + cosine * small[slot, 1, b]
        return carry

    lax.fori_loop(0, MULTIPLES // 16, some_multiples, 0)


def fill_products(products, rows_of, tables):
    polar, azimuth = tables
    rows = 4 * products.shape[1]
    upper = iota((8, LANES), 0) >= 4

    def some_columns(group, carry):
        start = pl.multiple_of(group * 128, 128)
        for pair in range(16):
            values = []
            for offset in (2 * pair, 2 * pair + 1):
                degree = pl.multiple_of(rows_of[group, offset], rows)
                order = pl.multiple_of(rows_of[16 + group, offset], rows)
                wave = azimuth[pl.ds(order, rows), :]
                values.append([polar[c, pl.ds(degree, rows), :] * wave for c in range(2)])
            place = pl.ds(start + pair * 8, 8)
            for component in range(2):
                for half in range(rows // 8):
                    one = values[0][component][8 * half : 8 * half + 8, :]
                    two = values[1][component][8 * half : 8 * half + 8, :]
                    products[component, 2 * half, place, :] = jnp.where(upper, pltpu.roll(two, 4, 0), one)
                    products[component, 2 * half + 1, place, :] = jnp.where(
                        upper, two, pltpu.roll(one, 4, 0)
                    )
        return carry

    lax.fori_loop(0, 16, some_columns, 0)


def fill_signal(design, component, panel, values):
    span = values.shape[1]
    design[component, panel : panel + 16, 0:span] = jnp.where(
        iota((16, span), 0) == 0, values, 0.0
    ).astype(BF16)


def labels_of(flags):
    square = (LANES, LANES)
    low_tri = (iota(square, 0) >= iota(square, 1)).astype(BF16)
    up_tri = (iota(square, 0) <= iota(square, 1)).astype(BF16)
    low_strict = (iota(square, 0) > iota(square, 1)).astype(BF16)
    up_strict = (iota(square, 0) < iota(square, 1)).astype(BF16)
    ones = jnp.ones(square, BF16)
    by_lane = dot_nn(flags, up_tri) + dot_nn(dot_nn(low_strict, flags).astype(BF16), ones)
    by_sublane = dot_nt(low_tri, flags) + dot_nn(dot_nt(ones, flags).astype(BF16), up_strict)
    return by_lane, by_sublane


def filter_matrices(first_row, by_lane, by_sublane, toeplitz):
    square = (LANES, LANES)
    parts = ([], [])
    for sb in range(4):
        left = jnp.broadcast_to(by_sublane[:, first_row + sb : first_row + sb + 1], square)
        across = ([], [])
        for tb in range(2):
            d = tb - sb + 2
            same = None
            if 0 <= d <= 2:
                same = left == by_lane[first_row + 2 + tb : first_row + 3 + tb, :]
            for component in range(2):
                kept = jnp.zeros(square, F32)
                if same is not None:
                    kept = jnp.where(same, toeplitz(component, d), 0.0)
                across[component].append(kept.astype(BF16))
        for component in range(2):
            parts[component].append(jnp.concatenate(across[component], axis=1))
    return [jnp.concatenate(part, axis=0) for part in parts]


def products_kernel(
    *refs,
    core,
):
    colat_ref, lon_ref, scalar_ref = refs[:3]
    packed_ref = refs[3]
    packed_out, products, turns, polar, azimuth, small, scalars, scalars_sem = refs[-8:]
    packed_out[...] = packed_ref[...]

    @pl.when(lax.axis_index("core") == core)
    def _():
        scalars_copy = pltpu.make_async_copy(scalar_ref, scalars, scalars_sem)
        scalars_copy.start()
        rows, _ = colat_ref.shape
        spread_turns(turns, colat_ref[...], 0, 0)
        spread_turns(turns, lon_ref[...], 1, 0)
        fill_tables((polar, azimuth.reshape(2, MULTIPLES * rows, LANES)), turns, small)
        scalars_copy.wait()
        fill_products(products, scalars, (polar, azimuth))


def three_quadrants(filtered, panel):
    half = panel // 2
    upper = jnp.concatenate([filtered[0:half, :], filtered[panel : panel + 16, :]], axis=0)
    lower = filtered[half:panel, :]
    return dot_nt(upper, filtered[0:panel, :]), dot_nt(lower, lower)


def own_kernel(
    products,
    obs_ref,
    start_ref,
    harmonic_ref,
    taps_ref,
    gram_ref,
    head_ref,
    columns_ref,
    toeplitz_ref,
    design,
    filtered,
    starts,
):
    rows, _ = start_ref.shape
    panel = harmonic_ref.shape[1]
    blocks = rows // 2

    wide = harmonic_ref[...].astype(F32)
    tall = jnp.transpose(jnp.concatenate([wide, jnp.zeros((6, panel), F32)], axis=0))
    for zl in range(4):
        for y in range(4):
            part = tall[zl * 128 + y * 32 : zl * 128 + y * 32 + 32, :]
            low = y * 128 + zl * 32
            degree = jnp.broadcast_to(part[:, 0:1], (32, LANES))
            order = jnp.broadcast_to(part[:, 1:2], (32, LANES))
            columns_ref[0, low : low + 32, :] = degree
            columns_ref[1, low : low + 32, :] = jnp.abs(order)
            columns_ref[2, low : low + 32, :] = jnp.where(order < 0.0, 0.25, 0.0)

    starts[...] = jnp.zeros_like(starts)
    starts[0:rows, :] = start_ref[...].astype(F32)
    by_lane, by_sublane = labels_of(starts[...].astype(BF16))

    for component in range(2):
        padded = jnp.concatenate(
            [taps_ref[component : component + 1, :].astype(F32), jnp.zeros((1, TAPS), F32)], axis=1
        )
        spread = jnp.broadcast_to(padded, (LANES, 2 * TAPS))
        rolled = pltpu.roll(spread, 0, 1, stride=1, stride_axis=0)
        for d in range(3):
            toeplitz_ref[component, d] = rolled[:, d * LANES : (d + 1) * LANES]
    for component in range(2):
        fill_signal(design, component, panel, obs_ref[component : component + 1, :].astype(F32))

    def to_lanes(block):
        for component in range(2):
            for row in (2 * block, 2 * block + 1):
                for low in range(0, panel, 16):
                    tile = products[component, row // 4, pl.ds(low * 4 + row % 4, 16, stride=4), :]
                    design[component, low : low + 16, row * LANES : (row + 1) * LANES] = tile.astype(BF16)

    to_lanes(0)
    for component in range(2):
        head_ref[component] = design[component, :, 0:TAPS]
    for block in range(blocks - 1):
        to_lanes(block + 1)
        filters = filter_matrices(2 * block, by_lane, by_sublane, lambda c, d: toeplitz_ref[c, d])
        for component in range(2):
            window = design[component, :, block * TAPS : block * TAPS + 2 * TAPS]
            low = (component * (blocks - 1) + block) * TAPS
            filtered[:, low : low + TAPS] = dot_nn(window, filters[component]).astype(BF16)
    upper, lower = three_quadrants(filtered, panel)
    half = panel // 2
    gram_ref[0 : half + 16, :] = upper
    gram_ref[half + 16 : panel + 16, half:panel] = lower


def edge_kernel(
    near_ref,
    far_ref,
    start_ref,
    before_ref,
    head_ref,
    columns_ref,
    toeplitz_ref,
    out_ref,
    design,
    filtered,
    turns,
    starts,
    gram,
    halo_ref,
    *,
    row_scale,
    gram_scale,
):
    panel = columns_ref.shape[1]
    halo_ref[...] = near_ref[...] + far_ref[...]
    spread_turns(turns, halo_ref[0:2, :], 0, 0)
    spread_turns(turns, halo_ref[2:4, :], 1, 0)

    square = (LANES, LANES)
    starts[...] = jnp.zeros_like(starts)
    starts[0:2, :] = halo_ref[8:10, :]
    starts[2:4, :] = start_ref[0:2, :].astype(F32)
    by_lane, by_sublane = labels_of(starts[...].astype(BF16))
    lonely = 1.0 - halo_ref[10:11, :]
    by_lane = by_lane + jnp.where(iota(square, 0) >= 2, lonely, 0.0)
    by_sublane = by_sublane + jnp.where(iota(square, 1) >= 2, lonely, 0.0)
    filters = filter_matrices(0, by_lane, by_sublane, lambda c, d: toeplitz_ref[c, d])

    fill_design(design, columns_ref, turns, 2)
    for component in range(2):
        low = 4 + 2 * component
        halo = jnp.concatenate([halo_ref[low : low + 1, :], halo_ref[low + 1 : low + 2, :]], axis=1)
        fill_signal(design, component, panel, halo)
        sums = dot_nn(design[component], filters[component][0:TAPS, :]) + dot_nn(
            head_ref[component], filters[component][TAPS : 2 * TAPS, :]
        )
        filtered[:, component * TAPS : (component + 1) * TAPS] = sums.astype(BF16)

    upper, lower = three_quadrants(filtered, panel)
    half = panel // 2
    upper = upper + before_ref[0 : half + 16, :]
    gram[0:half, :] = upper[0:half, :]
    gram[panel : panel + 16, :] = upper[half : half + 16, :]
    gram[half:panel, half:panel] = lower + before_ref[half + 16 : panel + 16, half:panel]
    gram[half:panel, 0:half] = jnp.transpose(upper[0:half, half:panel])

    eye = iota(square, 0) == iota(square, 1)
    rhs = [gram[panel : panel + 1, y * LANES : (y + 1) * LANES] * gram_scale for y in range(4)]
    diagonal = [
        jnp.sum(
            jnp.where(eye, gram[y * LANES : (y + 1) * LANES, y * LANES : (y + 1) * LANES], 0.0),
            axis=0,
            keepdims=True,
        )
        * row_scale
        for y in range(4)
    ]
    small = jnp.concatenate(rhs + diagonal, axis=0).astype(BF16)
    for y in range(4):
        for x in range(4):
            for core in range(2):
                peer = y * 8 + x * 2 + core
                for zh in range(4):
                    low = x * 128 + zh * 32 + core * 16
                    out_ref[peer, zh * 16 : zh * 16 + 16, :] = (
                        gram[low : low + 16, y * LANES : (y + 1) * LANES] * gram_scale
                    ).astype(BF16)
                out_ref[peer, 64:72, :] = small


def middle_kernel(in_ref, out_ref):
    total = in_ref[0].astype(F32)
    for peer in range(1, in_ref.shape[0]):
        total = total + in_ref[peer].astype(F32)
    rounded = total.astype(BF16)
    for zl in range(4):
        for zh in range(4):
            low = 3 * (zl * 4 + zh)
            for b in range(4):
                out_ref[low, :, b * 32 : b * 32 + 32] = rounded[
                    zh * 16 + 4 * b : zh * 16 + 4 * b + 4, zl * 32 : zl * 32 + 32
                ]
            out_ref[low + 1] = rounded[64:68, :]
            out_ref[low + 2] = rounded[68:72, :]


def last_kernel(in_ref, normal_ref, rhs_ref, diagonal_ref):
    totals = []
    for part in range(3):
        total = in_ref[part].astype(F32)
        for peer in range(1, in_ref.shape[0] // 3):
            total = total + in_ref[3 * peer + part].astype(F32)
        totals.append(total)
    for b in range(4):
        normal_ref[4 * b : 4 * b + 4, :] = totals[0][:, b * 32 : b * 32 + 32]
    rows, cols = normal_ref.shape
    row_low = (lax.axis_index("zh") * 8 + lax.axis_index("x") * 2 + lax.axis_index("core")) * rows
    col_low = (lax.axis_index("zl") * 4 + lax.axis_index("y")) * cols
    on_diagonal = row_low + iota((rows, cols), 0) == col_low + iota((rows, cols), 1)
    normal_ref[...] = jnp.where(on_diagonal, 0.0, normal_ref[...])
    for out_ref, total in ((rhs_ref, totals[1]), (diagonal_ref, totals[2])):
        for zl in range(4):
            for y in range(4):
                out_ref[0:1, zl * 128 + y * 32 : zl * 128 + y * 32 + 32] = total[
                    y : y + 1, zl * 32 : zl * 32 + 32
                ]


def load_kernel(*refs):
    count = (len(refs) - 3) // 2
    sources, packed_ref, rows_ref = refs[:count], refs[count], refs[count + 1]
    targets, sems = refs[count + 2 : -1], refs[-1]
    copies = [
        pltpu.make_async_copy(source, target, sems.at[index])
        for index, (source, target) in enumerate(zip(sources, targets))
    ]
    for copy in copies:
        copy.start()
    for copy in copies:
        copy.wait()
    colat_ref, lon_ref, obs_ref, start_ref = targets[:4]
    last = colat_ref.shape[0] - 2
    span = obs_ref.shape[1]
    packed_ref[0:2, :] = colat_ref[last : last + 2, :]
    packed_ref[2:4, :] = lon_ref[last : last + 2, :]
    for component in range(2):
        for half in range(2):
            low = span - (2 - half) * LANES
            row = 4 + 2 * component + half
            packed_ref[row : row + 1, :] = obs_ref[component : component + 1, low : low + LANES].astype(
                F32
            )
    packed_ref[8:10, :] = start_ref[last : last + 2, :].astype(F32)
    packed_ref[10:16, :] = jnp.ones((6, LANES), F32)
    rows = colat_ref.shape[0]
    degree = targets[4][0:1, :]
    order = targets[4][1:2, :]
    wave = jnp.abs(order) + jnp.where(order < 0, MULTIPLES, 0)
    for y in range(4):
        for zl in range(4):
            group = y * 4 + zl
            lanes = slice(zl * LANES + y * 32, zl * LANES + y * 32 + 32)
            rows_ref[group : group + 1, 0:32] = degree[:, lanes] * rows
            rows_ref[16 + group : 17 + group, 0:32] = wave[:, lanes] * rows


def on_device(colatitude, longitude, observed, filter_taps, segment_start, harmonic):
    rows_here = colatitude.shape[0]
    panel = harmonic.shape[1]
    rows_total = rows_here * 512
    vmem = pl.BlockSpec(memory_space=pltpu.VMEM)
    hbm = pl.BlockSpec(memory_space=pltpu.HBM)

    def kernel(body, outs, scratch, mebibytes, operands, estimate=None):
        return pl.pallas_call(
            body,
            out_shape=outs,
            in_specs=[vmem] * len(operands),
            out_specs=jax.tree.map(lambda _: vmem, outs),
            scratch_shapes=scratch,
            cost_estimate=estimate,
            compiler_params=pltpu.CompilerParams(vmem_limit_bytes=mebibytes * 1024 * 1024),
        )(*operands)

    colat = colatitude.reshape(-1, LANES)
    lon = longitude.reshape(-1, LANES)
    start = segment_start.reshape(-1, LANES)
    arguments = (colat, lon, observed, start, harmonic, filter_taps)
    packed, table_rows, colat, lon, observed, start, harmonic, filter_taps = pl.pallas_call(
        load_kernel,
        name="load_and_pack",
        out_shape=(
            jax.ShapeDtypeStruct((16, LANES), F32),
            jax.ShapeDtypeStruct((32, LANES), jnp.int32),
            *(jax.ShapeDtypeStruct(value.shape, value.dtype) for value in arguments),
        ),
        in_specs=[hbm] * len(arguments),
        out_specs=(vmem,) * (len(arguments) + 2),
        scratch_shapes=[pltpu.SemaphoreType.DMA((len(arguments),))],
        compiler_params=pltpu.CompilerParams(vmem_limit_bytes=4 * 1024 * 1024),
    )(*(pltpu.with_memory_space_constraint(value, pltpu.HBM) for value in arguments))
    ring = ("zh", "x", "core")
    sub_rows = rows_here // LANES

    def products_on(core, *before):
        operands = (colat, lon, table_rows, packed, *before)
        outs = (
            jax.ShapeDtypeStruct((16, LANES), F32),
            jax.ShapeDtypeStruct((2, sub_rows // 4, panel * 4, LANES), F32),
        )
        return pl.pallas_call(
            functools.partial(products_kernel, core=core),
            out_shape=outs,
            in_specs=[vmem] * len(operands),
            out_specs=(vmem, vmem),
            scratch_shapes=[
                pltpu.VMEM((4, sub_rows, LANES), F32),
                pltpu.VMEM((2, MULTIPLES * sub_rows, LANES), F32),
                pltpu.VMEM((2 * MULTIPLES * sub_rows, LANES), F32),
                pltpu.VMEM((2, 2, 16, sub_rows, LANES), F32),
                pltpu.SMEM((32, LANES), jnp.int32),
                pltpu.SemaphoreType.DMA(()),
            ],
            input_output_aliases={4: 1} if before else {},
            cost_estimate=pl.CostEstimate(
                flops=40_000_000, bytes_accessed=8_000_000, transcendentals=0
            ),
            compiler_params=pltpu.CompilerParams(vmem_limit_bytes=16 * 1024 * 1024),
        )(*operands)

    packed_far, products = products_on(1)
    halo_far = lax.ppermute(packed_far, ring, [(i, i + 1) for i in range(1, 31, 2)])
    packed_near, products = products_on(0, products)
    halo_near = lax.ppermute(packed_near, ring, [(i, i + 1) for i in range(0, 31, 2)])
    before, head, columns, toeplitz = kernel(
        own_kernel,
        (
            jax.ShapeDtypeStruct((panel + 16, panel), F32),
            jax.ShapeDtypeStruct((2, panel + 16, TAPS), BF16),
            jax.ShapeDtypeStruct((3, panel, LANES), F32),
            jax.ShapeDtypeStruct((2, 3, LANES, LANES), F32),
        ),
        [
            pltpu.VMEM((2, panel + 16, rows_here), BF16),
            pltpu.VMEM((panel + 16, 2 * (rows_here - TAPS)), BF16),
            pltpu.VMEM((LANES, LANES), F32),
        ],
        24,
        (products, observed, start, harmonic, filter_taps),
        pl.CostEstimate(flops=4_000_000_000, bytes_accessed=4_000_000, transcendentals=0),
    )
    payload = kernel(
        functools.partial(
            edge_kernel, row_scale=1.0 / rows_total, gram_scale=1.0 / math.sqrt(rows_total)
        ),
        jax.ShapeDtypeStruct((32, 72, LANES), BF16),
        [
            pltpu.VMEM((2, panel + 16, TAPS), BF16),
            pltpu.VMEM((panel + 16, 2 * TAPS), BF16),
            pltpu.VMEM((4, 8, LANES), F32),
            pltpu.VMEM((LANES, LANES), F32),
            pltpu.VMEM((panel + 16, panel), F32),
            pltpu.VMEM((16, LANES), F32),
        ],
        16,
        (halo_near, halo_far, start, before, head, columns, toeplitz),
    )
    arrived = lax.all_to_all(payload, ("y", "x", "core"), 0, 0)
    sums = kernel(middle_kernel, jax.ShapeDtypeStruct((48, 4, LANES), BF16), [], 8, (arrived,))
    gathered = lax.all_to_all(sums, ("zl", "zh"), 0, 0, tiled=True)
    normal, right_side, diagonal = kernel(
        last_kernel,
        (
            jax.ShapeDtypeStruct((16, 32), F32),
            jax.ShapeDtypeStruct((1, panel), F32),
            jax.ShapeDtypeStruct((1, panel), F32),
        ),
        [],
        8,
        (gathered,),
    )
    return normal, right_side.reshape(panel), diagonal.reshape(panel)


def solution(mesh):
    fine = Mesh(mesh.devices.reshape(4, 4, 4, 4, 2), ("zl", "y", "zh", "x", "core"))
    everywhere = ("zl", "y", "zh", "x", "core")
    return jax.shard_map(
        on_device,
        mesh=fine,
        in_specs=(P(everywhere), P(everywhere), P(None, everywhere), P(), P(everywhere), P()),
        out_specs=(P(("zh", "x", "core"), ("zl", "y")), P(), P()),
        check_vma=False,
    )
```

```python
import functools
import math

import jax
import jax.numpy as jnp
from jax import lax
from jax.experimental import pallas as pl
from jax.experimental.pallas import tpu as pltpu
from jax.sharding import Mesh, PartitionSpec as P


F32 = jnp.float32
BF16 = jnp.bfloat16
LANES = 128
TAPS = 256
MULTIPLES = 288
SIN_COEFFS = (3.141592639, -5.167709953, 2.550074404, -0.5982681334, 0.07760505745)
COS_COEFFS = (0.9999999504, -4.934792377, 4.058400535, -1.331796279, 0.2195071918)
TWO_PI_PARTS = (6.28125, 0.0019340515136718750, 1.2556659146854654e-06)
HALF_UP = 1.5 * 2.0**23


def horner(coeffs, z):
    total = z * coeffs[-1] + coeffs[-2]
    for coeff in coeffs[-3::-1]:
        total = total * z + coeff
    return total


def nearest(value):
    return (value + HALF_UP) - HALF_UP


def turns_of(angle):
    coarse = nearest(angle * (65536.0 / (2.0 * math.pi))) * (1.0 / 65536.0)
    rest = angle
    for part in TWO_PI_PARTS:
        rest = rest - coarse * part
    return coarse, rest * (1.0 / (2.0 * math.pi))


def dot_nt(a, b):
    return lax.dot_general(a, b, (((1,), (1,)), ((), ())), preferred_element_type=F32)


def dot_nn(a, b):
    return lax.dot_general(a, b, (((1,), (0,)), ((), ())), preferred_element_type=F32)


def iota(shape, axis):
    return lax.broadcasted_iota(jnp.int32, shape, axis)


def spread_turns(turns, angle, slot, low):
    coarse, fine = turns_of(angle)
    turns[2 * slot, low : low + angle.shape[0], :] = coarse
    turns[2 * slot + 1, low : low + angle.shape[0], :] = fine


def fill_design(design, columns, turns, chunks):
    def some_columns(step, carry):
        low = pl.multiple_of(step * 32, 32)
        degree = columns[0, pl.ds(low, 32), :]
        order = columns[1, pl.ds(low, 32), :]
        phase = columns[2, pl.ds(low, 32), :]
        for chunk in range(chunks):
            row = slice(chunk, chunk + 1)
            lane = slice(chunk * LANES, (chunk + 1) * LANES)
            polar = degree * turns[0, row, :]
            polar = (polar - nearest(polar)) + degree * turns[1, row, :]
            z = polar * polar
            half_sin = polar * horner(SIN_COEFFS, z)
            half_cos = horner(COS_COEFFS, z)
            twice = half_sin + half_sin
            cos_polar = 1.0 - twice * half_sin
            sin_polar = twice * half_cos
            azimuth = order * turns[2, row, :] - phase
            azimuth = (azimuth - nearest(azimuth)) + order * turns[3, row, :]
            half = azimuth * horner(SIN_COEFFS, azimuth * azimuth)
            wave = 1.0 - (half + half) * half
            design[0, pl.ds(low, 32), lane] = (cos_polar * wave).astype(BF16)
            design[1, pl.ds(low, 32), lane] = (sin_polar * wave).astype(BF16)
        return carry

    lax.fori_loop(0, columns.shape[1] // 32, some_columns, 0)


def sine_and_cosine(turns, slot, factor):
    part = turns[2 * slot] * factor
    part = (part - nearest(part)) + turns[2 * slot + 1] * factor
    z = part * part
    half_sin = part * horner(SIN_COEFFS, z)
    twice = half_sin + half_sin
    return twice * horner(COS_COEFFS, z), 1.0 - twice * half_sin


def fill_tables(tables, turns, small):
    rows = turns.shape[1]
    for slot in range(2):
        for b in range(16):
            sine, cosine = sine_and_cosine(turns, slot, float(b))
            small[slot, 0, b] = cosine
            small[slot, 1, b] = sine

    def some_multiples(step, carry):
        for a in range(3):
            first = 3 * step + a
            for slot, table in enumerate(tables):
                sine, cosine = sine_and_cosine(turns, slot, (16 * first).astype(F32))
                for b in range(16):
                    place = pl.ds(pl.multiple_of(first * (16 * rows), 16 * rows) + b * rows, rows)
                    table[0, place, :] = cosine * small[slot, 0, b] - sine * small[slot, 1, b]
                    table[1, place, :] = sine * small[slot, 0, b] + cosine * small[slot, 1, b]
        return carry

    lax.fori_loop(0, MULTIPLES // 48, some_multiples, 0)


def fill_products(products, rows_of, tables):
    polar, azimuth = tables
    rows = 4 * products.shape[1]
    upper = iota((8, LANES), 0) >= 4

    def some_columns(group, carry):
        start = pl.multiple_of(group * 128, 128)
        for pair in range(16):
            values = []
            for offset in (2 * pair, 2 * pair + 1):
                degree = pl.multiple_of(rows_of[group, offset], rows)
                order = pl.multiple_of(rows_of[16 + group, offset], rows)
                wave = azimuth[pl.ds(order, rows), :]
                values.append([polar[c, pl.ds(degree, rows), :] * wave for c in range(2)])
            place = pl.ds(start + pair * 8, 8)
            for component in range(2):
                for half in range(rows // 8):
                    one = values[0][component][8 * half : 8 * half + 8, :]
                    two = values[1][component][8 * half : 8 * half + 8, :]
                    products[component, 2 * half, place, :] = jnp.where(upper, pltpu.roll(two, 4, 0), one)
                    products[component, 2 * half + 1, place, :] = jnp.where(
                        upper, two, pltpu.roll(one, 4, 0)
                    )
        return carry

    lax.fori_loop(0, 16, some_columns, 0)


def fill_signal(design, component, panel, values):
    span = values.shape[1]
    design[component, panel : panel + 16, 0:span] = jnp.where(
        iota((16, span), 0) == 0, values, 0.0
    ).astype(BF16)


def labels_of(flags):
    square = (LANES, LANES)
    low_tri = (iota(square, 0) >= iota(square, 1)).astype(BF16)
    up_tri = (iota(square, 0) <= iota(square, 1)).astype(BF16)
    low_strict = (iota(square, 0) > iota(square, 1)).astype(BF16)
    up_strict = (iota(square, 0) < iota(square, 1)).astype(BF16)
    ones = jnp.ones(square, BF16)
    by_lane = dot_nn(flags, up_tri) + dot_nn(dot_nn(low_strict, flags).astype(BF16), ones)
    by_sublane = dot_nt(low_tri, flags) + dot_nn(dot_nt(ones, flags).astype(BF16), up_strict)
    return by_lane, by_sublane


def filter_matrices(first_row, by_lane, by_sublane, toeplitz):
    square = (LANES, LANES)
    parts = ([], [])
    for sb in range(4):
        left = jnp.broadcast_to(by_sublane[:, first_row + sb : first_row + sb + 1], square)
        across = ([], [])
        for tb in range(2):
            d = tb - sb + 2
            same = None
            if 0 <= d <= 2:
                same = left == by_lane[first_row + 2 + tb : first_row + 3 + tb, :]
            for component in range(2):
                kept = jnp.zeros(square, F32)
                if same is not None:
                    kept = jnp.where(same, toeplitz(component, d), 0.0)
                across[component].append(kept.astype(BF16))
        for component in range(2):
            parts[component].append(jnp.concatenate(across[component], axis=1))
    return [jnp.concatenate(part, axis=0) for part in parts]


def products_kernel(
    *refs,
    core,
):
    colat_ref, lon_ref, scalar_ref = refs[:3]
    packed_ref = refs[3]
    packed_out, products, turns, polar, azimuth, small, scalars, scalars_sem = refs[-8:]
    packed_out[...] = packed_ref[...]

    @pl.when(lax.axis_index("core") == core)
    def _():
        scalars_copy = pltpu.make_async_copy(scalar_ref, scalars, scalars_sem)
        scalars_copy.start()
        rows, _ = colat_ref.shape
        spread_turns(turns, colat_ref[...], 0, 0)
        spread_turns(turns, lon_ref[...], 1, 0)
        fill_tables((polar, azimuth.reshape(2, MULTIPLES * rows, LANES)), turns, small)
        scalars_copy.wait()
        fill_products(products, scalars, (polar, azimuth))


def three_quadrants(filtered, panel):
    half = panel // 2
    upper = jnp.concatenate([filtered[0:half, :], filtered[panel : panel + 16, :]], axis=0)
    lower = filtered[half:panel, :]
    return dot_nt(upper, filtered[0:panel, :]), dot_nt(lower, lower)


def own_kernel(
    products,
    obs_ref,
    start_ref,
    harmonic_ref,
    taps_ref,
    gram_ref,
    head_ref,
    columns_ref,
    toeplitz_ref,
    design,
    filtered,
    starts,
):
    rows, _ = start_ref.shape
    panel = harmonic_ref.shape[1]
    blocks = rows // 2

    wide = harmonic_ref[...].astype(F32)
    tall = jnp.transpose(jnp.concatenate([wide, jnp.zeros((6, panel), F32)], axis=0))
    for zl in range(4):
        for y in range(4):
            part = tall[zl * 128 + y * 32 : zl * 128 + y * 32 + 32, :]
            low = y * 128 + zl * 32
            degree = jnp.broadcast_to(part[:, 0:1], (32, LANES))
            order = jnp.broadcast_to(part[:, 1:2], (32, LANES))
            columns_ref[0, low : low + 32, :] = degree
            columns_ref[1, low : low + 32, :] = jnp.abs(order)
            columns_ref[2, low : low + 32, :] = jnp.where(order < 0.0, 0.25, 0.0)

    starts[...] = jnp.zeros_like(starts)
    starts[0:rows, :] = start_ref[...].astype(F32)
    by_lane, by_sublane = labels_of(starts[...].astype(BF16))

    for component in range(2):
        padded = jnp.concatenate(
            [taps_ref[component : component + 1, :].astype(F32), jnp.zeros((1, TAPS), F32)], axis=1
        )
        spread = jnp.broadcast_to(padded, (LANES, 2 * TAPS))
        rolled = pltpu.roll(spread, 0, 1, stride=1, stride_axis=0)
        for d in range(3):
            toeplitz_ref[component, d] = rolled[:, d * LANES : (d + 1) * LANES]
    for component in range(2):
        fill_signal(design, component, panel, obs_ref[component : component + 1, :].astype(F32))

    def to_lanes(block):
        for component in range(2):
            for row in (2 * block, 2 * block + 1):
                for low in range(0, panel, 16):
                    tile = products[component, row // 4, pl.ds(low * 4 + row % 4, 16, stride=4), :]
                    design[component, low : low + 16, row * LANES : (row + 1) * LANES] = tile.astype(BF16)

    to_lanes(0)
    for component in range(2):
        head_ref[component] = design[component, :, 0:TAPS]
    for block in range(blocks - 1):
        to_lanes(block + 1)
        filters = filter_matrices(2 * block, by_lane, by_sublane, lambda c, d: toeplitz_ref[c, d])
        for component in range(2):
            window = design[component, :, block * TAPS : block * TAPS + 2 * TAPS]
            low = (component * (blocks - 1) + block) * TAPS
            filtered[:, low : low + TAPS] = dot_nn(window, filters[component]).astype(BF16)
    upper, lower = three_quadrants(filtered, panel)
    half = panel // 2
    gram_ref[0 : half + 16, :] = upper
    gram_ref[half + 16 : panel + 16, half:panel] = lower


def edge_kernel(
    near_ref,
    far_ref,
    start_ref,
    before_ref,
    head_ref,
    columns_ref,
    toeplitz_ref,
    out_ref,
    design,
    filtered,
    turns,
    starts,
    gram,
    halo_ref,
):
    panel = columns_ref.shape[1]
    halo_ref[...] = near_ref[...] + far_ref[...]
    spread_turns(turns, halo_ref[0:2, :], 0, 0)
    spread_turns(turns, halo_ref[2:4, :], 1, 0)

    square = (LANES, LANES)
    starts[...] = jnp.zeros_like(starts)
    starts[0:2, :] = halo_ref[8:10, :]
    starts[2:4, :] = start_ref[0:2, :].astype(F32)
    by_lane, by_sublane = labels_of(starts[...].astype(BF16))
    lonely = 1.0 - halo_ref[10:11, :]
    by_lane = by_lane + jnp.where(iota(square, 0) >= 2, lonely, 0.0)
    by_sublane = by_sublane + jnp.where(iota(square, 1) >= 2, lonely, 0.0)
    filters = filter_matrices(0, by_lane, by_sublane, lambda c, d: toeplitz_ref[c, d])

    fill_design(design, columns_ref, turns, 2)
    for component in range(2):
        low = 4 + 2 * component
        halo = jnp.concatenate([halo_ref[low : low + 1, :], halo_ref[low + 1 : low + 2, :]], axis=1)
        fill_signal(design, component, panel, halo)
        sums = dot_nn(design[component], filters[component][0:TAPS, :]) + dot_nn(
            head_ref[component], filters[component][TAPS : 2 * TAPS, :]
        )
        filtered[:, component * TAPS : (component + 1) * TAPS] = sums.astype(BF16)

    upper, lower = three_quadrants(filtered, panel)
    half = panel // 2
    upper = upper + before_ref[0 : half + 16, :]
    gram[0:half, :] = upper[0:half, :]
    gram[panel : panel + 16, :] = upper[half : half + 16, :]
    gram[half:panel, half:panel] = lower + before_ref[half + 16 : panel + 16, half:panel]
    gram[half:panel, 0:half] = jnp.transpose(upper[0:half, half:panel])

    eye = iota(square, 0) == iota(square, 1)
    rhs = [gram[panel : panel + 1, y * LANES : (y + 1) * LANES] for y in range(4)]
    diagonal = [
        jnp.sum(
            jnp.where(eye, gram[y * LANES : (y + 1) * LANES, y * LANES : (y + 1) * LANES], 0.0),
            axis=0,
            keepdims=True,
        )
        for y in range(4)
    ]
    small = jnp.concatenate(rhs + diagonal, axis=0).astype(BF16)
    for y in range(4):
        for x in range(4):
            for core in range(2):
                peer = y * 8 + x * 2 + core
                for zh in range(4):
                    low = x * 128 + zh * 32 + core * 16
                    out_ref[peer, zh * 16 : zh * 16 + 16, :] = gram[
                        low : low + 16, y * LANES : (y + 1) * LANES
                    ].astype(BF16)
                out_ref[peer, 64:72, :] = small


def middle_kernel(in_ref, out_ref):
    total = in_ref[0].astype(F32)
    for peer in range(1, in_ref.shape[0]):
        total = total + in_ref[peer].astype(F32)
    rounded = total.astype(BF16)
    for zl in range(4):
        for zh in range(4):
            low = 3 * (zl * 4 + zh)
            for b in range(4):
                out_ref[low, :, b * 32 : b * 32 + 32] = rounded[
                    zh * 16 + 4 * b : zh * 16 + 4 * b + 4, zl * 32 : zl * 32 + 32
                ]
            out_ref[low + 1] = rounded[64:68, :]
            out_ref[low + 2] = rounded[68:72, :]


def last_kernel(in_ref, normal_ref, rhs_ref, diagonal_ref, *, row_scale, gram_scale):
    totals = []
    for part in range(3):
        total = in_ref[part].astype(F32)
        for peer in range(1, in_ref.shape[0] // 3):
            total = total + in_ref[3 * peer + part].astype(F32)
        totals.append(total * (gram_scale, gram_scale, row_scale)[part])
    for b in range(4):
        normal_ref[4 * b : 4 * b + 4, :] = totals[0][:, b * 32 : b * 32 + 32]
    rows, cols = normal_ref.shape
    row_low = (lax.axis_index("zh") * 8 + lax.axis_index("x") * 2 + lax.axis_index("core")) * rows
    col_low = (lax.axis_index("zl") * 4 + lax.axis_index("y")) * cols
    on_diagonal = row_low + iota((rows, cols), 0) == col_low + iota((rows, cols), 1)
    normal_ref[...] = jnp.where(on_diagonal, 0.0, normal_ref[...])
    for out_ref, total in ((rhs_ref, totals[1]), (diagonal_ref, totals[2])):
        for zl in range(4):
            for y in range(4):
                out_ref[0:1, zl * 128 + y * 32 : zl * 128 + y * 32 + 32] = total[
                    y : y + 1, zl * 32 : zl * 32 + 32
                ]


def load_kernel(*refs):
    count = (len(refs) - 3) // 2
    sources, packed_ref, rows_ref = refs[:count], refs[count], refs[count + 1]
    targets, sems = refs[count + 2 : -1], refs[-1]
    copies = [
        pltpu.make_async_copy(source, target, sems.at[index])
        for index, (source, target) in enumerate(zip(sources, targets))
    ]
    for copy in copies:
        copy.start()
    for copy in copies:
        copy.wait()
    colat_ref, lon_ref, obs_ref, start_ref = targets[:4]
    last = colat_ref.shape[0] - 2
    span = obs_ref.shape[1]
    packed_ref[0:2, :] = colat_ref[last : last + 2, :]
    packed_ref[2:4, :] = lon_ref[last : last + 2, :]
    for component in range(2):
        for half in range(2):
            low = span - (2 - half) * LANES
            row = 4 + 2 * component + half
            packed_ref[row : row + 1, :] = obs_ref[component : component + 1, low : low + LANES].astype(
                F32
            )
    packed_ref[8:10, :] = start_ref[last : last + 2, :].astype(F32)
    packed_ref[10:16, :] = jnp.ones((6, LANES), F32)
    rows = colat_ref.shape[0]
    degree = targets[4][0:1, :]
    order = targets[4][1:2, :]
    wave = jnp.abs(order) + jnp.where(order < 0, MULTIPLES, 0)
    for y in range(4):
        for zl in range(4):
            group = y * 4 + zl
            lanes = slice(zl * LANES + y * 32, zl * LANES + y * 32 + 32)
            rows_ref[group : group + 1, 0:32] = degree[:, lanes] * rows
            rows_ref[16 + group : 17 + group, 0:32] = wave[:, lanes] * rows


def on_device(colatitude, longitude, observed, filter_taps, segment_start, harmonic):
    rows_here = colatitude.shape[0]
    panel = harmonic.shape[1]
    rows_total = rows_here * 512
    vmem = pl.BlockSpec(memory_space=pltpu.VMEM)
    hbm = pl.BlockSpec(memory_space=pltpu.HBM)

    def kernel(body, outs, scratch, mebibytes, operands, estimate=None):
        return pl.pallas_call(
            body,
            out_shape=outs,
            in_specs=[vmem] * len(operands),
            out_specs=jax.tree.map(lambda _: vmem, outs),
            scratch_shapes=scratch,
            cost_estimate=estimate,
            compiler_params=pltpu.CompilerParams(vmem_limit_bytes=mebibytes * 1024 * 1024),
        )(*operands)

    colat = colatitude.reshape(-1, LANES)
    lon = longitude.reshape(-1, LANES)
    start = segment_start.reshape(-1, LANES)
    arguments = (colat, lon, observed, start, harmonic, filter_taps)
    packed, table_rows, colat, lon, observed, start, harmonic, filter_taps = pl.pallas_call(
        load_kernel,
        name="load_and_pack",
        out_shape=(
            jax.ShapeDtypeStruct((16, LANES), F32),
            jax.ShapeDtypeStruct((32, LANES), jnp.int32),
            *(jax.ShapeDtypeStruct(value.shape, value.dtype) for value in arguments),
        ),
        in_specs=[hbm] * len(arguments),
        out_specs=(vmem,) * (len(arguments) + 2),
        scratch_shapes=[pltpu.SemaphoreType.DMA((len(arguments),))],
        compiler_params=pltpu.CompilerParams(vmem_limit_bytes=4 * 1024 * 1024),
    )(*(pltpu.with_memory_space_constraint(value, pltpu.HBM) for value in arguments))
    ring = ("zh", "x", "core")
    sub_rows = rows_here // LANES

    def products_on(core, *before):
        operands = (colat, lon, table_rows, packed, *before)
        outs = (
            jax.ShapeDtypeStruct((16, LANES), F32),
            jax.ShapeDtypeStruct((2, sub_rows // 4, panel * 4, LANES), F32),
        )
        return pl.pallas_call(
            functools.partial(products_kernel, core=core),
            out_shape=outs,
            in_specs=[vmem] * len(operands),
            out_specs=(vmem, vmem),
            scratch_shapes=[
                pltpu.VMEM((4, sub_rows, LANES), F32),
                pltpu.VMEM((2, MULTIPLES * sub_rows, LANES), F32),
                pltpu.VMEM((2 * MULTIPLES * sub_rows, LANES), F32),
                pltpu.VMEM((2, 2, 16, sub_rows, LANES), F32),
                pltpu.SMEM((32, LANES), jnp.int32),
                pltpu.SemaphoreType.DMA(()),
            ],
            input_output_aliases={4: 1} if before else {},
            cost_estimate=pl.CostEstimate(
                flops=40_000_000, bytes_accessed=8_000_000, transcendentals=0
            ),
            compiler_params=pltpu.CompilerParams(vmem_limit_bytes=16 * 1024 * 1024),
        )(*operands)

    packed_far, products = products_on(1)
    halo_far = lax.ppermute(packed_far, ring, [(i, i + 1) for i in range(1, 31, 2)])
    packed_near, products = products_on(0, products)
    halo_near = lax.ppermute(packed_near, ring, [(i, i + 1) for i in range(0, 31, 2)])
    before, head, columns, toeplitz = kernel(
        own_kernel,
        (
            jax.ShapeDtypeStruct((panel + 16, panel), F32),
            jax.ShapeDtypeStruct((2, panel + 16, TAPS), BF16),
            jax.ShapeDtypeStruct((3, panel, LANES), F32),
            jax.ShapeDtypeStruct((2, 3, LANES, LANES), F32),
        ),
        [
            pltpu.VMEM((2, panel + 16, rows_here), BF16),
            pltpu.VMEM((panel + 16, 2 * (rows_here - TAPS)), BF16),
            pltpu.VMEM((LANES, LANES), F32),
        ],
        24,
        (products, observed, start, harmonic, filter_taps),
        pl.CostEstimate(flops=4_000_000_000, bytes_accessed=4_000_000, transcendentals=0),
    )
    payload = kernel(
        edge_kernel,
        jax.ShapeDtypeStruct((32, 72, LANES), BF16),
        [
            pltpu.VMEM((2, panel + 16, TAPS), BF16),
            pltpu.VMEM((panel + 16, 2 * TAPS), BF16),
            pltpu.VMEM((4, 8, LANES), F32),
            pltpu.VMEM((LANES, LANES), F32),
            pltpu.VMEM((panel + 16, panel), F32),
            pltpu.VMEM((16, LANES), F32),
        ],
        16,
        (halo_near, halo_far, start, before, head, columns, toeplitz),
    )
    arrived = lax.all_to_all(payload, ("y", "x", "core"), 0, 0)
    sums = kernel(middle_kernel, jax.ShapeDtypeStruct((48, 4, LANES), BF16), [], 8, (arrived,))
    gathered = lax.all_to_all(sums, ("zl", "zh"), 0, 0, tiled=True)
    normal, right_side, diagonal = kernel(
        functools.partial(
            last_kernel, row_scale=1.0 / rows_total, gram_scale=1.0 / math.sqrt(rows_total)
        ),
        (
            jax.ShapeDtypeStruct((16, 32), F32),
            jax.ShapeDtypeStruct((1, panel), F32),
            jax.ShapeDtypeStruct((1, panel), F32),
        ),
        [],
        8,
        (gathered,),
    )
    return normal, right_side.reshape(panel), diagonal.reshape(panel)


def solution(mesh):
    fine = Mesh(mesh.devices.reshape(4, 4, 4, 4, 2), ("zl", "y", "zh", "x", "core"))
    everywhere = ("zl", "y", "zh", "x", "core")
    return jax.shard_map(
        on_device,
        mesh=fine,
        in_specs=(P(everywhere), P(everywhere), P(None, everywhere), P(), P(everywhere), P()),
        out_specs=(P(("zh", "x", "core"), ("zl", "y")), P(), P()),
        check_vma=False,
    )
```

```python
import functools
import math

import jax
import jax.numpy as jnp
from jax import lax
from jax.experimental import pallas as pl
from jax.experimental.pallas import tpu as pltpu
from jax.sharding import Mesh, PartitionSpec as P


F32 = jnp.float32
BF16 = jnp.bfloat16
LANES = 128
TAPS = 256
MULTIPLES = 288
SIN_COEFFS = (3.141592639, -5.167709953, 2.550074404, -0.5982681334, 0.07760505745)
COS_COEFFS = (0.9999999504, -4.934792377, 4.058400535, -1.331796279, 0.2195071918)
TWO_PI_PARTS = (6.28125, 0.0019340515136718750, 1.2556659146854654e-06)
HALF_UP = 1.5 * 2.0**23


def horner(coeffs, z):
    total = z * coeffs[-1] + coeffs[-2]
    for coeff in coeffs[-3::-1]:
        total = total * z + coeff
    return total


def nearest(value):
    return (value + HALF_UP) - HALF_UP


def turns_of(angle):
    coarse = nearest(angle * (65536.0 / (2.0 * math.pi))) * (1.0 / 65536.0)
    rest = angle
    for part in TWO_PI_PARTS:
        rest = rest - coarse * part
    return coarse, rest * (1.0 / (2.0 * math.pi))


def dot_nt(a, b):
    return lax.dot_general(a, b, (((1,), (1,)), ((), ())), preferred_element_type=F32)


def dot_nn(a, b):
    return lax.dot_general(a, b, (((1,), (0,)), ((), ())), preferred_element_type=F32)


def iota(shape, axis):
    return lax.broadcasted_iota(jnp.int32, shape, axis)


def spread_turns(turns, angle, slot, low):
    coarse, fine = turns_of(angle)
    turns[2 * slot, low : low + angle.shape[0], :] = coarse
    turns[2 * slot + 1, low : low + angle.shape[0], :] = fine


def fill_design(design, columns, turns, chunks):
    def some_columns(step, carry):
        low = pl.multiple_of(step * 32, 32)
        degree = columns[0, pl.ds(low, 32), :]
        order = columns[1, pl.ds(low, 32), :]
        phase = columns[2, pl.ds(low, 32), :]
        for chunk in range(chunks):
            row = slice(chunk, chunk + 1)
            lane = slice(chunk * LANES, (chunk + 1) * LANES)
            polar = degree * turns[0, row, :]
            polar = (polar - nearest(polar)) + degree * turns[1, row, :]
            z = polar * polar
            half_sin = polar * horner(SIN_COEFFS, z)
            half_cos = horner(COS_COEFFS, z)
            twice = half_sin + half_sin
            cos_polar = 1.0 - twice * half_sin
            sin_polar = twice * half_cos
            azimuth = order * turns[2, row, :] - phase
            azimuth = (azimuth - nearest(azimuth)) + order * turns[3, row, :]
            half = azimuth * horner(SIN_COEFFS, azimuth * azimuth)
            wave = 1.0 - (half + half) * half
            design[0, pl.ds(low, 32), lane] = (cos_polar * wave).astype(BF16)
            design[1, pl.ds(low, 32), lane] = (sin_polar * wave).astype(BF16)
        return carry

    lax.fori_loop(0, columns.shape[1] // 32, some_columns, 0)


def sine_and_cosine(turns, slot, factor):
    part = turns[2 * slot] * factor
    part = (part - nearest(part)) + turns[2 * slot + 1] * factor
    z = part * part
    half_sin = part * horner(SIN_COEFFS, z)
    twice = half_sin + half_sin
    return twice * horner(COS_COEFFS, z), 1.0 - twice * half_sin


def fill_tables(tables, turns, small):
    rows = turns.shape[1]

    def added(one, two):
        return one[0] * two[1] + one[1] * two[0], one[1] * two[1] - one[0] * two[0]

    for slot in range(2):
        few = {b: sine_and_cosine(turns, slot, float(b)) for b in (0, 1, 2, 3, 4, 8, 12, 16, 32)}
        for b in range(16):
            sine, cosine = few[b] if b in few else added(few[b // 4 * 4], few[b % 4])
            small[slot, 0, b] = cosine
            small[slot, 1, b] = sine
        for index, b in ((16, 16), (17, 32)):
            small[slot, 0, index] = few[b][1]
            small[slot, 1, index] = few[b][0]

    def some_multiples(step, carry):
        for slot, table in enumerate(tables):
            first = sine_and_cosine(turns, slot, (48 * step).astype(F32))
            for a in range(3):
                sine, cosine = first
                if a:
                    sine, cosine = added(first, (small[slot, 1, 15 + a], small[slot, 0, 15 + a]))
                for b in range(16):
                    place = pl.ds(pl.multiple_of(step * (48 * rows), 48 * rows) + (16 * a + b) * rows, rows)
                    table[0, place, :] = cosine * small[slot, 0, b] - sine * small[slot, 1, b]
                    table[1, place, :] = sine * small[slot, 0, b] + cosine * small[slot, 1, b]
        return carry

    lax.fori_loop(0, MULTIPLES // 48, some_multiples, 0)


def fill_products(products, rows_of, tables):
    polar, azimuth = tables
    rows = 4 * products.shape[1]
    upper = iota((8, LANES), 0) >= 4

    def some_columns(group, carry):
        start = pl.multiple_of(group * 128, 128)
        for pair in range(16):
            values = []
            for offset in (2 * pair, 2 * pair + 1):
                degree = pl.multiple_of(rows_of[group, offset], rows)
                order = pl.multiple_of(rows_of[16 + group, offset], rows)
                wave = azimuth[pl.ds(order, rows), :]
                values.append([polar[c, pl.ds(degree, rows), :] * wave for c in range(2)])
            place = pl.ds(start + pair * 8, 8)
            for component in range(2):
                for half in range(rows // 8):
                    one = values[0][component][8 * half : 8 * half + 8, :]
                    two = values[1][component][8 * half : 8 * half + 8, :]
                    products[component, 2 * half, place, :] = jnp.where(upper, pltpu.roll(two, 4, 0), one)
                    products[component, 2 * half + 1, place, :] = jnp.where(
                        upper, two, pltpu.roll(one, 4, 0)
                    )
        return carry

    lax.fori_loop(0, 16, some_columns, 0)


def fill_signal(design, component, panel, values):
    span = values.shape[1]
    design[component, panel : panel + 16, 0:span] = jnp.where(
        iota((16, span), 0) == 0, values, 0.0
    ).astype(BF16)


def labels_of(flags):
    square = (LANES, LANES)
    low_tri = (iota(square, 0) >= iota(square, 1)).astype(BF16)
    up_tri = (iota(square, 0) <= iota(square, 1)).astype(BF16)
    low_strict = (iota(square, 0) > iota(square, 1)).astype(BF16)
    up_strict = (iota(square, 0) < iota(square, 1)).astype(BF16)
    ones = jnp.ones(square, BF16)
    by_lane = dot_nn(flags, up_tri) + dot_nn(dot_nn(low_strict, flags).astype(BF16), ones)
    by_sublane = dot_nt(low_tri, flags) + dot_nn(dot_nt(ones, flags).astype(BF16), up_strict)
    return by_lane, by_sublane


def filter_matrices(first_row, by_lane, by_sublane, toeplitz):
    square = (LANES, LANES)
    parts = ([], [])
    for sb in range(4):
        left = jnp.broadcast_to(by_sublane[:, first_row + sb : first_row + sb + 1], square)
        across = ([], [])
        for tb in range(2):
            d = tb - sb + 2
            same = None
            if 0 <= d <= 2:
                same = left == by_lane[first_row + 2 + tb : first_row + 3 + tb, :]
            for component in range(2):
                kept = jnp.zeros(square, F32)
                if same is not None:
                    kept = jnp.where(same, toeplitz(component, d), 0.0)
                across[component].append(kept.astype(BF16))
        for component in range(2):
            parts[component].append(jnp.concatenate(across[component], axis=1))
    return [jnp.concatenate(part, axis=0) for part in parts]


def products_kernel(
    *refs,
    core,
):
    colat_ref, lon_ref, scalar_ref = refs[:3]
    packed_ref = refs[3]
    packed_out, products, turns, polar, azimuth, small, scalars, scalars_sem = refs[-8:]
    packed_out[...] = packed_ref[...]

    @pl.when(lax.axis_index("core") == core)
    def _():
        scalars_copy = pltpu.make_async_copy(scalar_ref, scalars, scalars_sem)
        scalars_copy.start()
        rows, _ = colat_ref.shape
        spread_turns(turns, colat_ref[...], 0, 0)
        spread_turns(turns, lon_ref[...], 1, 0)
        fill_tables((polar, azimuth.reshape(2, MULTIPLES * rows, LANES)), turns, small)
        scalars_copy.wait()
        fill_products(products, scalars, (polar, azimuth))


def three_quadrants(filtered, panel):
    half = panel // 2
    upper = jnp.concatenate([filtered[0:half, :], filtered[panel : panel + 16, :]], axis=0)
    lower = filtered[half:panel, :]
    return dot_nt(upper, filtered[0:panel, :]), dot_nt(lower, lower)


def own_kernel(
    products,
    obs_ref,
    start_ref,
    harmonic_ref,
    taps_ref,
    gram_ref,
    head_ref,
    columns_ref,
    toeplitz_ref,
    design,
    filtered,
    starts,
):
    rows, _ = start_ref.shape
    panel = harmonic_ref.shape[1]
    blocks = rows // 2

    wide = harmonic_ref[...].astype(F32)
    tall = jnp.transpose(jnp.concatenate([wide, jnp.zeros((6, panel), F32)], axis=0))
    for zl in range(4):
        for y in range(4):
            part = tall[zl * 128 + y * 32 : zl * 128 + y * 32 + 32, :]
            low = y * 128 + zl * 32
            degree = jnp.broadcast_to(part[:, 0:1], (32, LANES))
            order = jnp.broadcast_to(part[:, 1:2], (32, LANES))
            columns_ref[0, low : low + 32, :] = degree
            columns_ref[1, low : low + 32, :] = jnp.abs(order)
            columns_ref[2, low : low + 32, :] = jnp.where(order < 0.0, 0.25, 0.0)

    starts[...] = jnp.zeros_like(starts)
    starts[0:rows, :] = start_ref[...].astype(F32)
    by_lane, by_sublane = labels_of(starts[...].astype(BF16))

    for component in range(2):
        padded = jnp.concatenate(
            [taps_ref[component : component + 1, :].astype(F32), jnp.zeros((1, TAPS), F32)], axis=1
        )
        spread = jnp.broadcast_to(padded, (LANES, 2 * TAPS))
        rolled = pltpu.roll(spread, 0, 1, stride=1, stride_axis=0)
        for d in range(3):
            toeplitz_ref[component, d] = rolled[:, d * LANES : (d + 1) * LANES]
    for component in range(2):
        fill_signal(design, component, panel, obs_ref[component : component + 1, :].astype(F32))

    def to_lanes(block):
        for component in range(2):
            for row in (2 * block, 2 * block + 1):
                for low in range(0, panel, 16):
                    tile = products[component, row // 4, pl.ds(low * 4 + row % 4, 16, stride=4), :]
                    design[component, low : low + 16, row * LANES : (row + 1) * LANES] = tile.astype(BF16)

    to_lanes(0)
    for component in range(2):
        head_ref[component] = design[component, :, 0:TAPS]
    for block in range(blocks - 1):
        to_lanes(block + 1)
        filters = filter_matrices(2 * block, by_lane, by_sublane, lambda c, d: toeplitz_ref[c, d])
        for component in range(2):
            window = design[component, :, block * TAPS : block * TAPS + 2 * TAPS]
            low = (component * (blocks - 1) + block) * TAPS
            filtered[:, low : low + TAPS] = dot_nn(window, filters[component]).astype(BF16)
    upper, lower = three_quadrants(filtered, panel)
    half = panel // 2
    gram_ref[0 : half + 16, :] = upper
    gram_ref[half + 16 : panel + 16, half:panel] = lower


def edge_kernel(
    near_ref,
    far_ref,
    start_ref,
    before_ref,
    head_ref,
    columns_ref,
    toeplitz_ref,
    out_ref,
    design,
    filtered,
    turns,
    starts,
    gram,
    halo_ref,
):
    panel = columns_ref.shape[1]
    halo_ref[...] = near_ref[...] + far_ref[...]
    spread_turns(turns, halo_ref[0:2, :], 0, 0)
    spread_turns(turns, halo_ref[2:4, :], 1, 0)

    square = (LANES, LANES)
    starts[...] = jnp.zeros_like(starts)
    starts[0:2, :] = halo_ref[8:10, :]
    starts[2:4, :] = start_ref[0:2, :].astype(F32)
    by_lane, by_sublane = labels_of(starts[...].astype(BF16))
    lonely = 1.0 - halo_ref[10:11, :]
    by_lane = by_lane + jnp.where(iota(square, 0) >= 2, lonely, 0.0)
    by_sublane = by_sublane + jnp.where(iota(square, 1) >= 2, lonely, 0.0)
    filters = filter_matrices(0, by_lane, by_sublane, lambda c, d: toeplitz_ref[c, d])

    fill_design(design, columns_ref, turns, 2)
    for component in range(2):
        low = 4 + 2 * component
        halo = jnp.concatenate([halo_ref[low : low + 1, :], halo_ref[low + 1 : low + 2, :]], axis=1)
        fill_signal(design, component, panel, halo)
        sums = dot_nn(design[component], filters[component][0:TAPS, :]) + dot_nn(
            head_ref[component], filters[component][TAPS : 2 * TAPS, :]
        )
        filtered[:, component * TAPS : (component + 1) * TAPS] = sums.astype(BF16)

    upper, lower = three_quadrants(filtered, panel)
    half = panel // 2
    upper = upper + before_ref[0 : half + 16, :]
    gram[0:half, :] = upper[0:half, :]
    gram[panel : panel + 16, :] = upper[half : half + 16, :]
    gram[half:panel, half:panel] = lower + before_ref[half + 16 : panel + 16, half:panel]
    gram[half:panel, 0:half] = jnp.transpose(upper[0:half, half:panel])

    eye = iota(square, 0) == iota(square, 1)
    rhs = [gram[panel : panel + 1, y * LANES : (y + 1) * LANES] for y in range(4)]
    diagonal = [
        jnp.sum(
            jnp.where(eye, gram[y * LANES : (y + 1) * LANES, y * LANES : (y + 1) * LANES], 0.0),
            axis=0,
            keepdims=True,
        )
        for y in range(4)
    ]
    small = jnp.concatenate(rhs + diagonal, axis=0).astype(BF16)
    for y in range(4):
        for x in range(4):
            for core in range(2):
                peer = y * 8 + x * 2 + core
                for zh in range(4):
                    low = x * 128 + zh * 32 + core * 16
                    out_ref[peer, zh * 16 : zh * 16 + 16, :] = gram[
                        low : low + 16, y * LANES : (y + 1) * LANES
                    ].astype(BF16)
                out_ref[peer, 64:72, :] = small


def middle_kernel(in_ref, out_ref):
    total = in_ref[0].astype(F32)
    for peer in range(1, in_ref.shape[0]):
        total = total + in_ref[peer].astype(F32)
    rounded = total.astype(BF16)
    for zl in range(4):
        for zh in range(4):
            low = 3 * (zl * 4 + zh)
            for b in range(4):
                out_ref[low, :, b * 32 : b * 32 + 32] = rounded[
                    zh * 16 + 4 * b : zh * 16 + 4 * b + 4, zl * 32 : zl * 32 + 32
                ]
            out_ref[low + 1] = rounded[64:68, :]
            out_ref[low + 2] = rounded[68:72, :]


def last_kernel(in_ref, normal_ref, rhs_ref, diagonal_ref, *, row_scale, gram_scale):
    totals = []
    for part in range(3):
        total = in_ref[part].astype(F32)
        for peer in range(1, in_ref.shape[0] // 3):
            total = total + in_ref[3 * peer + part].astype(F32)
        totals.append(total * (gram_scale, gram_scale, row_scale)[part])
    for b in range(4):
        normal_ref[4 * b : 4 * b + 4, :] = totals[0][:, b * 32 : b * 32 + 32]
    rows, cols = normal_ref.shape
    row_low = (lax.axis_index("zh") * 8 + lax.axis_index("x") * 2 + lax.axis_index("core")) * rows
    col_low = (lax.axis_index("zl") * 4 + lax.axis_index("y")) * cols
    on_diagonal = row_low + iota((rows, cols), 0) == col_low + iota((rows, cols), 1)
    normal_ref[...] = jnp.where(on_diagonal, 0.0, normal_ref[...])
    for out_ref, total in ((rhs_ref, totals[1]), (diagonal_ref, totals[2])):
        for zl in range(4):
            for y in range(4):
                out_ref[0:1, zl * 128 + y * 32 : zl * 128 + y * 32 + 32] = total[
                    y : y + 1, zl * 32 : zl * 32 + 32
                ]


def load_kernel(*refs):
    count = (len(refs) - 3) // 2
    sources, packed_ref, rows_ref = refs[:count], refs[count], refs[count + 1]
    targets, sems = refs[count + 2 : -1], refs[-1]
    copies = [
        pltpu.make_async_copy(source, target, sems.at[index])
        for index, (source, target) in enumerate(zip(sources, targets))
    ]
    for copy in copies:
        copy.start()
    for copy in copies:
        copy.wait()
    colat_ref, lon_ref, obs_ref, start_ref = targets[:4]
    last = colat_ref.shape[0] - 2
    span = obs_ref.shape[1]
    packed_ref[0:2, :] = colat_ref[last : last + 2, :]
    packed_ref[2:4, :] = lon_ref[last : last + 2, :]
    for component in range(2):
        for half in range(2):
            low = span - (2 - half) * LANES
            row = 4 + 2 * component + half
            packed_ref[row : row + 1, :] = obs_ref[component : component + 1, low : low + LANES].astype(
                F32
            )
    packed_ref[8:10, :] = start_ref[last : last + 2, :].astype(F32)
    packed_ref[10:16, :] = jnp.ones((6, LANES), F32)
    rows = colat_ref.shape[0]
    degree = targets[4][0:1, :]
    order = targets[4][1:2, :]
    wave = jnp.abs(order) + jnp.where(order < 0, MULTIPLES, 0)
    for y in range(4):
        for zl in range(4):
            group = y * 4 + zl
            lanes = slice(zl * LANES + y * 32, zl * LANES + y * 32 + 32)
            rows_ref[group : group + 1, 0:32] = degree[:, lanes] * rows
            rows_ref[16 + group : 17 + group, 0:32] = wave[:, lanes] * rows


def on_device(colatitude, longitude, observed, filter_taps, segment_start, harmonic):
    rows_here = colatitude.shape[0]
    panel = harmonic.shape[1]
    rows_total = rows_here * 512
    vmem = pl.BlockSpec(memory_space=pltpu.VMEM)
    hbm = pl.BlockSpec(memory_space=pltpu.HBM)

    def kernel(body, outs, scratch, mebibytes, operands, estimate=None):
        return pl.pallas_call(
            body,
            out_shape=outs,
            in_specs=[vmem] * len(operands),
            out_specs=jax.tree.map(lambda _: vmem, outs),
            scratch_shapes=scratch,
            cost_estimate=estimate,
            compiler_params=pltpu.CompilerParams(vmem_limit_bytes=mebibytes * 1024 * 1024),
        )(*operands)

    colat = colatitude.reshape(-1, LANES)
    lon = longitude.reshape(-1, LANES)
    start = segment_start.reshape(-1, LANES)
    arguments = (colat, lon, observed, start, harmonic, filter_taps)
    packed, table_rows, colat, lon, observed, start, harmonic, filter_taps = pl.pallas_call(
        load_kernel,
        name="load_and_pack",
        out_shape=(
            jax.ShapeDtypeStruct((16, LANES), F32),
            jax.ShapeDtypeStruct((32, LANES), jnp.int32),
            *(jax.ShapeDtypeStruct(value.shape, value.dtype) for value in arguments),
        ),
        in_specs=[hbm] * len(arguments),
        out_specs=(vmem,) * (len(arguments) + 2),
        scratch_shapes=[pltpu.SemaphoreType.DMA((len(arguments),))],
        compiler_params=pltpu.CompilerParams(vmem_limit_bytes=4 * 1024 * 1024),
    )(*(pltpu.with_memory_space_constraint(value, pltpu.HBM) for value in arguments))
    ring = ("zh", "x", "core")
    sub_rows = rows_here // LANES

    def products_on(core, *before):
        operands = (colat, lon, table_rows, packed, *before)
        outs = (
            jax.ShapeDtypeStruct((16, LANES), F32),
            jax.ShapeDtypeStruct((2, sub_rows // 4, panel * 4, LANES), F32),
        )
        return pl.pallas_call(
            functools.partial(products_kernel, core=core),
            out_shape=outs,
            in_specs=[vmem] * len(operands),
            out_specs=(vmem, vmem),
            scratch_shapes=[
                pltpu.VMEM((4, sub_rows, LANES), F32),
                pltpu.VMEM((2, MULTIPLES * sub_rows, LANES), F32),
                pltpu.VMEM((2 * MULTIPLES * sub_rows, LANES), F32),
                pltpu.VMEM((2, 2, 18, sub_rows, LANES), F32),
                pltpu.SMEM((32, LANES), jnp.int32),
                pltpu.SemaphoreType.DMA(()),
            ],
            input_output_aliases={4: 1} if before else {},
            cost_estimate=pl.CostEstimate(
                flops=40_000_000, bytes_accessed=8_000_000, transcendentals=0
            ),
            compiler_params=pltpu.CompilerParams(vmem_limit_bytes=16 * 1024 * 1024),
        )(*operands)

    packed_far, products = products_on(1)
    halo_far = lax.ppermute(packed_far, ring, [(i, i + 1) for i in range(1, 31, 2)])
    packed_near, products = products_on(0, products)
    halo_near = lax.ppermute(packed_near, ring, [(i, i + 1) for i in range(0, 31, 2)])
    before, head, columns, toeplitz = kernel(
        own_kernel,
        (
            jax.ShapeDtypeStruct((panel + 16, panel), F32),
            jax.ShapeDtypeStruct((2, panel + 16, TAPS), BF16),
            jax.ShapeDtypeStruct((3, panel, LANES), F32),
            jax.ShapeDtypeStruct((2, 3, LANES, LANES), F32),
        ),
        [
            pltpu.VMEM((2, panel + 16, rows_here), BF16),
            pltpu.VMEM((panel + 16, 2 * (rows_here - TAPS)), BF16),
            pltpu.VMEM((LANES, LANES), F32),
        ],
        24,
        (products, observed, start, harmonic, filter_taps),
        pl.CostEstimate(flops=4_000_000_000, bytes_accessed=4_000_000, transcendentals=0),
    )
    payload = kernel(
        edge_kernel,
        jax.ShapeDtypeStruct((32, 72, LANES), BF16),
        [
            pltpu.VMEM((2, panel + 16, TAPS), BF16),
            pltpu.VMEM((panel + 16, 2 * TAPS), BF16),
            pltpu.VMEM((4, 8, LANES), F32),
            pltpu.VMEM((LANES, LANES), F32),
            pltpu.VMEM((panel + 16, panel), F32),
            pltpu.VMEM((16, LANES), F32),
        ],
        16,
        (halo_near, halo_far, start, before, head, columns, toeplitz),
    )
    arrived = lax.all_to_all(payload, ("y", "x", "core"), 0, 0)
    sums = kernel(middle_kernel, jax.ShapeDtypeStruct((48, 4, LANES), BF16), [], 8, (arrived,))
    gathered = lax.all_to_all(sums, ("zl", "zh"), 0, 0, tiled=True)
    normal, right_side, diagonal = kernel(
        functools.partial(
            last_kernel, row_scale=1.0 / rows_total, gram_scale=1.0 / math.sqrt(rows_total)
        ),
        (
            jax.ShapeDtypeStruct((16, 32), F32),
            jax.ShapeDtypeStruct((1, panel), F32),
            jax.ShapeDtypeStruct((1, panel), F32),
        ),
        [],
        8,
        (gathered,),
    )
    return normal, right_side.reshape(panel), diagonal.reshape(panel)


def solution(mesh):
    fine = Mesh(mesh.devices.reshape(4, 4, 4, 4, 2), ("zl", "y", "zh", "x", "core"))
    everywhere = ("zl", "y", "zh", "x", "core")
    return jax.shard_map(
        on_device,
        mesh=fine,
        in_specs=(P(everywhere), P(everywhere), P(None, everywhere), P(), P(everywhere), P()),
        out_specs=(P(("zh", "x", "core"), ("zl", "y")), P(), P()),
        check_vma=False,
    )
```
